32 devices in a mesh: dp: 4 (over y, core), fsdp: 8 (over z, x).
Axes of the slice: x: 2, y: 2, z: 4, core: 2. Of those that a mesh axis runs over, the one named last changes fastest.
Arguments:
- context: bfloat16 [16384, 1024], P(('dp', 'fsdp')), may hold values from -6 to 6
- residual: bfloat16 [16384, 2048], P(('dp', 'fsdp')), may hold values from -6 to 6
- out_weight: bfloat16 [1024, 2048], P('fsdp'), may hold values from -0.1875 to 0.1875
- norm_gain: float32 [2048], replicated, may hold values from 0.5 to 1.5
- user_vectors: bfloat16 [256, 2048], P(('dp', 'fsdp')), may hold values from -12 to 12
- positive: int32 [256], P(('dp', 'fsdp')), may hold values from 0 to 63
- item_ids: int32 [64], P(('dp', 'fsdp')), may hold values from 0 to 31
- item_counts: int32 [64], P(('dp', 'fsdp')), may hold values from 1 to 5000
- lengths: int32 [64], P(('dp', 'fsdp')), may hold values from 64 to 256
Outputs:
- mean_loss: float32 [], replicated
- residual_grad: bfloat16 [16384, 2048], P(('dp', 'fsdp'))
- context_grad: bfloat16 [16384, 1024], P(('dp', 'fsdp'))
- weight_grad: bfloat16 [1024, 2048], P('fsdp')
- norm_gain_grad: float32 [2048], replicated
- user_grad: bfloat16 [256, 2048], P(('dp', 'fsdp'))
The draws below stay inside these ranges and needn't reach their ends.
All inputs are finite; a program needn't handle non-finite values.
Results may differ from the reference program's by a relative error of at most 0.015.
Values may be sent and summed in bfloat16 or wider, within the bound.
A program may use at most 128 MiB of HBM per device.

```python
import math
import jax
import jax.numpy as jnp
import numpy as np
from jax import lax

D = 2048
H = 1024
LENGTH = 256
ITEMS = 64
USER_COUNT = 256
TOKENS = 16384


def draw_user_vectors(key, part):
    key_normal = jax.random.fold_in(key, 11)
    row_index = jnp.arange(USER_COUNT, dtype=jnp.float32)
    row_factor = 0.05 * (1.0 + 2.0 * row_index / max(USER_COUNT - 1, 1))
    normed_share = jax.random.normal(key_normal, (USER_COUNT, D), jnp.float32)
    value_rows = normed_share * row_factor[:, None]
    return jnp.clip(value_rows, -12.0, 12.0).astype(jnp.bfloat16)


def plant(entries, key, smallest, largest):
    longest = entries.shape.index(max(entries.shape))
    spots = []
    for shift in (0, 1):
        where = [jax.random.randint(jax.random.fold_in(key, axis), (), 0, length) for axis, length in enumerate(entries.shape)]
        where[longest] = (where[longest] + shift) % entries.shape[longest]
        spots.append(tuple(where))
    return entries.at[spots[0]].set(smallest).at[spots[1]].set(largest)


def shard_levels(stream_key, extent, split, low, high):
    loudness = 1.0
    for axis_at, blocks in split:
        draws = jax.random.uniform(jax.random.fold_in(jax.random.fold_in(stream_key, 6), axis_at), (blocks,), jnp.float32, low / len(split), high / len(split))
        loudness = loudness * jnp.repeat(jnp.exp(draws), extent[axis_at] // blocks).reshape((-1,) + (1,) * (len(extent) - 1 - axis_at))
    return loudness


def rank_table(count, slope):
    loads = [(1 << 20) // math.isqrt(rank ** slope) + 1 for rank in range(1, count + 1)]
    spread = 1 + sum(loads) // (1 << 30)
    return np.cumsum(np.array([max(1, weight // spread) for weight in loads]))


def ranked_ids(own_key, shape, number_of, skew):
    listing = rank_table(number_of, skew)
    pick = jax.random.randint(jax.random.fold_in(own_key, 1), shape, 0, int(listing[number_of - 1]))
    grade = jnp.searchsorted(jnp.asarray(listing, jnp.int32), pick, side="right")
    return jax.random.permutation(jax.random.fold_in(own_key, 2), number_of)[grade].astype(jnp.int32)


def gaussian(stream_key, dims, scale, limit, cuts=(), kind=jnp.bfloat16):
    entries = jax.random.normal(stream_key, dims, jnp.float32) * scale
    if len(cuts) > 0:
        entries = shard_levels(stream_key, dims, cuts, -0.22, 0.18) * entries
    return jnp.clip(entries, min=-limit, max=limit).astype(kind)


def setup_inputs(seed: int = 0) -> dict:
    splits = jax.random.split(jax.random.key(seed), 10)
    context = gaussian(splits[0], (TOKENS, H), 1.0, 6.0, ((0, 32),))
    residual = gaussian(splits[1], (TOKENS, D), 1.0, 6.0, ((0, 32),))
    out_weight = gaussian(splits[2], (H, D), H ** -0.5, 0.1875, ((0, 8),))
    norm_gain = jnp.clip(1.0 + 0.1 * jax.random.normal(splits[3], (D,), jnp.float32), 0.5, 1.5)
    user_vectors = draw_user_vectors(jax.random.fold_in(splits[9], 71), 0)
    positive = plant(jax.random.randint(splits[5], (USER_COUNT,), 0, ITEMS), jax.random.fold_in(splits[5], 1), 0, ITEMS - 1).astype(jnp.int32)
    item_ids = plant(ranked_ids(splits[6], (ITEMS,), ITEMS // 2, 2), jax.random.fold_in(splits[6], 3), 0, (ITEMS // 2) - 1).astype(jnp.int32)
    item_counts = plant(jax.random.randint(splits[7], (ITEMS,), 1, 5001), jax.random.fold_in(splits[7], 1), 1, 5000).astype(jnp.int32)
    lengths = plant(jax.random.randint(splits[8], (ITEMS,), LENGTH // 4, LENGTH + 1), jax.random.fold_in(splits[8], 1), LENGTH // 4, LENGTH).astype(jnp.int32)
    return dict(context=context, residual=residual, out_weight=out_weight, norm_gain=norm_gain, user_vectors=user_vectors, positive=positive, item_ids=item_ids, item_counts=item_counts, lengths=lengths)


EPSILON = 1e-06
MASKED_FILL = -1e+30

def stream_of(context_rows, residual_rows, out_weight, norm_gain):
    attended = jnp.dot(context_rows, out_weight, preferred_element_type=jnp.float32)
    stream = residual_rows.astype(jnp.float32) + attended
    inverse_root_mean = lax.rsqrt(lax.optimization_barrier(jnp.mean(stream * stream, axis=-1, keepdims=True)) + EPSILON)
    return (stream, inverse_root_mean, stream * inverse_root_mean * norm_gain)

def reference(context, residual, out_weight, norm_gain, user_vectors, positive, item_ids, item_counts, lengths):
    context_items = context.reshape(ITEMS, LENGTH, H)
    residual_items = residual.reshape(ITEMS, LENGTH, D)
    positions = jnp.arange(LENGTH, dtype=jnp.int32)

    def pool_item(packed):
        context_rows, residual_rows, length_here = packed
        stream, inverse_root_mean, normed = stream_of(context_rows, residual_rows, out_weight, norm_gain)
        inside = (positions < length_here)[:, None]
        return lax.optimization_barrier(jnp.sum(jnp.where(inside, normed, 0.0), axis=0)) / length_here.astype(jnp.float32)
    pooled = lax.map(pool_item, (context_items, residual_items, lengths))
    emb_scale = lax.rsqrt(lax.optimization_barrier(jnp.mean(pooled * pooled, axis=-1, keepdims=True)) + EPSILON)
    embedding = (pooled * emb_scale).astype(jnp.bfloat16)
    scores = jnp.dot(user_vectors, embedding.T, preferred_element_type=jnp.float32)
    columns = jnp.arange(ITEMS, dtype=jnp.int32)
    onehot = columns[None, :] == positive[:, None]
    positive_id = lax.optimization_barrier(jnp.sum(jnp.where(onehot, item_ids[None, :], 0), axis=1))
    excluded = (item_ids[None, :] == positive_id[:, None]) & jnp.logical_not(onehot)
    log_counts = jnp.log(item_counts.astype(jnp.float32))
    logits = jnp.where(excluded, MASKED_FILL, scores - log_counts[None, :])
    row_max = lax.optimization_barrier(jnp.max(logits, axis=1, keepdims=True))
    weights = jnp.where(excluded, 0.0, jnp.exp(logits - row_max))
    row_total = lax.optimization_barrier(jnp.sum(weights, axis=1, keepdims=True))
    log_total = row_max[:, 0] + jnp.log(row_total[:, 0])
    picked = lax.optimization_barrier(jnp.sum(jnp.where(onehot, logits, 0.0), axis=1))
    mean_loss = jnp.mean(log_total - picked)
    logit_grad = (weights / row_total - onehot.astype(jnp.float32)).astype(jnp.bfloat16)
    user_grad = jnp.dot(logit_grad, embedding, preferred_element_type=jnp.float32).astype(jnp.bfloat16)
    emb_grad = jnp.dot(logit_grad.T, user_vectors, preferred_element_type=jnp.float32)
    pooled_grad = emb_scale * emb_grad - pooled * emb_scale ** 3 * lax.optimization_barrier(jnp.mean(pooled * emb_grad, axis=-1, keepdims=True))

    def backward_item(carried, packed):
        weight_sum, gain_sum = carried
        context_rows, residual_rows, length_here, grad_row = packed
        stream, inverse_root_mean, normed = stream_of(context_rows, residual_rows, out_weight, norm_gain)
        inside = (positions < length_here)[:, None]
        normed_grad = jnp.where(inside, grad_row[None, :] / length_here.astype(jnp.float32), 0.0)
        gain_sum = gain_sum + lax.optimization_barrier(jnp.sum(normed_grad * stream * inverse_root_mean, axis=0))
        scaled = norm_gain * normed_grad
        stream_grad = inverse_root_mean * scaled - stream * inverse_root_mean ** 3 * lax.optimization_barrier(jnp.mean(scaled * stream, axis=-1, keepdims=True))
        residual_grad = stream_grad.astype(jnp.bfloat16)
        context_grad = jnp.dot(residual_grad, out_weight.T, preferred_element_type=jnp.float32).astype(jnp.bfloat16)
        weight_sum = weight_sum + jnp.dot(context_rows.T, residual_grad, preferred_element_type=jnp.float32)
        return ((weight_sum, gain_sum), (residual_grad, context_grad))
    start_sums = (jnp.zeros((H, D), jnp.float32), jnp.zeros((D,), jnp.float32))
    final_sums, outputs = lax.scan(backward_item, start_sums, (context_items, residual_items, lengths, pooled_grad))
    weight_sum, gain_sum = final_sums
    residual_grad = outputs[0].reshape(TOKENS, D)
    context_grad = outputs[1].reshape(TOKENS, H)
    return (mean_loss, residual_grad, context_grad, weight_sum.astype(jnp.bfloat16), gain_sum, user_grad)
```

```python
import functools

import jax
import jax.numpy as jnp
from jax import lax
from jax.experimental import pallas as pl
from jax.experimental.pallas import tpu as pltpu
from jax.sharding import PartitionSpec as P

EPSILON = 1e-06
MASKED_FILL = -1e30
MESH = pl.DeviceIdType.MESH
CHUNKS = 4


def contract_rows(left, right):
    return lax.dot_general(
        left, right, (((0,), (0,)), ((), ())), preferred_element_type=jnp.float32
    )


def contract_last(left, right):
    return lax.dot_general(
        left, right, (((1,), (1,)), ((), ())), preferred_element_type=jnp.float32
    )


def ring_place(index, count):
    return jnp.where(index % 2 == 0, index // 2, count - 1 - index // 2)


def ring_index(place, count):
    return jnp.where(place < count // 2, 2 * place, 2 * (count - 1 - place) + 1)


def greet(devices):
    barrier = pltpu.get_barrier_semaphore()
    for device in devices:
        pl.semaphore_signal(barrier, inc=1, device_id=device, device_id_type=MESH)
    pl.semaphore_wait(barrier, len(devices))


def greet_all(groups, ring, me):
    total = groups * ring
    barrier = pltpu.get_barrier_semaphore()

    def signal(k, carry):
        peer = lax.rem(me + k, total)
        pl.semaphore_signal(
            barrier, inc=1, device_id=(peer // ring, lax.rem(peer, ring)), device_id_type=MESH
        )
        return carry

    lax.fori_loop(1, total, signal, 0)
    pl.semaphore_wait(barrier, total - 1)


def remote(src, dst, send_sem, recv_sem, device):
    return pltpu.make_async_remote_copy(
        src_ref=src,
        dst_ref=dst,
        send_sem=send_sem,
        recv_sem=recv_sem,
        device_id=device,
        device_id_type=MESH,
    )


def gather_kernel(
    groups, ring, w_in, u_in, k_in, w_out, u_out, k_out,
    own_sem, w_send, w_recv, p_send, p_recv, y_send, y_recv,
    u_send, u_recv, k_send, k_recv, ul_send, ul_recv, kl_send, kl_recv,
    up_send, up_recv, kp_send, kp_recv,
):
    group, index = lax.axis_index("dp"), lax.axis_index("fsdp")
    lines = groups // 2
    split = lines == 2
    slots = CHUNKS - 1 if split else CHUNKS
    line = group // 2
    core = lax.rem(group, 2)
    partner = group + 1 - 2 * core
    across = lax.rem(group + 2, groups)
    place = ring_place(index, ring)
    turn = 1 - 2 * core
    ends = (
        ring_index(lax.rem(place + ring + turn, ring), ring),
        ring_index(lax.rem(place + ring - turn, ring), ring),
    )
    rows = w_in.shape[0]
    half = rows // 2
    part = half // CHUNKS
    hops = ring - 1

    def owner(m, way=turn):
        if m == hops + 2:
            return index
        away = -(m // 2) if m % 2 == 0 else m // 2
        return ring_index(lax.rem(place + ring + way * away, ring), ring)

    def chunk(j):
        if not split or j < CHUNKS - 2:
            return j
        return CHUNKS - 2 + (line if j == CHUNKS - 2 else 1 - line)

    def w_slice(who, j, side=core):
        start = pl.multiple_of(who * rows + side * half + chunk(j) * part, part)
        return w_out.at[pl.ds(start, part), :]

    greet(
        [(lax.rem(group + k, groups), index) for k in range(1, groups)]
        + [(group, end) for end in ends]
    )
    own = [
        pltpu.make_async_copy(
            w_in, w_out.at[pl.ds(pl.multiple_of(index * rows, rows), rows), :], own_sem.at[0]
        ),
        pltpu.make_async_copy(u_in, u_out.at[group * ring + index], own_sem.at[1]),
        pltpu.make_async_copy(k_in, k_out.at[group * ring + index], own_sem.at[2]),
    ]
    for copy in own:
        copy.start()
    for copy in own:
        copy.wait()

    def w_ring(m, j, shift=0):
        ref = w_slice(owner(m + shift), j)
        return remote(ref, ref, w_send.at[m, j], w_recv.at[m, j], (group, ends[m % 2]))

    def w_part(m, j, side=core):
        ref = w_slice(owner(m + 2, 1 - 2 * side), j, side)
        return remote(ref, ref, p_send.at[m, j], p_recv.at[m, j], (partner, index))

    def w_across(m, j):
        ref = w_slice(owner(m + 2), j)
        return remote(ref, ref, y_send.at[m], y_recv.at[m], (across, index))

    small = (
        (u_out, u_send, u_recv, ul_send, ul_recv, up_send, up_recv),
        (k_out, k_send, k_recv, kl_send, kl_recv, kp_send, kp_recv),
    )

    def s_ring(a, m, shift):
        out, send, recv = small[a][:3]
        ref = out.at[group * ring + owner(m + shift)]
        return remote(ref, ref, send.at[m], recv.at[m], (group, ends[m % 2]))

    def s_line(a, s, k):
        out, _, _, send, recv = small[a][:5]
        ref = out.at[group * ring + owner(s + 2)]
        peer = lax.rem(group + 2 * k, groups)
        return remote(ref, ref, send.at[s, k - 1], recv.at[s, k - 1], (peer, index))

    def s_line_in(a, s, k):
        out, _, _, send, recv = small[a][:5]
        source = lax.rem(group + groups - 2 * k, groups)
        ref = out.at[source * ring + owner(s + 2)]
        return remote(ref, ref, send.at[s, k - 1], recv.at[s, k - 1], (source, index))

    def s_part(a, s, k):
        out, send, recv = small[a][0], small[a][5], small[a][6]
        source = lax.rem(group + groups - 2 * k, groups)
        ref = out.at[source * ring + owner(s + 2)]
        return remote(ref, ref, send.at[s, k], recv.at[s, k], (partner, index))

    def s_part_in(a, s, k):
        out, send, recv = small[a][0], small[a][5], small[a][6]
        source = lax.rem(partner + groups - 2 * k, groups)
        ref = out.at[source * ring + owner(s + 2, -turn)]
        return remote(ref, ref, send.at[s, k], recv.at[s, k], (partner, index))

    def w_pass(s):
        if split:
            w_across(s, CHUNKS - 1).wait_recv()
            w_part(s, CHUNKS - 1).start()

    def spread(s):
        for a in (0, 1):
            for k in range(1, lines):
                s_line(a, s, k).start()
            s_part(a, s, 0).start()

    def s_pass(s):
        for a in (0, 1):
            for k in range(1, lines):
                s_line_in(a, s, k).wait_recv()
                s_part(a, s, k).start()

    for m in range(min(2, hops)):
        for j in range(slots):
            w_ring(m, j).start()
    for m in range(min(2, hops)):
        for a in (0, 1):
            s_ring(a, m, 0).start()
    spread(hops)
    for m in range(hops):
        more = m + 2 < hops
        for j in range(slots):
            w_ring(m, j, 2).wait_recv()
            if more:
                w_ring(m + 2, j).start()
            if split and j == CHUNKS - 2:
                w_across(m, j).start()
            w_part(m, j).start()
        for a in (0, 1):
            s_ring(a, m, 2).wait_recv()
            if more:
                s_ring(a, m + 2, 0).start()
        spread(m)
        if m == 1:
            s_pass(hops)
        if m >= 2:
            w_pass(m - 2)
            s_pass(m - 2)
    for m in range(hops - 2, hops):
        w_pass(m)
        s_pass(m)
    for m in range(hops):
        for j in range(slots):
            w_ring(m, j).wait_send()
        if split:
            w_across(m, CHUNKS - 2).wait_send()
        for j in range(CHUNKS):
            w_part(m, j).wait_send()
            w_part(m, j, 1 - core).wait_recv()
        for a in (0, 1):
            s_ring(a, m, 0).wait_send()
    for m in range(ring):
        for a in (0, 1):
            for k in range(1, lines):
                s_line(a, m, k).wait_send()
            for k in range(lines):
                s_part(a, m, k).wait_send()
                s_part_in(a, m, k).wait_recv()


def gather_inputs(groups, ring, weight, users, keys):
    total = groups * ring
    lines = groups // 2
    rows, width = weight.shape
    dma = pltpu.SemaphoreType.DMA
    vmem = pl.BlockSpec(memory_space=pltpu.VMEM)
    anywhere = pl.BlockSpec(memory_space=pl.ANY)
    return pl.pallas_call(
        functools.partial(gather_kernel, groups, ring),
        out_shape=(
            jax.ShapeDtypeStruct((ring * rows, width), weight.dtype),
            jax.ShapeDtypeStruct((total,) + users.shape, users.dtype),
            jax.ShapeDtypeStruct((total,) + keys.shape, keys.dtype),
        ),
        in_specs=[anywhere, anywhere, anywhere],
        out_specs=(vmem, vmem, vmem),
        scratch_shapes=[dma((3,))]
        + [dma((ring - 1, CHUNKS))] * 4
        + [dma((ring - 1,))] * 2
        + [dma((ring - 1,))] * 4
        + [dma((ring, max(lines - 1, 1)))] * 4
        + [dma((ring, lines))] * 4,
        compiler_params=pltpu.CompilerParams(
            collective_id=0, has_side_effects=True, vmem_limit_bytes=32 << 20
        ),
        name="gather_inputs",
    )(weight, users, keys)


def share_kernel(groups, ring, x_in, x_out, own_sem, send_sem, recv_sem, wide_send, wide_recv):
    group, index = lax.axis_index("dp"), lax.axis_index("fsdp")
    greet(
        [(group, lax.rem(index + k, ring)) for k in range(1, ring)]
        + [(lax.rem(group + k, groups), index) for k in range(1, groups)]
    )

    def along(k, source):
        return remote(
            x_in, x_out.at[group * ring + source], send_sem.at[k - 1], recv_sem.at[k - 1],
            (group, lax.rem(index + k, ring)),
        )

    def wide(k, source):
        ref = x_out.at[pl.ds(source * ring, ring)]
        return remote(
            ref, ref, wide_send.at[k - 1], wide_recv.at[k - 1], (lax.rem(group + k, groups), index)
        )

    for k in range(1, ring):
        along(k, index).start()
    own = pltpu.make_async_copy(x_in, x_out.at[group * ring + index], own_sem)
    own.start()
    own.wait()
    for k in range(1, ring):
        along(k, lax.rem(index + ring - k, ring)).wait_recv()
    for k in range(1, groups):
        wide(k, group).start()
    for k in range(1, ring):
        along(k, index).wait_send()
    for k in range(1, groups):
        wide(k, group).wait_send()
        wide(k, lax.rem(group + groups - k, groups)).wait_recv()


def share(groups, ring, block):
    total = groups * ring
    dma = pltpu.SemaphoreType.DMA
    vmem = pl.BlockSpec(memory_space=pltpu.VMEM)
    return pl.pallas_call(
        functools.partial(share_kernel, groups, ring),
        out_shape=jax.ShapeDtypeStruct((total,) + block.shape, block.dtype),
        in_specs=[vmem],
        out_specs=vmem,
        scratch_shapes=[dma] + [dma((ring - 1,))] * 2 + [dma((groups - 1,))] * 2,
        compiler_params=pltpu.CompilerParams(collective_id=1, has_side_effects=True),
        name="share",
    )(block)


def reduce_kernel(
    groups, ring, part_in, gain_in, out, gain_out,
    cross, held, arrived, totals, lent, borrowed,
    own_sem, g_send, g_recv, x_send, x_recv, r_send, r_recv, t_send, t_recv, o_send, o_recv,
    y_send, y_recv, f_send, f_recv,
):
    total = groups * ring
    group, index = lax.axis_index("dp"), lax.axis_index("fsdp")
    me = group * ring + index
    core = lax.rem(group, 2)
    partner = group + 1 - 2 * core
    place = ring_place(index, ring)
    turn = 1 - 2 * core
    ends = (
        ring_index(lax.rem(place + ring + turn, ring), ring),
        ring_index(lax.rem(place + ring - turn, ring), ring),
    )
    hops = ring - 1
    rows = part_in.shape[0] // ring
    half = rows // 2
    piece = half // CHUNKS
    lines = groups // 2
    line = group // 2
    split = lines == 2
    slots = CHUNKS - 1 if split else CHUNKS
    across = lax.rem(group + 2, groups)

    def owner(m, way=turn):
        if m == hops:
            return index
        away = ring // 2 - m // 2 if m % 2 == 0 else m // 2 - (ring - 1) // 2
        return ring_index(lax.rem(place + ring + way * away, ring), ring)

    def chunk(j):
        if not split or j < CHUNKS - 2:
            return j
        return CHUNKS - 2 + (line if j == CHUNKS - 2 else 1 - line)

    greet_all(groups, ring, me)

    def cross_out(m):
        start = pl.multiple_of(owner(m, -turn) * rows + (1 - core) * half, half)
        return remote(
            part_in.at[pl.ds(start, half), :], cross.at[m], x_send.at[m], x_recv.at[m],
            (partner, index),
        )

    for m in range(ring):
        cross_out(m).start()

    def gain_push(k):
        peer = lax.rem(me + k, total)
        return remote(
            gain_in, gain_out.at[me], g_send.at[k - 1], g_recv.at[k - 1],
            (peer // ring, lax.rem(peer, ring)),
        )

    def gain_pull(k):
        source = lax.rem(me + total - k, total)
        return remote(
            gain_in, gain_out.at[source], g_send.at[k - 1], g_recv.at[k - 1],
            (source // ring, lax.rem(source, ring)),
        )

    def start_gain(k, carry):
        gain_push(k).start()
        return carry

    lax.fori_loop(1, total, start_gain, 0)
    own = pltpu.make_async_copy(gain_in, gain_out.at[me], own_sem)
    own.start()

    def ring_copy(s, c):
        at = pl.ds(c * piece, piece)
        return remote(
            held.at[s, at, :], arrived.at[s, at, :], r_send.at[s, c], r_recv.at[s, c],
            (group, ends[s % 2]),
        )

    def local_term(s, j):
        offset = chunk(j) * piece
        start = pl.multiple_of(owner(s) * rows + core * half + offset, piece)
        mine = part_in[pl.ds(start, piece), :].astype(jnp.float32)
        return mine + cross[s, pl.ds(pl.multiple_of(offset, piece), piece), :].astype(jnp.float32)

    def lend(s):
        return remote(lent.at[s], borrowed.at[s], y_send.at[s], y_recv.at[s], (across, index))

    def prepare(s):
        cross_out(s).wait_recv()
        if split:
            lent[s] = local_term(s, CHUNKS - 1).astype(lent.dtype)
            lend(s).start()

    def term_of(s, j):
        term = local_term(s, j)
        if split and j == CHUNKS - 2:
            lend(s).wait_recv()
            term = term + borrowed[s].astype(jnp.float32)
        return term

    for m in range(min(2, hops)):
        prepare(m)
    for m in range(hops):
        for j in range(slots):
            at = pl.ds(j * piece, piece)
            if j == max(CHUNKS - 2, 0) and m + 2 < ring:
                prepare(m + 2)
            term = term_of(m, j)
            if m >= 2:
                ring_copy(m - 2, j).wait_recv()
                term = term + arrived[m - 2, at, :].astype(jnp.float32)
            held[m, at, :] = term.astype(held.dtype)
            ring_copy(m, j).start()
    last = hops

    def total_copy(k, j):
        ref = totals.at[line, pl.ds(j * piece, piece), :]
        return remote(
            ref, ref, t_send.at[k - 1, j], t_recv.at[k - 1, j],
            (lax.rem(group + 2 * k, groups), index),
        )

    def total_in(k, j):
        source = lax.rem(group + groups - 2 * k, groups)
        ref = totals.at[source // 2, pl.ds(j * piece, piece), :]
        return remote(ref, ref, t_send.at[k - 1, j], t_recv.at[k - 1, j], (source, index))

    def out_rows(j, side=core):
        return pl.ds(pl.multiple_of(side * half + chunk(j) * piece, piece), piece)

    def out_copy(j, side):
        ref = out.at[out_rows(j, side), :]
        return remote(ref, ref, o_send.at[j], o_recv.at[j], (partner, index))

    def out_across(j):
        ref = out.at[out_rows(j), :]
        return remote(ref, ref, f_send.at[0], f_recv.at[0], (across, index))

    shared = range(CHUNKS - 2) if split else range(CHUNKS)
    for j in range(slots):
        at = pl.ds(j * piece, piece)
        term = term_of(last, j)
        for m in range(max(hops - 2, 0), hops):
            ring_copy(m, j).wait_recv()
            term = term + arrived[m, at, :].astype(jnp.float32)
        value = term.astype(totals.dtype)
        if j in shared:
            totals[line, at, :] = value
            for k in range(1, lines):
                total_copy(k, j).start()
        else:
            out[out_rows(j), :] = value
            out_across(j).start()
            out_copy(j, core).start()

    for j in shared:
        at = pl.ds(j * piece, piece)
        for k in range(1, lines):
            total_in(k, j).wait_recv()
        value = totals[0, at, :].astype(jnp.float32)
        for other in range(1, lines):
            value = value + totals[other, at, :].astype(jnp.float32)
        out[out_rows(j), :] = value.astype(out.dtype)
        out_copy(j, core).start()
    if split:
        out_across(CHUNKS - 1).wait_recv()
        out_copy(CHUNKS - 1, core).start()

    for m in range(ring):
        cross_out(m).wait_send()
        if split:
            lend(m).wait_send()
    for m in range(hops):
        for j in range(slots):
            ring_copy(m, j).wait_send()
    own.wait()

    def finish_gain(k, carry):
        gain_push(k).wait_send()
        gain_pull(k).wait_recv()
        return carry

    lax.fori_loop(1, total, finish_gain, 0)
    for j in shared:
        for k in range(1, lines):
            total_copy(k, j).wait_send()
    for j in range(CHUNKS):
        out_copy(j, core).wait_send()
        out_copy(j, 1 - core).wait_recv()
    if split:
        out_across(CHUNKS - 2).wait_send()


def reduce_weight(groups, ring, partial, gain):
    total = groups * ring
    rows = partial.shape[0] // ring
    half, width = rows // 2, partial.shape[1]
    dma = pltpu.SemaphoreType.DMA
    vmem = pl.BlockSpec(memory_space=pltpu.VMEM)
    return pl.pallas_call(
        functools.partial(reduce_kernel, groups, ring),
        out_shape=(
            jax.ShapeDtypeStruct((rows, width), partial.dtype),
            jax.ShapeDtypeStruct((total,) + gain.shape, gain.dtype),
        ),
        in_specs=[vmem, vmem],
        out_specs=(vmem, vmem),
        scratch_shapes=[
            pltpu.VMEM((ring, half, width), partial.dtype),
            pltpu.VMEM((ring - 1, half, width), partial.dtype),
            pltpu.VMEM((ring - 1, half, width), partial.dtype),
            pltpu.VMEM((groups // 2, half, width), partial.dtype),
            pltpu.VMEM((ring, half // CHUNKS, width), partial.dtype),
            pltpu.VMEM((ring, half // CHUNKS, width), partial.dtype),
            dma,
            dma((total - 1,)),
            dma((total - 1,)),
            dma((ring,)),
            dma((ring,)),
            dma((ring - 1, CHUNKS)),
            dma((ring - 1, CHUNKS)),
            dma((max(groups // 2 - 1, 1), CHUNKS)),
            dma((max(groups // 2 - 1, 1), CHUNKS)),
            dma((CHUNKS,)),
            dma((CHUNKS,)),
            dma((ring,)),
            dma((ring,)),
            dma((1,)),
            dma((1,)),
        ],
        compiler_params=pltpu.CompilerParams(
            collective_id=2, has_side_effects=True, vmem_limit_bytes=40 << 20
        ),
        name="reduce_weight",
    )(partial, gain)


def on_device(
    groups, ring,
    context, residual, out_weight, norm_gain, user_vectors, positive, item_ids, item_counts, lengths
):
    tok_rows, head_width = context.shape
    model_width = residual.shape[1]
    items_here = lengths.shape[0]
    item_length = tok_rows // items_here
    users_here = user_vectors.shape[0]
    devices_all = groups * ring
    keys = jnp.concatenate([positive, item_ids, item_counts])
    lanes = 128 * pl.cdiv(keys.shape[0], 128)
    keys = jnp.broadcast_to(jnp.pad(keys, (0, lanes - keys.shape[0]))[None, :], (8, lanes))
    weight_all, users_all, keys_all = gather_inputs(groups, ring, out_weight, user_vectors, keys)
    users_all = users_all.reshape(devices_all * users_here, model_width)
    positive_all = keys_all[:, 0, :users_here].reshape(-1)
    ids_all = keys_all[:, 0, users_here : users_here + items_here].reshape(-1)
    counts_all = keys_all[:, 0, users_here + items_here : users_here + 2 * items_here].reshape(-1)
    attended = jnp.dot(context, weight_all, preferred_element_type=jnp.float32)
    stream = residual.astype(jnp.float32) + attended
    inverse_root_mean = lax.rsqrt(jnp.mean(stream * stream, axis=-1, keepdims=True) + EPSILON)
    normed = stream * inverse_root_mean * norm_gain
    positions = jnp.arange(item_length, dtype=jnp.int32)
    inside = (positions[None, :] < lengths[:, None])[:, :, None]
    length_float = lengths.astype(jnp.float32)[:, None]
    normed_items = normed.reshape(items_here, item_length, model_width)
    pooled = jnp.sum(jnp.where(inside, normed_items, 0.0), axis=1) / length_float
    emb_scale = lax.rsqrt(jnp.mean(pooled * pooled, axis=-1, keepdims=True) + EPSILON)
    embedding = (pooled * emb_scale).astype(jnp.bfloat16)
    emb_all = share(groups, ring, embedding).reshape(devices_all * items_here, model_width)
    me = lax.axis_index("dp") * ring + lax.axis_index("fsdp")
    items_all = jnp.arange(ids_all.shape[0], dtype=jnp.int32)
    onehot = items_all[None, :] == positive_all[:, None]
    positive_id = jnp.sum(jnp.where(onehot, ids_all[None, :], 0), axis=1)
    excluded = (ids_all[None, :] == positive_id[:, None]) & jnp.logical_not(onehot)
    scores = contract_last(users_all, emb_all)
    log_counts = jnp.log(counts_all.astype(jnp.float32))
    logits = jnp.where(excluded, MASKED_FILL, scores - log_counts[None, :])
    row_max = jnp.max(logits, axis=1, keepdims=True)
    weights = jnp.where(excluded, 0.0, jnp.exp(logits - row_max))
    row_total = jnp.sum(weights, axis=1, keepdims=True)
    log_total = row_max[:, 0] + jnp.log(row_total[:, 0])
    mean_loss = jnp.mean(log_total - jnp.sum(jnp.where(onehot, logits, 0.0), axis=1))
    logit_grad = (weights / row_total - onehot.astype(jnp.float32)).astype(jnp.bfloat16)
    own_users = lax.dynamic_slice_in_dim(logit_grad, me * users_here, users_here, axis=0)
    user_grad = jnp.dot(own_users, emb_all, preferred_element_type=jnp.float32).astype(
        jnp.bfloat16
    )
    own_items = lax.dynamic_slice_in_dim(logit_grad, me * items_here, items_here, axis=1)
    emb_grad = contract_rows(own_items, users_all)
    pooled_grad = emb_scale * emb_grad - pooled * emb_scale**3 * jnp.mean(
        pooled * emb_grad, axis=-1, keepdims=True
    )
    normed_grad = jnp.where(inside, pooled_grad[:, None, :] / length_float[:, :, None], 0.0)
    normed_grad = normed_grad.reshape(tok_rows, model_width)
    gain_part = jnp.sum(normed_grad * stream * inverse_root_mean, axis=0)
    scaled = norm_gain * normed_grad
    stream_grad = inverse_root_mean * scaled - stream * inverse_root_mean**3 * jnp.mean(
        scaled * stream, axis=-1, keepdims=True
    )
    residual_grad = stream_grad.astype(jnp.bfloat16)
    context_grad = contract_last(residual_grad, weight_all).astype(jnp.bfloat16)
    partial = contract_rows(context, residual_grad).astype(jnp.bfloat16)
    weight_grad, gain_all = reduce_weight(groups, ring, partial, gain_part[None, :])
    gain_grad = jnp.sum(gain_all[:, 0, :], axis=0)
    return (mean_loss, residual_grad, context_grad, weight_grad, gain_grad, user_grad)


def solution(mesh):
    placed = (
        P(("dp", "fsdp"), None),
        P(("dp", "fsdp"), None),
        P("fsdp", None),
        P(),
        P(("dp", "fsdp"), None),
        P(("dp", "fsdp")),
        P(("dp", "fsdp")),
        P(("dp", "fsdp")),
        P(("dp", "fsdp")),
    )
    return jax.shard_map(
        functools.partial(on_device, mesh.shape["dp"], mesh.shape["fsdp"]),
        mesh=mesh,
        in_specs=placed,
        out_specs=(
            P(),
            P(("dp", "fsdp"), None),
            P(("dp", "fsdp"), None),
            P("fsdp", None),
            P(),
            P(("dp", "fsdp"), None),
        ),
        check_vma=False,
    )
```

```python
import functools

import jax
import jax.numpy as jnp
from jax import lax
from jax.experimental import pallas as pl
from jax.experimental.pallas import tpu as pltpu
from jax.sharding import PartitionSpec as P

EPSILON = 1e-06
MASKED_FILL = -1e30
MESH = pl.DeviceIdType.MESH
CHUNKS = 4
LAG = 0


def contract_last(left, right):
    return lax.dot_general(
        left, right, (((1,), (1,)), ((), ())), preferred_element_type=jnp.float32
    )


def ring_place(index, count):
    return jnp.where(index % 2 == 0, index // 2, count - 1 - index // 2)


def ring_index(place, count):
    return jnp.where(place < count // 2, 2 * place, 2 * (count - 1 - place) + 1)


def remote(src, dst, send_sem, recv_sem, device):
    return pltpu.make_async_remote_copy(
        src_ref=src,
        dst_ref=dst,
        send_sem=send_sem,
        recv_sem=recv_sem,
        device_id=device,
        device_id_type=MESH,
    )


def rows_of(table, row):
    at = lax.broadcasted_iota(jnp.int32, table.shape, 0)
    return jnp.sum(jnp.where(at == row, table, 0.0), axis=0, keepdims=True)


def line_of(table, first, count):
    return jnp.concatenate([rows_of(table, first + r) for r in range(count)], axis=1)


def step_kernel(
    groups, ring, users_here, items_here,
    ctx_in, res_in, w_in, gain_in, u_in, pos_in, ids_in, counts_in, len_in,
    loss_out, rg_out, cg_out, out, gain_out, ug_out,
    ctx, ctx_t, res, w_out, u_out, k_out, acc, inv, users, pooled, emb, e_all, e_rows, e_grad,
    part_in, cross, held, arrived, totals, lent, borrowed,
    own_sem, w_send, w_recv, p_send, p_recv, y_send, y_recv,
    u_send, u_recv, k_send, k_recv, ul_send, ul_recv, kl_send, kl_recv,
    up_send, up_recv, kp_send, kp_recv,
    e_send, e_recv, ep_send, ep_recv,
    x_send, x_recv, r_send, r_recv, t_send, t_recv, o_send, o_recv,
    b_send, b_recv, f_send, f_recv,
):
    group, index = lax.axis_index("dp"), lax.axis_index("fsdp")
    total = groups * ring
    me = group * ring + index
    lines = groups // 2
    cells = lines * ring
    split = lines == 2
    line = group // 2
    core = lax.rem(group, 2)
    cell = line * ring + index
    partner = group + 1 - 2 * core
    across = lax.rem(group + 2, groups)
    place = ring_place(index, ring)
    turn = 1 - 2 * core
    ends = (
        ring_index(lax.rem(place + ring + turn, ring), ring),
        ring_index(lax.rem(place + ring - turn, ring), ring),
    )
    rows, width = w_in.shape
    tokens = ctx_in.shape[0]
    item_length = tokens // items_here
    users_total, items_total = total * users_here, total * items_here
    half = rows // 2
    part = half // CHUNKS
    hops = ring - 1

    def cell_device(c):
        return (2 * (c // ring) + core, lax.rem(c, ring))

    own = [
        pltpu.make_async_copy(u_in, u_out.at[me], own_sem.at[0]),
        pltpu.make_async_copy(ctx_in, ctx, own_sem.at[1]),
        pltpu.make_async_copy(
            w_in, w_out.at[pl.ds(pl.multiple_of(index * rows, rows), rows), :], own_sem.at[2]
        ),
        pltpu.make_async_copy(res_in, res, own_sem.at[3]),
    ]
    for copy in own:
        copy.start()

    barrier = pltpu.get_barrier_semaphore()

    def greet(k, carry):
        peer = cell_device(lax.rem(cell + k, cells))
        pl.semaphore_signal(barrier, inc=1, device_id=peer, device_id_type=MESH)
        return carry

    pl.semaphore_signal(barrier, inc=1, device_id=(partner, index), device_id_type=MESH)
    lax.fori_loop(1, cells, greet, 0)

    rows_users, rows_items = pl.cdiv(users_total, 128), pl.cdiv(items_total, 128)
    key_rows = k_out.shape[1]
    spot = lax.broadcasted_iota(jnp.int32, (key_rows, 128), 0) * 128 + lax.broadcasted_iota(
        jnp.int32, (key_rows, 128), 1
    )
    keys = jnp.zeros((key_rows, 128), jnp.float32)
    for ref, first, count in (
        (pos_in, 0, users_here),
        (ids_in, rows_users * 128, items_here),
        (counts_in, (rows_users + rows_items) * 128, items_here),
    ):
        for k in range(count):
            keys = jnp.where(spot == first + me * count + k, ref[k].astype(jnp.float32), keys)
    k_out[me] = keys

    pl.semaphore_wait(barrier, cells)

    def owner(m, way=turn):
        if m == hops + 2:
            return index
        away = -(m // 2) if m % 2 == 0 else m // 2
        return ring_index(lax.rem(place + ring + way * away, ring), ring)

    def chunk(j):
        if not split or j < CHUNKS - 2:
            return j
        return CHUNKS - 2 + (line if j == CHUNKS - 2 else 1 - line)

    def w_slice(who, j, side=core):
        start = pl.multiple_of(who * rows + side * half + chunk(j) * part, part)
        return w_out.at[pl.ds(start, part), :]

    def ring_pieces(m):
        if not split:
            return list(range(CHUNKS))
        first = [CHUNKS - 2] + list(range(CHUNKS - 2))
        return first + [CHUNKS - 1] if m == hops - 1 else first

    def w_ring(m, j, shift=0):
        ref = w_slice(owner(m + shift), j)
        src = ref
        if m + shift < 2:
            src = w_in.at[pl.ds(pl.multiple_of(core * half + chunk(j) * part, part), part), :]
        return remote(src, ref, w_send.at[m, j], w_recv.at[m, j], (group, ends[m % 2]))

    def w_part(m, j, side=core):
        ref = w_slice(owner(m + 2, 1 - 2 * side), j, side)
        return remote(ref, ref, p_send.at[m, j], p_recv.at[m, j], (partner, index))

    def w_across(m, j):
        ref = w_slice(owner(m + 2), j)
        return remote(ref, ref, y_send.at[m], y_recv.at[m], (across, index))

    small = (
        (u_out, u_send, u_recv, ul_send, ul_recv, up_send, up_recv),
        (k_out, k_send, k_recv, kl_send, kl_recv, kp_send, kp_recv),
    )

    def s_ring(a, m, shift):
        into, send, recv = small[a][:3]
        ref = into.at[group * ring + owner(m + shift)]
        return remote(ref, ref, send.at[m], recv.at[m], (group, ends[m % 2]))

    def s_line(a, s, k):
        into, _, _, send, recv = small[a][:5]
        ref = into.at[group * ring + owner(s + 2)]
        peer = lax.rem(group + 2 * k, groups)
        return remote(ref, ref, send.at[s, k - 1], recv.at[s, k - 1], (peer, index))

    def s_line_in(a, s, k):
        into, _, _, send, recv = small[a][:5]
        source = lax.rem(group + groups - 2 * k, groups)
        ref = into.at[source * ring + owner(s + 2)]
        return remote(ref, ref, send.at[s, k - 1], recv.at[s, k - 1], (source, index))

    def s_part(a, s, k):
        into, send, recv = small[a][0], small[a][5], small[a][6]
        source = lax.rem(group + groups - 2 * k, groups)
        ref = into.at[source * ring + owner(s + 2)]
        return remote(ref, ref, send.at[s, k], recv.at[s, k], (partner, index))

    def s_part_in(a, s, k):
        into, send, recv = small[a][0], small[a][5], small[a][6]
        source = lax.rem(partner + groups - 2 * k, groups)
        ref = into.at[source * ring + owner(s + 2, -turn)]
        return remote(ref, ref, send.at[s, k], recv.at[s, k], (partner, index))

    def spread(s):
        for a in (0, 1):
            for k in range(1, lines):
                s_line(a, s, k).start()
            s_part(a, s, 0).start()

    def s_pass(s):
        for a in (0, 1):
            for k in range(1, lines):
                s_line_in(a, s, k).wait_recv()
                s_part(a, s, k).start()

    def s_step(m):
        for a in (0, 1):
            s_ring(a, m, 2).wait_recv()
            if m + 2 < hops:
                s_ring(a, m + 2, 0).start()
        spread(m)
        if m == 1:
            s_pass(hops)
        if m >= 2:
            s_pass(m - 2)

    def has_across(m):
        return split and m < hops - 1

    def w_pass(m):
        if has_across(m):
            w_across(m, CHUNKS - 1).wait_recv()
            w_part(m, CHUNKS - 1).start()
            if m + 2 == hops - 1:
                w_ring(m + 2, CHUNKS - 1).start()

    tile = 256

    def forward(who, start=False):
        at = pl.ds(pl.multiple_of(who * rows, rows), rows)

        def tiles(n, carry):
            cols = pl.ds(pl.multiple_of(n * tile, tile), tile)
            base = res[:, cols].astype(jnp.float32) if start else acc[:, cols]
            acc[:, cols] = base + jnp.dot(
                ctx[:, at], w_out[at, cols], preferred_element_type=jnp.float32
            )
            return carry

        lax.fori_loop(0, width // tile, tiles, 0)

    def w_ready(m):
        for j in range(CHUNKS):
            w_part(m, j, 1 - core).wait_recv()

    def turn_over(s, carry):
        at = pl.ds(pl.multiple_of(s * rows, rows), rows)
        ctx_t[at, :] = ctx[:, at].astype(jnp.float32).T.astype(ctx_t.dtype)
        return carry

    for j in ring_pieces(0):
        for m in range(min(2, hops)):
            w_ring(m, j).start()
    own[0].wait()
    for m in range(min(2, hops)):
        for a in (0, 1):
            s_ring(a, m, 0).start()
    spread(hops)
    own[1].wait()
    own[2].wait()
    own[3].wait()
    forward(index, True)
    for pair in range(pl.cdiv(hops, 2)):
        both = [m for m in (2 * pair, 2 * pair + 1) if m < hops]
        for j in ring_pieces(both[0]):
            for m in both:
                w_ring(m, j, 2).wait_recv()
                if m + 2 < hops:
                    w_ring(m + 2, j).start()
                if has_across(m) and j == CHUNKS - 2:
                    w_across(m, j).start()
                w_part(m, j).start()
            if pair >= 1 and j == ring_pieces(0)[0]:
                for m in (2 * pair - 2, 2 * pair - 1):
                    w_pass(m)
        for m in both:
            s_step(m)
        if pair == 0:
            lax.fori_loop(0, ring, turn_over, 0)
        if pair >= 1:
            for m in (2 * pair - 2, 2 * pair - 1):
                w_ready(m)
            forward(owner(2 * pair))
            forward(owner(2 * pair + 1))
    for m in both:
        w_pass(m)
        w_ready(m)
        forward(owner(m + 2, 1))
    for m in range(max(hops - 2, 0), hops):
        s_pass(m)

    gain = gain_in[...]
    block = 32
    cap = 16

    def spans(i):
        return len_in[i].astype(jnp.float32)

    def inside_of(i, r):
        at = r * block + lax.broadcasted_iota(jnp.int32, (block, 1), 0)
        return (at < len_in[i]).astype(jnp.float32)

    values = []
    for i in range(items_here):

        def pool(r, carry, i=i):
            at = pl.ds(pl.multiple_of(i * item_length + r * block, block), block)
            x = acc[at, :]
            scale = lax.rsqrt(jnp.sum(x * x, axis=1, keepdims=True) / width + EPSILON)
            inv[at, :] = scale
            y = x * (scale * inside_of(i, r))
            for q in range(block // 8):
                carry = carry + y[q * 8 : q * 8 + 8, :]
            return carry

        summed = lax.fori_loop(
            0, item_length // block, pool, jnp.zeros((8, width), jnp.float32)
        )
        summed = jnp.sum(summed, axis=0, keepdims=True)
        mean = gain * summed / spans(i)
        scale = lax.rsqrt(jnp.mean(mean * mean, axis=1, keepdims=True) + EPSILON)
        pooled[pl.ds(i, 1), :] = mean
        values.append((mean, scale))
        emb[pl.ds(i, 1), :] = mean * scale
    e_all[me] = emb[pl.ds(0, items_here), :].astype(e_all.dtype)

    def e_push(k):
        return remote(
            e_all.at[me], e_all.at[me], e_send.at[k - 1], e_recv.at[k - 1],
            cell_device(lax.rem(cell + k, cells)),
        )

    def e_slot(k, side=core):
        c = lax.rem(cell + cells - k, cells)
        return (2 * (c // ring) + side) * ring + lax.rem(c, ring)

    def e_pull(k):
        ref = e_all.at[e_slot(k)]
        return remote(
            ref, ref, e_send.at[k - 1], e_recv.at[k - 1], cell_device(lax.rem(cell + cells - k, cells))
        )

    def e_part(k, side=core):
        ref = e_all.at[e_slot(k, side)]
        return remote(ref, ref, ep_send.at[k], ep_recv.at[k], (partner, index))

    def push(k, carry):
        e_push(k).start()
        return carry

    lax.fori_loop(1, cells, push, 0)
    e_part(0).start()

    for m in range(ring):
        for a in (0, 1):
            for k in range(lines):
                s_part_in(a, m, k).wait_recv()

    def join(p, carry):
        block_rows = [u_out[2 * p].astype(jnp.float32), u_out[2 * p + 1].astype(jnp.float32)]
        at = pl.ds(pl.multiple_of(p * 2 * users_here, 2 * users_here), 2 * users_here)
        users[at, :] = jnp.concatenate(block_rows, axis=0).astype(users.dtype)
        return carry

    lax.fori_loop(0, total // 2, join, 0)
    table = lax.fori_loop(
        0, total, lambda d, t: t + k_out[d], jnp.zeros((key_rows, 128), jnp.float32)
    )
    positive = line_of(table, 0, rows_users)[:, :users_total]
    wide = (items_total, rows_items * 128)
    diagonal = lax.broadcasted_iota(jnp.int32, wide, 0) == lax.broadcasted_iota(jnp.int32, wide, 1)

    def column(first):
        row = line_of(table, first, rows_items)
        return jnp.sum(jnp.where(diagonal, row, 0.0), axis=1, keepdims=True)

    ids = column(rows_users)
    log_counts = jnp.log(column(rows_users + rows_items))
    item_at = lax.broadcasted_iota(jnp.int32, (items_total, users_total), 0).astype(jnp.float32)
    chosen = item_at == positive
    positive_id = jnp.sum(jnp.where(chosen, ids, 0.0), axis=0, keepdims=True)
    excluded = (ids == positive_id) & jnp.logical_not(chosen)

    def relay(k, carry):
        e_pull(k).wait_recv()
        e_part(k).start()
        return carry

    lax.fori_loop(1, cells, relay, 0)

    def landed(k, carry):
        e_part(k, 1 - core).wait_recv()
        return carry

    lax.fori_loop(0, cells, landed, 0)
    for d in range(total):
        e_rows[pl.ds(d * items_here, items_here), :] = e_all[d].astype(jnp.float32)
    emb_all = e_rows[...].astype(jnp.bfloat16)
    scores = contract_last(emb_all, users[...])
    logits = jnp.where(excluded, MASKED_FILL, scores - log_counts)
    top = jnp.max(logits, axis=0, keepdims=True)
    weights = jnp.where(excluded, 0.0, jnp.exp(logits - top))
    sums = jnp.sum(weights, axis=0, keepdims=True)
    logit_grad = (weights / sums - chosen.astype(jnp.float32)).astype(jnp.bfloat16)
    e_grad[...] = jnp.dot(logit_grad, users[...], preferred_element_type=jnp.float32)

    for i in range(items_here):
        mean, scale = values[i]
        grad = e_grad[pl.ds(me * items_here + i, 1), :]
        pooled_grad = scale * grad - mean * (
            scale * scale * scale * jnp.mean(mean * grad, axis=1, keepdims=True)
        )
        reach = jnp.broadcast_to(gain * (pooled_grad / spans(i)), (8, width))

        def back(r, carry, i=i, reach=reach):
            at = pl.ds(pl.multiple_of(i * item_length + r * cap, cap), cap)
            x = acc[at, :]
            scale = inv[at, :]
            h = jnp.concatenate([reach] * (cap // 8), axis=0)
            where = r * cap + lax.broadcasted_iota(jnp.int32, (cap, 1), 0)
            keep = jnp.where(where < len_in[i], scale, 0.0)
            dots = jnp.sum(x * h, axis=1, keepdims=True) / width
            rg_out[at, :] = (keep * h - x * (keep * scale * scale * dots)).astype(rg_out.dtype)
            return carry

        lax.fori_loop(0, item_length // cap, back, 0, unroll=2)

    def target(m, way=turn):
        if m == hops:
            return index
        away = ring // 2 - m // 2 if m % 2 == 0 else m // 2 - (ring - 1) // 2
        return ring_index(lax.rem(place + ring + way * away, ring), ring)

    def weight_block(m):
        at = pl.ds(pl.multiple_of(target(m) * rows, rows), rows)
        wide = 512

        def tiles(n, carry):
            cols = pl.ds(pl.multiple_of(n * wide, wide), wide)
            part_in[at, cols] = jnp.dot(
                ctx_t[at, :], rg_out[:, cols], preferred_element_type=jnp.float32
            ).astype(part_in.dtype)
            return carry

        lax.fori_loop(0, width // wide, tiles, 0)

    def cross_out(m):
        start = pl.multiple_of(target(m, -turn) * rows + (1 - core) * half, half)
        return remote(
            part_in.at[pl.ds(start, half), :], cross.at[m], x_send.at[m], x_recv.at[m],
            (partner, index),
        )

    slots = CHUNKS - 1 if split else CHUNKS

    def ring_copy(s, c):
        at = pl.ds(c * part, part)
        return remote(
            held.at[s, at, :], arrived.at[s, at, :], r_send.at[s, c], r_recv.at[s, c],
            (group, ends[s % 2]),
        )

    def local_term(s, j):
        offset = chunk(j) * part
        start = pl.multiple_of(target(s) * rows + core * half + offset, part)
        mine = part_in[pl.ds(start, part), :].astype(jnp.float32)
        return mine + cross[s, pl.ds(pl.multiple_of(offset, part), part), :].astype(jnp.float32)

    def lend(s):
        return remote(lent.at[s], borrowed.at[s], b_send.at[s], b_recv.at[s], (across, index))

    def prepare(s):
        cross_out(s).wait_recv()
        if split:
            lent[s] = local_term(s, CHUNKS - 1).astype(lent.dtype)
            lend(s).start()

    def term_of(s, j):
        term = local_term(s, j)
        if split and j == CHUNKS - 2:
            lend(s).wait_recv()
            term = term + borrowed[s].astype(jnp.float32)
        return term

    head_width = cg_out.shape[1]

    def context_block(n):
        at = pl.ds(n * tile, tile)

        def tiles(r, carry):
            rr = pl.ds(pl.multiple_of(r * tile, tile), tile)
            cg_out[rr, at] = contract_last(rg_out[rr, :], w_out[at, :]).astype(cg_out.dtype)
            return carry

        lax.fori_loop(0, tokens // tile, tiles, 0)

    def last_bits():
        log_total = top + jnp.log(sums)
        picked = jnp.sum(jnp.where(chosen, logits, 0.0), axis=0, keepdims=True)
        loss_out[...] = jnp.mean(log_total - picked, axis=1, keepdims=True)
        shape = (16, users_total)
        seat = lax.broadcasted_iota(jnp.int32, shape, 0)
        mine = lax.broadcasted_iota(jnp.int32, shape, 1) == me * users_here + seat
        mine = (mine & (seat < users_here)).astype(jnp.float32).astype(jnp.bfloat16)
        own_grad = contract_last(mine, logit_grad).astype(jnp.bfloat16)
        found = jnp.dot(own_grad, emb_all, preferred_element_type=jnp.float32)
        ug_out[...] = found[:users_here, :].astype(ug_out.dtype)
        e = e_rows[...]
        g = e_grad[...]
        along = jnp.mean(e * g, axis=1, keepdims=True)
        gain_out[...] = jnp.sum(e * (g - e * along), axis=0, keepdims=True) / gain

    extra = [functools.partial(context_block, n) for n in range(head_width // tile)]
    extra.append(last_bits)

    weight_block(0)
    cross_out(0).start()
    for m in (1, 2):
        weight_block(m)
    for m in (1, 2):
        cross_out(m).start()
    for m in range(min(2, hops)):
        prepare(m)
    for m in range(hops):
        for j in range(slots):
            at = pl.ds(j * part, part)
            if j == max(CHUNKS - 2, 0) and m + 2 < ring:
                prepare(m + 2)
            term = term_of(m, j)
            if m >= 2:
                ring_copy(m - 2, j).wait_recv()
                term = term + arrived[m - 2, at, :].astype(jnp.float32)
            held[m, at, :] = term.astype(held.dtype)
            ring_copy(m, j).start()
        if 2 * m + 3 < ring:
            ahead = [s for s in (2 * m + 3, 2 * m + 4) if s < ring]
            for s in ahead:
                weight_block(s)
            for s in ahead:
                cross_out(s).start()
        elif extra:
            extra.pop(0)()
    for job in extra:
        job()
    last = hops

    def total_copy(k, j):
        ref = totals.at[line, pl.ds(j * part, part), :]
        return remote(
            ref, ref, t_send.at[k - 1, j], t_recv.at[k - 1, j],
            (lax.rem(group + 2 * k, groups), index),
        )

    def total_in(k, j):
        source = lax.rem(group + groups - 2 * k, groups)
        ref = totals.at[source // 2, pl.ds(j * part, part), :]
        return remote(ref, ref, t_send.at[k - 1, j], t_recv.at[k - 1, j], (source, index))

    def out_rows(j, side=core):
        return pl.ds(pl.multiple_of(side * half + chunk(j) * part, part), part)

    def out_copy(j, side):
        ref = out.at[out_rows(j, side), :]
        return remote(ref, ref, o_send.at[j], o_recv.at[j], (partner, index))

    def out_across(j):
        ref = out.at[out_rows(j), :]
        return remote(ref, ref, f_send.at[0], f_recv.at[0], (across, index))

    shared = range(CHUNKS - 2) if split else range(CHUNKS)
    for j in range(slots):
        at = pl.ds(j * part, part)
        term = term_of(last, j)
        for m in range(max(hops - 2, 0), hops):
            ring_copy(m, j).wait_recv()
            term = term + arrived[m, at, :].astype(jnp.float32)
        value = term.astype(totals.dtype)
        if j in shared:
            totals[line, at, :] = value
            for k in range(1, lines):
                total_copy(k, j).start()
        else:
            out[out_rows(j), :] = value
            out_across(j).start()
            out_copy(j, core).start()

    for j in shared:
        at = pl.ds(j * part, part)
        for k in range(1, lines):
            total_in(k, j).wait_recv()
        value = totals[0, at, :].astype(jnp.float32)
        for other in range(1, lines):
            value = value + totals[other, at, :].astype(jnp.float32)
        out[out_rows(j), :] = value.astype(out.dtype)
        out_copy(j, core).start()
    if split:
        out_across(CHUNKS - 1).wait_recv()
        out_copy(CHUNKS - 1, core).start()

    for m in range(hops):
        for j in ring_pieces(m):
            w_ring(m, j).wait_send()
        if has_across(m):
            w_across(m, CHUNKS - 2).wait_send()
        for j in range(CHUNKS):
            w_part(m, j).wait_send()
        for a in (0, 1):
            s_ring(a, m, 0).wait_send()
    for m in range(ring):
        for a in (0, 1):
            for k in range(1, lines):
                s_line(a, m, k).wait_send()
            for k in range(lines):
                s_part(a, m, k).wait_send()

    def sent(k, carry):
        e_push(k).wait_send()
        e_part(k).wait_send()
        return carry

    lax.fori_loop(1, cells, sent, 0)
    e_part(0).wait_send()
    for m in range(ring):
        cross_out(m).wait_send()
        if split:
            lend(m).wait_send()
    for m in range(hops):
        for j in range(slots):
            ring_copy(m, j).wait_send()
    for j in shared:
        for k in range(1, lines):
            total_copy(k, j).wait_send()
    for j in range(CHUNKS):
        out_copy(j, core).wait_send()
        out_copy(j, 1 - core).wait_recv()
    if split:
        out_across(CHUNKS - 2).wait_send()


def on_device(
    groups, ring,
    context, residual, out_weight, norm_gain, user_vectors, positive, item_ids, item_counts, lengths
):
    tokens, head_width = context.shape
    width = residual.shape[1]
    rows = out_weight.shape[0]
    half = rows // 2
    items_here = lengths.shape[0]
    users_here = user_vectors.shape[0]
    total = groups * ring
    lines = groups // 2
    cells = lines * ring
    hops = ring - 1
    users_total, items_total = total * users_here, total * items_here
    key_rows = pl.cdiv(users_total, 128) + 2 * pl.cdiv(items_total, 128)
    key_rows = 8 * pl.cdiv(key_rows, 8)
    dma = pltpu.SemaphoreType.DMA
    half_type, full_type = jnp.bfloat16, jnp.float32
    vmem = pl.BlockSpec(memory_space=pltpu.VMEM)
    smem = pl.BlockSpec(memory_space=pltpu.SMEM)
    anywhere = pl.BlockSpec(memory_space=pl.ANY)
    loss, residual_grad, context_grad, weight_grad, gain_grad, user_grad = pl.pallas_call(
        functools.partial(step_kernel, groups, ring, users_here, items_here),
        out_shape=(
            jax.ShapeDtypeStruct((1, 1), full_type),
            jax.ShapeDtypeStruct((tokens, width), half_type),
            jax.ShapeDtypeStruct((tokens, head_width), half_type),
            jax.ShapeDtypeStruct((rows, width), half_type),
            jax.ShapeDtypeStruct((1, width), full_type),
            jax.ShapeDtypeStruct((users_here, width), half_type),
        ),
        in_specs=[anywhere, anywhere, anywhere, vmem, anywhere, smem, smem, smem, smem],
        out_specs=(vmem,) * 6,
        scratch_shapes=[
            pltpu.VMEM((tokens, head_width), half_type),
            pltpu.VMEM((head_width, tokens), half_type),
            pltpu.VMEM((tokens, width), half_type),
            pltpu.VMEM((ring * rows, width), half_type),
            pltpu.VMEM((total, users_here, width), half_type),
            pltpu.VMEM((total, key_rows, 128), full_type),
            pltpu.VMEM((tokens, width), full_type),
            pltpu.VMEM((tokens, 1), full_type),
            pltpu.VMEM((users_total, width), half_type),
            pltpu.VMEM((8, width), full_type),
            pltpu.VMEM((8, width), full_type),
            pltpu.VMEM((total, items_here, width), half_type),
            pltpu.VMEM((items_total, width), full_type),
            pltpu.VMEM((items_total, width), full_type),
            pltpu.VMEM((ring * rows, width), half_type),
            pltpu.VMEM((ring, half, width), half_type),
            pltpu.VMEM((hops, half, width), half_type),
            pltpu.VMEM((hops, half, width), half_type),
            pltpu.VMEM((lines, half, width), half_type),
            pltpu.VMEM((ring, half // CHUNKS, width), half_type),
            pltpu.VMEM((ring, half // CHUNKS, width), half_type),
            dma((4,)),
        ]
        + [dma((hops, CHUNKS))] * 4
        + [dma((hops,))] * 2
        + [dma((hops,))] * 4
        + [dma((ring, max(lines - 1, 1)))] * 4
        + [dma((ring, lines))] * 4
        + [dma((max(cells - 1, 1),))] * 2
        + [dma((cells,))] * 2
        + [dma((ring,))] * 2
        + [dma((hops, CHUNKS))] * 2
        + [dma((max(lines - 1, 1), CHUNKS))] * 2
        + [dma((CHUNKS,))] * 2
        + [dma((ring,))] * 2
        + [dma((1,))] * 2,
        compiler_params=pltpu.CompilerParams(
            collective_id=0, has_side_effects=True, vmem_limit_bytes=48 << 20
        ),
        name="whole_step",
    )(
        context, residual, out_weight, norm_gain[None, :], user_vectors,
        positive, item_ids, item_counts, lengths,
    )
    return (loss[0, 0], residual_grad, context_grad, weight_grad, gain_grad[0], user_grad)


def solution(mesh):
    placed = (
        P(("dp", "fsdp"), None),
        P(("dp", "fsdp"), None),
        P("fsdp", None),
        P(),
        P(("dp", "fsdp"), None),
        P(("dp", "fsdp")),
        P(("dp", "fsdp")),
        P(("dp", "fsdp")),
        P(("dp", "fsdp")),
    )
    return jax.shard_map(
        functools.partial(on_device, mesh.shape["dp"], mesh.shape["fsdp"]),
        mesh=mesh,
        in_specs=placed,
        out_specs=(
            P(),
            P(("dp", "fsdp"), None),
            P(("dp", "fsdp"), None),
            P("fsdp", None),
            P(),
            P(("dp", "fsdp"), None),
        ),
        check_vma=False,
    )
```

```python
import functools

import jax
import jax.numpy as jnp
from jax import lax
from jax.experimental import pallas as pl
from jax.experimental.pallas import tpu as pltpu
from jax.sharding import PartitionSpec as P

EPSILON = 1e-06
MASKED_FILL = -1e30
MESH = pl.DeviceIdType.MESH
CHUNKS = 4
LAG = 1


def contract_last(left, right):
    return lax.dot_general(
        left, right, (((1,), (1,)), ((), ())), preferred_element_type=jnp.float32
    )


def ring_place(index, count):
    return jnp.where(index % 2 == 0, index // 2, count - 1 - index // 2)


def ring_index(place, count):
    return jnp.where(place < count // 2, 2 * place, 2 * (count - 1 - place) + 1)


def remote(src, dst, send_sem, recv_sem, device):
    return pltpu.make_async_remote_copy(
        src_ref=src,
        dst_ref=dst,
        send_sem=send_sem,
        recv_sem=recv_sem,
        device_id=device,
        device_id_type=MESH,
    )


def rows_of(table, row):
    at = lax.broadcasted_iota(jnp.int32, table.shape, 0)
    return jnp.sum(jnp.where(at == row, table, 0.0), axis=0, keepdims=True)


def line_of(table, first, count):
    return jnp.concatenate([rows_of(table, first + r) for r in range(count)], axis=1)


def step_kernel(
    groups, ring, users_here, items_here,
    ctx_in, res_in, w_in, gain_hbm, u_in, pos_hbm, ids_hbm, counts_hbm, len_hbm,
    loss_out, rg_out, cg_out, out, gain_out, ug_out,
    ctx, ctx_t, res, w_out, u_out, k_out, acc, inv, users, pooled, emb, e_all, e_rows, e_grad,
    part_in, cross, held, arrived, totals, lent, borrowed,
    gain_in, pos_in, ids_in, counts_in, len_in,
    own_sem, w_send, w_recv, p_send, p_recv, y_send, y_recv,
    u_send, u_recv, k_send, k_recv, ul_send, ul_recv, kl_send, kl_recv,
    up_send, up_recv, kp_send, kp_recv,
    e_send, e_recv, ep_send, ep_recv,
    x_send, x_recv, r_send, r_recv, t_send, t_recv, o_send, o_recv,
    b_send, b_recv, f_send, f_recv,
):
    group, index = lax.axis_index("dp"), lax.axis_index("fsdp")
    total = groups * ring
    me = group * ring + index
    lines = groups // 2
    cells = lines * ring
    split = lines == 2
    line = group // 2
    core = lax.rem(group, 2)
    cell = line * ring + index
    partner = group + 1 - 2 * core
    across = lax.rem(group + 2, groups)
    place = ring_place(index, ring)
    turn = 1 - 2 * core
    ends = (
        ring_index(lax.rem(place + ring + turn, ring), ring),
        ring_index(lax.rem(place + ring - turn, ring), ring),
    )
    rows, width = w_in.shape
    tokens = ctx_in.shape[0]
    item_length = tokens // items_here
    users_total, items_total = total * users_here, total * items_here
    half = rows // 2
    part = half // CHUNKS
    hops = ring - 1

    def cell_device(c):
        return (2 * (c // ring) + core, lax.rem(c, ring))

    own = [
        pltpu.make_async_copy(u_in, u_out.at[me], own_sem.at[0]),
        pltpu.make_async_copy(ctx_in, ctx, own_sem.at[1]),
        pltpu.make_async_copy(
            w_in, w_out.at[pl.ds(pl.multiple_of(index * rows, rows), rows), :], own_sem.at[2]
        ),
        pltpu.make_async_copy(res_in, res, own_sem.at[3]),
        pltpu.make_async_copy(gain_hbm, gain_in, own_sem.at[4]),
        pltpu.make_async_copy(pos_hbm, pos_in, own_sem.at[5]),
        pltpu.make_async_copy(ids_hbm, ids_in, own_sem.at[6]),
        pltpu.make_async_copy(counts_hbm, counts_in, own_sem.at[7]),
        pltpu.make_async_copy(len_hbm, len_in, own_sem.at[8]),
    ]
    for copy in own[4:] + own[:4]:
        copy.start()

    barrier = pltpu.get_barrier_semaphore()

    def greet(k, carry):
        peer = cell_device(lax.rem(cell + k, cells))
        pl.semaphore_signal(barrier, inc=1, device_id=peer, device_id_type=MESH)
        return carry

    near = [(partner, index), (group, ends[0]), (group, ends[1]), (across, index)]
    for peer in near if split else near[:1]:
        pl.semaphore_signal(barrier, inc=1, device_id=peer, device_id_type=MESH)
    if not split:
        lax.fori_loop(1, cells, greet, 0)

    for copy in own[4:]:
        copy.wait()
    rows_users, rows_items = pl.cdiv(users_total, 128), pl.cdiv(items_total, 128)
    key_rows = k_out.shape[1]
    spot = lax.broadcasted_iota(jnp.int32, (key_rows, 128), 0) * 128 + lax.broadcasted_iota(
        jnp.int32, (key_rows, 128), 1
    )
    keys = jnp.zeros((key_rows, 128), jnp.float32)
    for ref, first, count in (
        (pos_in, 0, users_here),
        (ids_in, rows_users * 128, items_here),
        (counts_in, (rows_users + rows_items) * 128, items_here),
    ):
        for k in range(count):
            keys = jnp.where(spot == first + me * count + k, ref[k].astype(jnp.float32), keys)
    k_out[me] = keys

    pl.semaphore_wait(barrier, len(near) if split else cells)

    def owner(m, way=turn):
        if m == hops + 2:
            return index
        away = -(m // 2) if m % 2 == 0 else m // 2
        return ring_index(lax.rem(place + ring + way * away, ring), ring)

    def chunk(j):
        if not split or j < CHUNKS - 2:
            return j
        return CHUNKS - 2 + (line if j == CHUNKS - 2 else 1 - line)

    def w_slice(who, j, side=core):
        start = pl.multiple_of(who * rows + side * half + chunk(j) * part, part)
        return w_out.at[pl.ds(start, part), :]

    def ring_pieces(m):
        if not split:
            return list(range(CHUNKS))
        first = [CHUNKS - 2] + list(range(CHUNKS - 2))
        return first + [CHUNKS - 1] if m == hops - 1 else first

    def w_ring(m, j, shift=0):
        ref = w_slice(owner(m + shift), j)
        src = ref
        if m + shift < 2:
            src = w_in.at[pl.ds(pl.multiple_of(core * half + chunk(j) * part, part), part), :]
        return remote(src, ref, w_send.at[m, j], w_recv.at[m, j], (group, ends[m % 2]))

    def w_part(m, j, side=core):
        ref = w_slice(owner(m + 2, 1 - 2 * side), j, side)
        return remote(ref, ref, p_send.at[m, j], p_recv.at[m, j], (partner, index))

    def w_across(m, j):
        ref = w_slice(owner(m + 2), j)
        return remote(ref, ref, y_send.at[m], y_recv.at[m], (across, index))

    small = (
        (u_out, u_send, u_recv, ul_send, ul_recv, up_send, up_recv),
        (k_out, k_send, k_recv, kl_send, kl_recv, kp_send, kp_recv),
    )

    def s_ring(a, m, shift):
        into, send, recv = small[a][:3]
        ref = into.at[group * ring + owner(m + shift)]
        return remote(ref, ref, send.at[m], recv.at[m], (group, ends[m % 2]))

    def s_line(a, s, k):
        into, _, _, send, recv = small[a][:5]
        ref = into.at[group * ring + owner(s + 2)]
        peer = lax.rem(group + 2 * k, groups)
        return remote(ref, ref, send.at[s, k - 1], recv.at[s, k - 1], (peer, index))

    def s_line_in(a, s, k):
        into, _, _, send, recv = small[a][:5]
        source = lax.rem(group + groups - 2 * k, groups)
        ref = into.at[source * ring + owner(s + 2)]
        return remote(ref, ref, send.at[s, k - 1], recv.at[s, k - 1], (source, index))

    def s_part(a, s, k):
        into, send, recv = small[a][0], small[a][5], small[a][6]
        source = lax.rem(group + groups - 2 * k, groups)
        ref = into.at[source * ring + owner(s + 2)]
        return remote(ref, ref, send.at[s, k], recv.at[s, k], (partner, index))

    def s_part_in(a, s, k):
        into, send, recv = small[a][0], small[a][5], small[a][6]
        source = lax.rem(partner + groups - 2 * k, groups)
        ref = into.at[source * ring + owner(s + 2, -turn)]
        return remote(ref, ref, send.at[s, k], recv.at[s, k], (partner, index))

    def spread(s):
        for a in (0, 1):
            for k in range(1, lines):
                s_line(a, s, k).start()
            s_part(a, s, 0).start()

    def s_pass(s):
        for a in (0, 1):
            for k in range(1, lines):
                s_line_in(a, s, k).wait_recv()
                s_part(a, s, k).start()

    def s_step(m):
        for a in (0, 1):
            s_ring(a, m, 2).wait_recv()
            if m + 2 < hops:
                s_ring(a, m + 2, 0).start()
        spread(m)
        if m == 1:
            s_pass(hops)
        if m >= 2:
            s_pass(m - 2)

    def has_across(m):
        return split and m < hops - 1

    def w_pass(m):
        if has_across(m):
            w_across(m, CHUNKS - 1).wait_recv()
            w_part(m, CHUNKS - 1).start()
            if m + 2 == hops - 1:
                w_ring(m + 2, CHUNKS - 1).start()

    def drain_gather():
        for m in range(hops):
            for j in ring_pieces(m):
                w_ring(m, j).wait_send()
            if has_across(m):
                w_across(m, CHUNKS - 2).wait_send()
            for j in range(CHUNKS):
                w_part(m, j).wait_send()
            for a in (0, 1):
                s_ring(a, m, 0).wait_send()
        for m in range(ring):
            for a in (0, 1):
                for k in range(1, lines):
                    s_line(a, m, k).wait_send()
                for k in range(lines):
                    s_part(a, m, k).wait_send()

    def both_rows(a, b):
        return [pl.ds(pl.multiple_of(who * rows, rows), rows) for who in (a, b)]

    def forward(a, b, start=False):
        first, second = both_rows(a, b)
        left = jnp.concatenate([ctx[:, first], ctx[:, second]], axis=1)
        right = jnp.concatenate([w_out[first, :], w_out[second, :]], axis=0)
        base = res[...].astype(jnp.float32) if start else acc[...]
        acc[...] = base + jnp.dot(left, right, preferred_element_type=jnp.float32)

    def w_ready(m):
        for j in range(CHUNKS):
            w_part(m, j, 1 - core).wait_recv()

    def turn_over(s, carry):
        at = pl.ds(pl.multiple_of(s * rows, rows), rows)
        ctx_t[at, :] = ctx[:, at].astype(jnp.float32).T.astype(ctx_t.dtype)
        return carry

    for j in ring_pieces(0):
        for m in range(2):
            w_ring(m, j).start()
    own[0].wait()
    spread(hops)

    def s_first():
        for m in range(2):
            for a in (0, 1):
                s_ring(a, m, 0).start()

    small_jobs = [[s_first]]
    for m in range(0, hops, 2):
        small_jobs.append([functools.partial(s_step, q) for q in (m, m + 1) if q < hops])
    for _ in range(LAG):
        small_jobs.insert(0, [])

    def small_turn():
        for job in small_jobs.pop(0) if small_jobs else ():
            job()

    small_turn()
    for copy in own[1:4]:
        copy.wait()
    pairs = ring // 2
    for pair in range(pairs):
        both = [m for m in (2 * pair, 2 * pair + 1) if m < hops]
        for j in ring_pieces(both[0]):
            for m in both:
                w_ring(m, j, 2).wait_recv()
                if m + 2 < hops:
                    w_ring(m + 2, j).start()
                if has_across(m) and j == CHUNKS - 2:
                    w_across(m, j).start()
                w_part(m, j).start()
            if pair >= 1 and j == ring_pieces(0)[0]:
                for m in (2 * pair - 2, 2 * pair - 1):
                    w_pass(m)
        small_turn()
        if pair == 0:
            lax.fori_loop(0, ring, turn_over, 0)
        else:
            for m in (2 * pair - 2, 2 * pair - 1):
                w_ready(m)
            forward(owner(2 * pair), owner(2 * pair + 1), pair == 1)
    w_pass(hops - 1)
    w_ready(hops - 1)
    forward(owner(hops + 1), index, pairs == 1)
    small_turn()

    gain = gain_in[...]
    block = 32
    cap = 16

    def spans(i):
        return len_in[i].astype(jnp.float32)

    def inside_of(i, r):
        at = r * block + lax.broadcasted_iota(jnp.int32, (block, 1), 0)
        return (at < len_in[i]).astype(jnp.float32)

    values = []
    for i in range(items_here):

        def pool(r, carry, i=i):
            at = pl.ds(pl.multiple_of(i * item_length + r * block, block), block)
            x = acc[at, :]
            scale = lax.rsqrt(jnp.sum(x * x, axis=1, keepdims=True) / width + EPSILON)
            inv[at, :] = scale
            y = x * (scale * inside_of(i, r))
            for q in range(block // 8):
                carry = carry + y[q * 8 : q * 8 + 8, :]
            return carry

        summed = lax.fori_loop(
            0, item_length // block, pool, jnp.zeros((8, width), jnp.float32)
        )
        summed = jnp.sum(summed, axis=0, keepdims=True)
        mean = gain * summed / spans(i)
        scale = lax.rsqrt(jnp.mean(mean * mean, axis=1, keepdims=True) + EPSILON)
        pooled[pl.ds(i, 1), :] = mean
        values.append((mean, scale))
        emb[pl.ds(i, 1), :] = mean * scale
    e_all[me] = emb[pl.ds(0, items_here), :].astype(e_all.dtype)

    def e_push(k):
        return remote(
            e_all.at[me], e_all.at[me], e_send.at[k - 1], e_recv.at[k - 1],
            cell_device(lax.rem(cell + k, cells)),
        )

    def e_slot(k, side=core):
        c = lax.rem(cell + cells - k, cells)
        return (2 * (c // ring) + side) * ring + lax.rem(c, ring)

    def e_pull(k):
        ref = e_all.at[e_slot(k)]
        return remote(
            ref, ref, e_send.at[k - 1], e_recv.at[k - 1], cell_device(lax.rem(cell + cells - k, cells))
        )

    def e_part(k, side=core):
        ref = e_all.at[e_slot(k, side)]
        return remote(ref, ref, ep_send.at[k], ep_recv.at[k], (partner, index))

    def push(k, carry):
        e_push(k).start()
        return carry

    def drain_share():
        def sent(k, carry):
            e_push(k).wait_send()
            e_part(k).wait_send()
            return carry

        lax.fori_loop(1, cells, sent, 0)
        e_part(0).wait_send()

    lax.fori_loop(1, cells, push, 0)
    e_part(0).start()
    while small_jobs:
        small_turn()
    for m in range(hops - 2, hops):
        s_pass(m)

    for m in range(ring):
        for a in (0, 1):
            for k in range(lines):
                s_part_in(a, m, k).wait_recv()

    def join(p, carry):
        block_rows = [u_out[2 * p].astype(jnp.float32), u_out[2 * p + 1].astype(jnp.float32)]
        at = pl.ds(pl.multiple_of(p * 2 * users_here, 2 * users_here), 2 * users_here)
        users[at, :] = jnp.concatenate(block_rows, axis=0).astype(users.dtype)
        return carry

    lax.fori_loop(0, total // 2, join, 0)
    table = lax.fori_loop(
        0, total, lambda d, t: t + k_out[d], jnp.zeros((key_rows, 128), jnp.float32)
    )
    positive = line_of(table, 0, rows_users)[:, :users_total]
    wide = (items_total, rows_items * 128)
    diagonal = lax.broadcasted_iota(jnp.int32, wide, 0) == lax.broadcasted_iota(jnp.int32, wide, 1)

    def column(first):
        row = line_of(table, first, rows_items)
        return jnp.sum(jnp.where(diagonal, row, 0.0), axis=1, keepdims=True)

    ids = column(rows_users)
    log_counts = jnp.log(column(rows_users + rows_items))
    item_at = lax.broadcasted_iota(jnp.int32, (items_total, users_total), 0).astype(jnp.float32)
    chosen = item_at == positive
    positive_id = jnp.sum(jnp.where(chosen, ids, 0.0), axis=0, keepdims=True)
    excluded = (ids == positive_id) & jnp.logical_not(chosen)

    def relay(k, carry):
        e_pull(k).wait_recv()
        e_part(k).start()
        return carry

    lax.fori_loop(1, cells, relay, 0)

    def landed(k, carry):
        e_part(k, 1 - core).wait_recv()
        return carry

    lax.fori_loop(0, cells, landed, 0)
    for d in range(total):
        e_rows[pl.ds(d * items_here, items_here), :] = e_all[d].astype(jnp.float32)
    emb_all = e_rows[...].astype(jnp.bfloat16)
    scores = contract_last(emb_all, users[...])
    logits = jnp.where(excluded, MASKED_FILL, scores - log_counts)
    top = jnp.max(logits, axis=0, keepdims=True)
    weights = jnp.where(excluded, 0.0, jnp.exp(logits - top))
    sums = jnp.sum(weights, axis=0, keepdims=True)
    logit_grad = (weights / sums - chosen.astype(jnp.float32)).astype(jnp.bfloat16)
    e_grad[...] = jnp.dot(logit_grad, users[...], preferred_element_type=jnp.float32)

    for i in range(items_here):
        mean, scale = values[i]
        grad = e_grad[pl.ds(me * items_here + i, 1), :]
        pooled_grad = scale * grad - mean * (
            scale * scale * scale * jnp.mean(mean * grad, axis=1, keepdims=True)
        )
        reach = jnp.broadcast_to(gain * (pooled_grad / spans(i)), (8, width))

        def back(r, carry, i=i, reach=reach):
            at = pl.ds(pl.multiple_of(i * item_length + r * cap, cap), cap)
            x = acc[at, :]
            scale = inv[at, :]
            h = jnp.concatenate([reach] * (cap // 8), axis=0)
            where = r * cap + lax.broadcasted_iota(jnp.int32, (cap, 1), 0)
            keep = jnp.where(where < len_in[i], scale, 0.0)
            dots = jnp.sum(x * h, axis=1, keepdims=True) / width
            rg_out[at, :] = (keep * h - x * (keep * scale * scale * dots)).astype(rg_out.dtype)
            return carry

        lax.fori_loop(0, item_length // cap, back, 0, unroll=2)

    def target(m, way=turn):
        if m == hops:
            return index
        away = ring // 2 - m // 2 if m % 2 == 0 else m // 2 - (ring - 1) // 2
        return ring_index(lax.rem(place + ring + way * away, ring), ring)

    def weight_block(a, b):
        first, second = both_rows(target(a), target(b))
        left = jnp.concatenate([ctx_t[first, :], ctx_t[second, :]], axis=0)
        found = jnp.dot(left, rg_out[...], preferred_element_type=jnp.float32)
        found = found.astype(part_in.dtype)
        part_in[first, :] = found[:rows, :]
        part_in[second, :] = found[rows:, :]

    def cross_out(m):
        start = pl.multiple_of(target(m, -turn) * rows + (1 - core) * half, half)
        return remote(
            part_in.at[pl.ds(start, half), :], cross.at[m], x_send.at[m], x_recv.at[m],
            (partner, index),
        )

    slots = CHUNKS - 1 if split else CHUNKS

    def ring_copy(s, c):
        at = pl.ds(c * part, part)
        return remote(
            held.at[s, at, :], arrived.at[s, at, :], r_send.at[s, c], r_recv.at[s, c],
            (group, ends[s % 2]),
        )

    def local_term(s, j):
        offset = chunk(j) * part
        start = pl.multiple_of(target(s) * rows + core * half + offset, part)
        mine = part_in[pl.ds(start, part), :].astype(jnp.float32)
        return mine + cross[s, pl.ds(pl.multiple_of(offset, part), part), :].astype(jnp.float32)

    def lend(s):
        return remote(lent.at[s], borrowed.at[s], b_send.at[s], b_recv.at[s], (across, index))

    def prepare(s):
        cross_out(s).wait_recv()
        if split:
            lent[s] = local_term(s, CHUNKS - 1).astype(lent.dtype)
            lend(s).start()

    def term_of(s, j):
        term = local_term(s, j)
        if split and j == CHUNKS - 2:
            lend(s).wait_recv()
            term = term + borrowed[s].astype(jnp.float32)
        return term

    head_width = cg_out.shape[1]

    tile = 256

    def context_block(n):
        at = pl.ds(n * tile, tile)
        cg_out[:, at] = contract_last(rg_out[...], w_out[at, :]).astype(cg_out.dtype)

    def last_bits():
        log_total = top + jnp.log(sums)
        picked = jnp.sum(jnp.where(chosen, logits, 0.0), axis=0, keepdims=True)
        loss_out[...] = jnp.mean(log_total - picked, axis=1, keepdims=True)
        shape = (16, users_total)
        seat = lax.broadcasted_iota(jnp.int32, shape, 0)
        mine = lax.broadcasted_iota(jnp.int32, shape, 1) == me * users_here + seat
        mine = (mine & (seat < users_here)).astype(jnp.float32).astype(jnp.bfloat16)
        own_grad = contract_last(mine, logit_grad).astype(jnp.bfloat16)
        found = jnp.dot(own_grad, emb_all, preferred_element_type=jnp.float32)
        ug_out[...] = found[:users_here, :].astype(ug_out.dtype)
        e = e_rows[...]
        g = e_grad[...]
        along = jnp.mean(e * g, axis=1, keepdims=True)
        gain_out[...] = jnp.sum(e * (g - e * along), axis=0, keepdims=True) / gain

    extra = [functools.partial(context_block, n) for n in range(head_width // tile)]
    extra.append(last_bits)

    weight_block(0, hops)
    cross_out(0).start()
    weight_block(1, 2)
    for m in (1, 2):
        cross_out(m).start()
    for m in range(min(2, hops)):
        prepare(m)
    for m in range(hops):
        for j in range(slots):
            at = pl.ds(j * part, part)
            if j == max(CHUNKS - 2, 0) and m + 2 < ring:
                prepare(m + 2)
            term = term_of(m, j)
            if m >= 2:
                ring_copy(m - 2, j).wait_recv()
                term = term + arrived[m - 2, at, :].astype(jnp.float32)
            held[m, at, :] = term.astype(held.dtype)
            ring_copy(m, j).start()
        if 2 * m + 4 < ring:
            weight_block(2 * m + 3, 2 * m + 4)
            for s in (2 * m + 3, 2 * m + 4):
                cross_out(s).start()
            if 2 * m + 4 == hops - 1:
                cross_out(hops).start()
        elif extra:
            extra.pop(0)()
    for job in extra:
        job()
    last = hops

    def total_copy(k, j):
        ref = totals.at[line, pl.ds(j * part, part), :]
        return remote(
            ref, ref, t_send.at[k - 1, j], t_recv.at[k - 1, j],
            (lax.rem(group + 2 * k, groups), index),
        )

    def total_in(k, j):
        source = lax.rem(group + groups - 2 * k, groups)
        ref = totals.at[source // 2, pl.ds(j * part, part), :]
        return remote(ref, ref, t_send.at[k - 1, j], t_recv.at[k - 1, j], (source, index))

    def out_rows(j, side=core):
        return pl.ds(pl.multiple_of(side * half + chunk(j) * part, part), part)

    def out_copy(j, side):
        ref = out.at[out_rows(j, side), :]
        return remote(ref, ref, o_send.at[j], o_recv.at[j], (partner, index))

    def out_across(j):
        ref = out.at[out_rows(j), :]
        return remote(ref, ref, f_send.at[0], f_recv.at[0], (across, index))

    shared = range(CHUNKS - 2) if split else range(CHUNKS)
    for j in range(slots):
        at = pl.ds(j * part, part)
        term = term_of(last, j)
        for m in range(max(hops - 2, 0), hops):
            ring_copy(m, j).wait_recv()
            term = term + arrived[m, at, :].astype(jnp.float32)
        value = term.astype(totals.dtype)
        if j in shared:
            totals[line, at, :] = value
            for k in range(1, lines):
                total_copy(k, j).start()
        else:
            out[out_rows(j), :] = value
            out_across(j).start()
            out_copy(j, core).start()

    for j in shared:
        at = pl.ds(j * part, part)
        for k in range(1, lines):
            total_in(k, j).wait_recv()
        value = totals[0, at, :].astype(jnp.float32)
        for other in range(1, lines):
            value = value + totals[other, at, :].astype(jnp.float32)
        out[out_rows(j), :] = value.astype(out.dtype)
        out_copy(j, core).start()
    if split:
        out_across(CHUNKS - 1).wait_recv()
        out_copy(CHUNKS - 1, core).start()

    drain_gather()
    drain_share()
    for m in range(ring):
        cross_out(m).wait_send()
        if split:
            lend(m).wait_send()
    for m in range(hops):
        for j in range(slots):
            ring_copy(m, j).wait_send()
    for j in shared:
        for k in range(1, lines):
            total_copy(k, j).wait_send()
    for j in range(CHUNKS):
        out_copy(j, core).wait_send()
        out_copy(j, 1 - core).wait_recv()
    if split:
        out_across(CHUNKS - 2).wait_send()


def finish_kernel(*refs):
    count = len(refs) // 2
    sems = refs[-1]
    copies = [
        pltpu.make_async_copy(refs[k], refs[count + k], sems.at[k]) for k in range(count)
    ]
    for copy in copies:
        copy.start()
    for copy in copies:
        copy.wait()


def on_device(
    groups, ring,
    context, residual, out_weight, norm_gain, user_vectors, positive, item_ids, item_counts, lengths
):
    tokens, head_width = context.shape
    width = residual.shape[1]
    rows = out_weight.shape[0]
    half = rows // 2
    items_here = lengths.shape[0]
    users_here = user_vectors.shape[0]
    total = groups * ring
    lines = groups // 2
    cells = lines * ring
    hops = ring - 1
    users_total, items_total = total * users_here, total * items_here
    key_rows = pl.cdiv(users_total, 128) + 2 * pl.cdiv(items_total, 128)
    key_rows = 8 * pl.cdiv(key_rows, 8)
    dma = pltpu.SemaphoreType.DMA
    half_type, full_type = jnp.bfloat16, jnp.float32
    vmem = pl.BlockSpec(memory_space=pltpu.VMEM)
    hbm = pl.BlockSpec(memory_space=pltpu.HBM)
    results = pl.pallas_call(
        functools.partial(step_kernel, groups, ring, users_here, items_here),
        out_shape=(
            jax.ShapeDtypeStruct((1, 1), full_type),
            jax.ShapeDtypeStruct((tokens, width), half_type),
            jax.ShapeDtypeStruct((tokens, head_width), half_type),
            jax.ShapeDtypeStruct((rows, width), half_type),
            jax.ShapeDtypeStruct((1, width), full_type),
            jax.ShapeDtypeStruct((users_here, width), half_type),
        ),
        in_specs=[hbm] * 9,
        out_specs=(vmem,) * 6,
        scratch_shapes=[
            pltpu.VMEM((tokens, head_width), half_type),
            pltpu.VMEM((head_width, tokens), half_type),
            pltpu.VMEM((tokens, width), half_type),
            pltpu.VMEM((ring * rows, width), half_type),
            pltpu.VMEM((total, users_here, width), half_type),
            pltpu.VMEM((total, key_rows, 128), full_type),
            pltpu.VMEM((tokens, width), full_type),
            pltpu.VMEM((tokens, 1), full_type),
            pltpu.VMEM((users_total, width), half_type),
            pltpu.VMEM((8, width), full_type),
            pltpu.VMEM((8, width), full_type),
            pltpu.VMEM((total, items_here, width), half_type),
            pltpu.VMEM((items_total, width), full_type),
            pltpu.VMEM((items_total, width), full_type),
            pltpu.VMEM((ring * rows, width), half_type),
            pltpu.VMEM((ring, half, width), half_type),
            pltpu.VMEM((hops, half, width), half_type),
            pltpu.VMEM((hops, half, width), half_type),
            pltpu.VMEM((lines, half, width), half_type),
            pltpu.VMEM((ring, half // CHUNKS, width), half_type),
            pltpu.VMEM((ring, half // CHUNKS, width), half_type),
            pltpu.VMEM((1, width), full_type),
            pltpu.SMEM((users_here,), jnp.int32),
            pltpu.SMEM((items_here,), jnp.int32),
            pltpu.SMEM((items_here,), jnp.int32),
            pltpu.SMEM((items_here,), jnp.int32),
            dma((9,)),
        ]
        + [dma((hops, CHUNKS))] * 4
        + [dma((hops,))] * 2
        + [dma((hops,))] * 4
        + [dma((ring, max(lines - 1, 1)))] * 4
        + [dma((ring, lines))] * 4
        + [dma((max(cells - 1, 1),))] * 2
        + [dma((cells,))] * 2
        + [dma((ring,))] * 2
        + [dma((hops, CHUNKS))] * 2
        + [dma((max(lines - 1, 1), CHUNKS))] * 2
        + [dma((CHUNKS,))] * 2
        + [dma((ring,))] * 2
        + [dma((1,))] * 2,
        compiler_params=pltpu.CompilerParams(
            collective_id=0, has_side_effects=True, vmem_limit_bytes=48 << 20
        ),
        name="whole_step",
    )(
        *(
            pltpu.with_memory_space_constraint(operand, pltpu.HBM)
            for operand in (
                context, residual, out_weight, norm_gain[None, :], user_vectors,
                positive, item_ids, item_counts, lengths,
            )
        )
    )
    loss, residual_grad, context_grad, weight_grad, gain_grad, user_grad = pl.pallas_call(
        finish_kernel,
        out_shape=tuple(jax.ShapeDtypeStruct(r.shape, r.dtype) for r in results),
        in_specs=[vmem] * len(results),
        out_specs=(hbm,) * len(results),
        scratch_shapes=[dma((len(results),))],
        compiler_params=pltpu.CompilerParams(vmem_limit_bytes=1 << 20),
        name="finish",
    )(*results)
    return (loss[0, 0], residual_grad, context_grad, weight_grad, gain_grad[0], user_grad)


def solution(mesh):
    placed = (
        P(("dp", "fsdp"), None),
        P(("dp", "fsdp"), None),
        P("fsdp", None),
        P(),
        P(("dp", "fsdp"), None),
        P(("dp", "fsdp")),
        P(("dp", "fsdp")),
        P(("dp", "fsdp")),
        P(("dp", "fsdp")),
    )
    return jax.shard_map(
        functools.partial(on_device, mesh.shape["dp"], mesh.shape["fsdp"]),
        mesh=mesh,
        in_specs=placed,
        out_specs=(
            P(),
            P(("dp", "fsdp"), None),
            P(("dp", "fsdp"), None),
            P("fsdp", None),
            P(),
            P(("dp", "fsdp"), None),
        ),
        check_vma=False,
    )
```

```python
import functools

import jax
import jax.numpy as jnp
from jax import lax
from jax.experimental import pallas as pl
from jax.experimental.pallas import tpu as pltpu
from jax.sharding import PartitionSpec as P

EPSILON = 1e-06
MASKED_FILL = -1e30
MESH = pl.DeviceIdType.MESH
CHUNKS = 4
LAG = 1


def contract_last(left, right):
    return lax.dot_general(
        left, right, (((1,), (1,)), ((), ())), preferred_element_type=jnp.float32
    )


def ring_place(index, count):
    return jnp.where(index % 2 == 0, index // 2, count - 1 - index // 2)


def ring_index(place, count):
    return jnp.where(place < count // 2, 2 * place, 2 * (count - 1 - place) + 1)


def remote(src, dst, send_sem, recv_sem, device):
    return pltpu.make_async_remote_copy(
        src_ref=src,
        dst_ref=dst,
        send_sem=send_sem,
        recv_sem=recv_sem,
        device_id=device,
        device_id_type=MESH,
    )


def step_kernel(
    groups, ring, users_here, items_here,
    ctx_in, res_in, w_in, gain_hbm, u_in, pos_hbm, ids_hbm, counts_hbm, len_hbm,
    loss_out, rg_out, cg_out, out, gain_out, ug_out,
    ctx, ctx_t, res, w_out, u_out, acc, inv, users, pooled, emb, e_all, e_rows, e_grad,
    part_in, cross, held, arrived, totals, lent, borrowed,
    gain_in, pos_in, ids_in, counts_in, len_in,
    own_sem, w_send, w_recv, p_recv, y_recv, u_send, u_recv, ul_recv, up_recv,
    e_send, e_recv, ep_recv, x_send, x_recv, r_send, r_recv, t_send, t_recv, o_send, o_recv,
    b_send, b_recv, f_send, f_recv,
):
    group, index = lax.axis_index("dp"), lax.axis_index("fsdp")
    total = groups * ring
    me = group * ring + index
    lines = groups // 2
    cells = lines * ring
    split = lines == 2
    line = group // 2
    core = lax.rem(group, 2)
    cell = line * ring + index
    partner = group + 1 - 2 * core
    across = lax.rem(group + 2, groups)
    place = ring_place(index, ring)
    turn = 1 - 2 * core
    ends = (
        ring_index(lax.rem(place + ring + turn, ring), ring),
        ring_index(lax.rem(place + ring - turn, ring), ring),
    )
    rows, width = w_in.shape
    tokens = ctx_in.shape[0]
    item_length = tokens // items_here
    users_total, items_total = total * users_here, total * items_here
    half = rows // 2
    part = half // CHUNKS
    hops = ring - 1

    def cell_device(c):
        return (2 * (c // ring) + core, lax.rem(c, ring))

    own = [
        pltpu.make_async_copy(u_in, u_out.at[me, :, pl.ds(0, width)], own_sem.at[0]),
        pltpu.make_async_copy(ctx_in, ctx, own_sem.at[1]),
        pltpu.make_async_copy(
            w_in, w_out.at[pl.ds(pl.multiple_of(index * rows, rows), rows), :], own_sem.at[2]
        ),
        pltpu.make_async_copy(res_in, res, own_sem.at[3]),
        pltpu.make_async_copy(gain_hbm, gain_in, own_sem.at[4]),
        pltpu.make_async_copy(pos_hbm, pos_in, own_sem.at[5]),
        pltpu.make_async_copy(ids_hbm, ids_in, own_sem.at[6]),
        pltpu.make_async_copy(counts_hbm, counts_in, own_sem.at[7]),
        pltpu.make_async_copy(len_hbm, len_in, own_sem.at[8]),
    ]
    for copy in own[4:] + own[:4]:
        copy.start()

    barrier = pltpu.get_barrier_semaphore()

    def greet(k, carry):
        peer = cell_device(lax.rem(cell + k, cells))
        pl.semaphore_signal(barrier, inc=1, device_id=peer, device_id_type=MESH)
        return carry

    near = [(partner, index), (group, ends[0]), (group, ends[1]), (across, index)]
    for peer in near if split else near[:1]:
        pl.semaphore_signal(barrier, inc=1, device_id=peer, device_id_type=MESH)
    if not split:
        lax.fori_loop(1, cells, greet, 0)

    for copy in own[4:]:
        copy.wait()
    seat = lax.broadcasted_iota(jnp.int32, (users_here, 128), 0)
    lane = lax.broadcasted_iota(jnp.int32, (users_here, 128), 1)
    keys = jnp.zeros((users_here, 128), jnp.float32)
    for k in range(users_here):
        value = pos_in[k].astype(jnp.float32)
        keys = jnp.where((seat == k) & (lane == 0), value, keys)
    for k in range(items_here):
        count = counts_in[k]
        for at, number in enumerate((ids_in[k], count // 256, lax.rem(count, 256))):
            value = number.astype(jnp.float32)
            keys = jnp.where((seat == k) & (lane == at + 1), value, keys)
    u_out[me, :, pl.ds(width, 128)] = keys.astype(u_out.dtype)

    pl.semaphore_wait(barrier, len(near) if split else cells)

    def owner(m, way=turn):
        if m == hops + 2:
            return index
        away = -(m // 2) if m % 2 == 0 else m // 2
        return ring_index(lax.rem(place + ring + way * away, ring), ring)

    def chunk(j):
        if not split or j < CHUNKS - 2:
            return j
        return CHUNKS - 2 + (line if j == CHUNKS - 2 else 1 - line)

    def w_slice(who, j, side=core):
        start = pl.multiple_of(who * rows + side * half + chunk(j) * part, part)
        return w_out.at[pl.ds(start, part), :]

    def ring_pieces(m):
        if not split:
            return list(range(CHUNKS))
        first = [CHUNKS - 2] + list(range(CHUNKS - 2))
        return first + [CHUNKS - 1] if m == hops - 1 else first

    def w_ring(m, j, shift=0):
        ref = w_slice(owner(m + shift), j)
        src = ref
        if m + shift < 2:
            src = w_in.at[pl.ds(pl.multiple_of(core * half + chunk(j) * part, part), part), :]
        return remote(src, ref, w_send.at[0], w_recv.at[m, j], (group, ends[m % 2]))

    def w_part(m, j, side=core):
        ref = w_slice(owner(m + 2, 1 - 2 * side), j, side)
        return remote(ref, ref, w_send.at[0], p_recv.at[m], (partner, index))

    def w_across(m, j):
        ref = w_slice(owner(m + 2), j)
        return remote(ref, ref, w_send.at[0], y_recv.at[m], (across, index))

    def settle(ref, sem):
        remote(ref, ref, sem, sem, (partner, index)).wait_send()

    def arrive(ref, sem):
        remote(ref, ref, sem, sem, (partner, index)).wait_recv()

    def s_ring(m, shift):
        ref = u_out.at[group * ring + owner(m + shift)]
        return remote(ref, ref, u_send.at[0], u_recv.at[m], (group, ends[m % 2]))

    def s_line(s, k):
        ref = u_out.at[group * ring + owner(s + 2)]
        peer = lax.rem(group + 2 * k, groups)
        return remote(ref, ref, u_send.at[0], ul_recv.at[s, k - 1], (peer, index))

    def s_line_in(s, k):
        source = lax.rem(group + groups - 2 * k, groups)
        ref = u_out.at[source * ring + owner(s + 2)]
        return remote(ref, ref, u_send.at[0], ul_recv.at[s, k - 1], (source, index))

    def s_part(s, k):
        source = lax.rem(group + groups - 2 * k, groups)
        ref = u_out.at[source * ring + owner(s + 2)]
        return remote(ref, ref, u_send.at[0], up_recv.at[source // 2], (partner, index))

    def spread(s):
        for k in range(1, lines):
            s_line(s, k).start()
        s_part(s, 0).start()

    def s_pass(s):
        for k in range(1, lines):
            s_line_in(s, k).wait_recv()
            s_part(s, k).start()

    def s_step(m):
        s_ring(m, 2).wait_recv()
        if m + 2 < hops:
            s_ring(m + 2, 0).start()
        spread(m)
        if m == 1:
            s_pass(hops)
        if m >= 2:
            s_pass(m - 2)

    def has_across(m):
        return split and m < hops - 1

    def w_pass(m):
        if has_across(m):
            w_across(m, CHUNKS - 1).wait_recv()
            w_part(m, CHUNKS - 1).start()
            if m + 2 == hops - 1:
                w_ring(m + 2, CHUNKS - 1).start()

    def drain_gather():
        sends = sum(len(ring_pieces(m)) + has_across(m) + CHUNKS for m in range(hops))
        settle(w_out.at[pl.ds(0, sends * part), :], w_send.at[0])
        settle(u_out.at[pl.ds(0, hops + ring * (2 * lines - 1))], u_send.at[0])

    def both_rows(a, b):
        return [pl.ds(pl.multiple_of(who * rows, rows), rows) for who in (a, b)]

    def forward(a, b, start=False):
        first, second = both_rows(a, b)
        left = jnp.concatenate([ctx[:, first], ctx[:, second]], axis=1)
        right = jnp.concatenate([w_out[first, :], w_out[second, :]], axis=0)
        base = res[...].astype(jnp.float32) if start else acc[...]
        acc[...] = base + jnp.dot(left, right, preferred_element_type=jnp.float32)

    def w_ready(m):
        who = owner(m + 2, -turn)
        start = pl.multiple_of(who * rows + (1 - core) * half, half)
        arrive(w_out.at[pl.ds(start, half), :], p_recv.at[m])

    def turn_over(s, carry):
        at = pl.ds(pl.multiple_of(s * rows, rows), rows)
        ctx_t[at, :] = ctx[:, at].astype(jnp.float32).T.astype(ctx_t.dtype)
        return carry

    for j in ring_pieces(0):
        for m in range(2):
            w_ring(m, j).start()
    own[0].wait()
    spread(hops)

    def s_first():
        for m in range(2):
            s_ring(m, 0).start()

    small_jobs = [[s_first]]
    for m in range(0, hops, 2):
        small_jobs.append([functools.partial(s_step, q) for q in (m, m + 1) if q < hops])
    for _ in range(LAG):
        small_jobs.insert(0, [])

    def small_turn():
        for job in small_jobs.pop(0) if small_jobs else ():
            job()

    small_turn()
    for copy in own[1:4]:
        copy.wait()
    pairs = ring // 2
    for pair in range(pairs):
        both = [m for m in (2 * pair, 2 * pair + 1) if m < hops]
        for j in ring_pieces(both[0]):
            for m in both:
                w_ring(m, j, 2).wait_recv()
                if m + 2 < hops:
                    w_ring(m + 2, j).start()
                if has_across(m) and j == CHUNKS - 2:
                    w_across(m, j).start()
                w_part(m, j).start()
            if pair >= 1 and j == ring_pieces(0)[0]:
                for m in (2 * pair - 2, 2 * pair - 1):
                    w_pass(m)
        small_turn()
        if pair == 0:
            lax.fori_loop(0, ring, turn_over, 0)
        else:
            for m in (2 * pair - 2, 2 * pair - 1):
                w_ready(m)
            forward(owner(2 * pair), owner(2 * pair + 1), pair == 1)
    w_pass(hops - 1)
    w_ready(hops - 1)
    forward(owner(hops + 1), index, pairs == 1)
    small_turn()

    gain = gain_in[...]
    block = 32
    cap = 16

    def spans(i):
        return len_in[i].astype(jnp.float32)

    def inside_of(i, r):
        at = r * block + lax.broadcasted_iota(jnp.int32, (block, 1), 0)
        return (at < len_in[i]).astype(jnp.float32)

    values = []
    for i in range(items_here):

        def pool(r, carry, i=i):
            at = pl.ds(pl.multiple_of(i * item_length + r * block, block), block)
            x = acc[at, :]
            scale = lax.rsqrt(jnp.sum(x * x, axis=1, keepdims=True) / width + EPSILON)
            inv[at, :] = scale
            y = x * (scale * inside_of(i, r))
            for q in range(block // 8):
                carry = carry + y[q * 8 : q * 8 + 8, :]
            return carry

        summed = lax.fori_loop(
            0, item_length // block, pool, jnp.zeros((8, width), jnp.float32)
        )
        summed = jnp.sum(summed, axis=0, keepdims=True)
        mean = gain * summed / spans(i)
        scale = lax.rsqrt(jnp.mean(mean * mean, axis=1, keepdims=True) + EPSILON)
        pooled[pl.ds(i, 1), :] = mean
        values.append((mean, scale))
        emb[pl.ds(i, 1), :] = mean * scale
    e_all[me] = emb[pl.ds(0, items_here), :].astype(e_all.dtype)

    def e_push(k):
        return remote(
            e_all.at[me], e_all.at[me], e_send.at[0], e_recv.at[line],
            cell_device(lax.rem(cell + k, cells)),
        )

    def e_part(row, side=core):
        ref = e_all.at[pl.ds((2 * row + side) * ring, ring)]
        return remote(ref, ref, e_send.at[0], ep_recv.at[row], (partner, index))

    def push(k, carry):
        e_push(k).start()
        return carry

    def drain_share():
        settle(e_all.at[pl.ds(0, cells - 1 + cells)], e_send.at[0])

    lax.fori_loop(1, cells, push, 0)
    while small_jobs:
        small_turn()
    for m in range(hops - 2, hops):
        s_pass(m)

    for row in range(lines):
        arrive(u_out.at[pl.ds((2 * row + 1 - core) * ring, ring)], up_recv.at[row])

    def join(p, carry):
        block_rows = [u_out[2 * p].astype(jnp.float32), u_out[2 * p + 1].astype(jnp.float32)]
        at = pl.ds(pl.multiple_of(p * 2 * users_here, 2 * users_here), 2 * users_here)
        users[at, :] = jnp.concatenate(block_rows, axis=0).astype(users.dtype)
        return carry

    lax.fori_loop(0, total // 2, join, 0)
    tags = users[:, pl.ds(width, 128)]
    shape = (16, 128)
    pick = lax.broadcasted_iota(jnp.int32, shape, 0) == lax.broadcasted_iota(jnp.int32, shape, 1)
    pick = pick.astype(jnp.float32).astype(jnp.bfloat16)
    positive = contract_last(pick, tags)[0:1, :]
    shape = (items_total, users_total)
    item_at = lax.broadcasted_iota(jnp.int32, shape, 0)
    user_at = lax.broadcasted_iota(jnp.int32, shape, 1)
    pick = (item_at // items_here == user_at // users_here) & (
        lax.rem(item_at, items_here) == lax.rem(user_at, users_here)
    )
    pick = pick.astype(jnp.float32).astype(jnp.bfloat16)
    table = jnp.dot(pick, tags, preferred_element_type=jnp.float32)
    ids = table[:, 1:2]
    log_counts = jnp.log(table[:, 2:3] * 256.0 + table[:, 3:4])
    chosen = item_at.astype(jnp.float32) == positive
    positive_id = jnp.sum(jnp.where(chosen, ids, 0.0), axis=0, keepdims=True)
    excluded = (ids == positive_id) & jnp.logical_not(chosen)

    for k in range(lines):
        if k == 0:
            arrive(e_all.at[pl.ds((2 * line + core) * ring, ring - 1)], e_recv.at[line])
        else:
            row = lax.rem(line + k, lines)
            arrive(e_all.at[pl.ds((2 * row + core) * ring, ring)], e_recv.at[row])
        e_part(lax.rem(line + k, lines)).start()
    for row in range(lines):
        arrive(e_all.at[pl.ds((2 * row + 1 - core) * ring, ring)], ep_recv.at[row])
    for d in range(total):
        e_rows[pl.ds(d * items_here, items_here), :] = e_all[d].astype(jnp.float32)
    emb_all = e_rows[...].astype(jnp.bfloat16)
    words = users[:, pl.ds(0, width)]
    scores = contract_last(emb_all, words)
    logits = jnp.where(excluded, MASKED_FILL, scores - log_counts)
    top = jnp.max(logits, axis=0, keepdims=True)
    weights = jnp.where(excluded, 0.0, jnp.exp(logits - top))
    sums = jnp.sum(weights, axis=0, keepdims=True)
    logit_grad = (weights / sums - chosen.astype(jnp.float32)).astype(jnp.bfloat16)
    e_grad[...] = jnp.dot(logit_grad, words, preferred_element_type=jnp.float32)

    for i in range(items_here):
        mean, scale = values[i]
        grad = e_grad[pl.ds(me * items_here + i, 1), :]
        pooled_grad = scale * grad - mean * (
            scale * scale * scale * jnp.mean(mean * grad, axis=1, keepdims=True)
        )
        reach = jnp.broadcast_to(gain * (pooled_grad / spans(i)), (8, width))

        def back(r, carry, i=i, reach=reach):
            at = pl.ds(pl.multiple_of(i * item_length + r * cap, cap), cap)
            x = acc[at, :]
            scale = inv[at, :]
            h = jnp.concatenate([reach] * (cap // 8), axis=0)
            where = r * cap + lax.broadcasted_iota(jnp.int32, (cap, 1), 0)
            keep = jnp.where(where < len_in[i], scale, 0.0)
            dots = jnp.sum(x * h, axis=1, keepdims=True) / width
            rg_out[at, :] = (keep * h - x * (keep * scale * scale * dots)).astype(rg_out.dtype)
            return carry

        lax.fori_loop(0, item_length // cap, back, 0, unroll=2)

    def target(m, way=turn):
        if m == hops:
            return index
        away = ring // 2 - m // 2 if m % 2 == 0 else m // 2 - (ring - 1) // 2
        return ring_index(lax.rem(place + ring + way * away, ring), ring)

    def weight_block(a, b):
        first, second = both_rows(target(a), target(b))
        left = jnp.concatenate([ctx_t[first, :], ctx_t[second, :]], axis=0)
        found = jnp.dot(left, rg_out[...], preferred_element_type=jnp.float32)
        found = found.astype(part_in.dtype)
        part_in[first, :] = found[:rows, :]
        part_in[second, :] = found[rows:, :]

    def cross_out(m):
        start = pl.multiple_of(target(m, -turn) * rows + (1 - core) * half, half)
        return remote(
            part_in.at[pl.ds(start, half), :], cross.at[m], x_send.at[0], x_recv.at[m],
            (partner, index),
        )

    slots = CHUNKS - 1 if split else CHUNKS

    def ring_copy(s, c):
        at = pl.ds(c * part, part)
        return remote(
            held.at[s, at, :], arrived.at[s, at, :], r_send.at[0], r_recv.at[s, c],
            (group, ends[s % 2]),
        )

    def local_term(s, j):
        offset = chunk(j) * part
        start = pl.multiple_of(target(s) * rows + core * half + offset, part)
        mine = part_in[pl.ds(start, part), :].astype(jnp.float32)
        return mine + cross[s, pl.ds(pl.multiple_of(offset, part), part), :].astype(jnp.float32)

    def lend(s):
        return remote(lent.at[s], borrowed.at[s], b_send.at[0], b_recv.at[s], (across, index))

    def prepare(s):
        cross_out(s).wait_recv()
        if split:
            lent[s] = local_term(s, CHUNKS - 1).astype(lent.dtype)
            lend(s).start()

    def term_of(s, j):
        term = local_term(s, j)
        if split and j == CHUNKS - 2:
            lend(s).wait_recv()
            term = term + borrowed[s].astype(jnp.float32)
        return term

    head_width = cg_out.shape[1]

    tile = 256

    def context_block(n):
        at = pl.ds(n * tile, tile)
        cg_out[:, at] = contract_last(rg_out[...], w_out[at, :]).astype(cg_out.dtype)

    def last_bits():
        log_total = top + jnp.log(sums)
        picked = jnp.sum(jnp.where(chosen, logits, 0.0), axis=0, keepdims=True)
        loss_out[...] = jnp.mean(log_total - picked, axis=1, keepdims=True)
        shape = (16, users_total)
        seat = lax.broadcasted_iota(jnp.int32, shape, 0)
        mine = lax.broadcasted_iota(jnp.int32, shape, 1) == me * users_here + seat
        mine = (mine & (seat < users_here)).astype(jnp.float32).astype(jnp.bfloat16)
        own_grad = contract_last(mine, logit_grad).astype(jnp.bfloat16)
        found = jnp.dot(own_grad, emb_all, preferred_element_type=jnp.float32)
        ug_out[...] = found[:users_here, :].astype(ug_out.dtype)
        e = e_rows[...]
        g = e_grad[...]
        along = jnp.mean(e * g, axis=1, keepdims=True)
        gain_out[...] = jnp.sum(e * (g - e * along), axis=0, keepdims=True) / gain

    extra = [functools.partial(context_block, n) for n in range(head_width // tile)]
    extra.append(last_bits)

    weight_block(0, hops)
    cross_out(0).start()
    weight_block(1, 2)
    for m in (1, 2):
        cross_out(m).start()
    for m in range(min(2, hops)):
        prepare(m)
    for m in range(hops):
        for j in range(slots):
            at = pl.ds(j * part, part)
            if j == max(CHUNKS - 2, 0) and m + 2 < ring:
                prepare(m + 2)
            term = term_of(m, j)
            if m >= 2:
                ring_copy(m - 2, j).wait_recv()
                term = term + arrived[m - 2, at, :].astype(jnp.float32)
            held[m, at, :] = term.astype(held.dtype)
            ring_copy(m, j).start()
        if 2 * m + 4 < ring:
            weight_block(2 * m + 3, 2 * m + 4)
            for s in (2 * m + 3, 2 * m + 4):
                cross_out(s).start()
            if 2 * m + 4 == hops - 1:
                cross_out(hops).start()
        elif extra:
            extra.pop(0)()
    for job in extra:
        job()
    last = hops

    def total_copy(k, j):
        ref = totals.at[line, pl.ds(j * part, part), :]
        return remote(
            ref, ref, t_send.at[0], t_recv.at[k - 1, j],
            (lax.rem(group + 2 * k, groups), index),
        )

    def total_in(k, j):
        source = lax.rem(group + groups - 2 * k, groups)
        ref = totals.at[source // 2, pl.ds(j * part, part), :]
        return remote(ref, ref, t_send.at[0], t_recv.at[k - 1, j], (source, index))

    def out_rows(j, side=core):
        return pl.ds(pl.multiple_of(side * half + chunk(j) * part, part), part)

    def out_copy(j, side):
        ref = out.at[out_rows(j, side), :]
        return remote(ref, ref, o_send.at[0], o_recv.at[0], (partner, index))

    def out_across(j):
        ref = out.at[out_rows(j), :]
        return remote(ref, ref, f_send.at[0], f_recv.at[0], (across, index))

    shared = range(CHUNKS - 2) if split else range(CHUNKS)
    for j in range(slots):
        at = pl.ds(j * part, part)
        term = term_of(last, j)
        for m in range(max(hops - 2, 0), hops):
            ring_copy(m, j).wait_recv()
            term = term + arrived[m, at, :].astype(jnp.float32)
        value = term.astype(totals.dtype)
        if j in shared:
            totals[line, at, :] = value
            for k in range(1, lines):
                total_copy(k, j).start()
        else:
            out[out_rows(j), :] = value
            out_across(j).start()
            out_copy(j, core).start()

    for j in shared:
        at = pl.ds(j * part, part)
        for k in range(1, lines):
            total_in(k, j).wait_recv()
        value = totals[0, at, :].astype(jnp.float32)
        for other in range(1, lines):
            value = value + totals[other, at, :].astype(jnp.float32)
        out[out_rows(j), :] = value.astype(out.dtype)
        out_copy(j, core).start()
    if split:
        out_across(CHUNKS - 1).wait_recv()
        out_copy(CHUNKS - 1, core).start()

    drain_gather()
    drain_share()
    settle(cross, x_send.at[0])
    if split:
        settle(lent, b_send.at[0])
    settle(part_in.at[pl.ds(0, hops * slots * part), :], r_send.at[0])
    settle(part_in.at[pl.ds(0, (lines - 1) * len(shared) * part), :], t_send.at[0])
    if split:
        out_across(CHUNKS - 2).wait_send()
    settle(out.at[pl.ds(pl.multiple_of(core * half, half), half), :], o_send.at[0])
    arrive(out.at[pl.ds(pl.multiple_of((1 - core) * half, half), half), :], o_recv.at[0])


def finish_kernel(*refs):
    count = len(refs) // 2
    sems = refs[-1]
    copies = [
        pltpu.make_async_copy(refs[k], refs[count + k], sems.at[k]) for k in range(count)
    ]
    for copy in copies:
        copy.start()
    for copy in copies:
        copy.wait()


def on_device(
    groups, ring,
    context, residual, out_weight, norm_gain, user_vectors, positive, item_ids, item_counts, lengths
):
    tokens, head_width = context.shape
    width = residual.shape[1]
    rows = out_weight.shape[0]
    half = rows // 2
    items_here = lengths.shape[0]
    users_here = user_vectors.shape[0]
    total = groups * ring
    lines = groups // 2
    cells = lines * ring
    hops = ring - 1
    users_total, items_total = total * users_here, total * items_here
    dma = pltpu.SemaphoreType.DMA
    half_type, full_type = jnp.bfloat16, jnp.float32
    vmem = pl.BlockSpec(memory_space=pltpu.VMEM)
    hbm = pl.BlockSpec(memory_space=pltpu.HBM)
    results = pl.pallas_call(
        functools.partial(step_kernel, groups, ring, users_here, items_here),
        out_shape=(
            jax.ShapeDtypeStruct((1, 1), full_type),
            jax.ShapeDtypeStruct((tokens, width), half_type),
            jax.ShapeDtypeStruct((tokens, head_width), half_type),
            jax.ShapeDtypeStruct((rows, width), half_type),
            jax.ShapeDtypeStruct((1, width), full_type),
            jax.ShapeDtypeStruct((users_here, width), half_type),
        ),
        in_specs=[hbm] * 9,
        out_specs=(vmem,) * 6,
        scratch_shapes=[
            pltpu.VMEM((tokens, head_width), half_type),
            pltpu.VMEM((head_width, tokens), half_type),
            pltpu.VMEM((tokens, width), half_type),
            pltpu.VMEM((ring * rows, width), half_type),
            pltpu.VMEM((total, users_here, width + 128), half_type),
            pltpu.VMEM((tokens, width), full_type),
            pltpu.VMEM((tokens, 1), full_type),
            pltpu.VMEM((users_total, width + 128), half_type),
            pltpu.VMEM((8, width), full_type),
            pltpu.VMEM((8, width), full_type),
            pltpu.VMEM((total, items_here, width), half_type),
            pltpu.VMEM((items_total, width), full_type),
            pltpu.VMEM((items_total, width), full_type),
            pltpu.VMEM((ring * rows, width), half_type),
            pltpu.VMEM((ring, half, width), half_type),
            pltpu.VMEM((hops, half, width), half_type),
            pltpu.VMEM((hops, half, width), half_type),
            pltpu.VMEM((lines, half, width), half_type),
            pltpu.VMEM((ring, half // CHUNKS, width), half_type),
            pltpu.VMEM((ring, half // CHUNKS, width), half_type),
            pltpu.VMEM((1, width), full_type),
            pltpu.SMEM((users_here,), jnp.int32),
            pltpu.SMEM((items_here,), jnp.int32),
            pltpu.SMEM((items_here,), jnp.int32),
            pltpu.SMEM((items_here,), jnp.int32),
            dma((9,)),
            dma((1,)),
            dma((hops, CHUNKS)),
            dma((hops,)),
            dma((hops,)),
            dma((1,)),
            dma((hops,)),
            dma((ring, max(lines - 1, 1))),
            dma((lines,)),
            dma((1,)),
            dma((lines,)),
            dma((lines,)),
            dma((1,)),
            dma((ring,)),
            dma((1,)),
            dma((hops, CHUNKS - 1 if lines == 2 else CHUNKS)),
            dma((1,)),
            dma((max(lines - 1, 1), CHUNKS)),
            dma((1,)),
            dma((1,)),
            dma((1,)),
            dma((ring,)),
            dma((1,)),
            dma((1,)),
        ],
        compiler_params=pltpu.CompilerParams(
            collective_id=0, has_side_effects=True, vmem_limit_bytes=48 << 20
        ),
        name="whole_step",
    )(
        *(
            pltpu.with_memory_space_constraint(operand, pltpu.HBM)
            for operand in (
                context, residual, out_weight, norm_gain[None, :], user_vectors,
                positive, item_ids, item_counts, lengths,
            )
        )
    )
    loss, residual_grad, context_grad, weight_grad, gain_grad, user_grad = pl.pallas_call(
        finish_kernel,
        out_shape=tuple(jax.ShapeDtypeStruct(r.shape, r.dtype) for r in results),
        in_specs=[vmem] * len(results),
        out_specs=(hbm,) * len(results),
        scratch_shapes=[dma((len(results),))],
        compiler_params=pltpu.CompilerParams(vmem_limit_bytes=1 << 20),
        name="finish",
    )(*results)
    return (loss[0, 0], residual_grad, context_grad, weight_grad, gain_grad[0], user_grad)


def solution(mesh):
    placed = (
        P(("dp", "fsdp"), None),
        P(("dp", "fsdp"), None),
        P("fsdp", None),
        P(),
        P(("dp", "fsdp"), None),
        P(("dp", "fsdp")),
        P(("dp", "fsdp")),
        P(("dp", "fsdp")),
        P(("dp", "fsdp")),
    )
    return jax.shard_map(
        functools.partial(on_device, mesh.shape["dp"], mesh.shape["fsdp"]),
        mesh=mesh,
        in_specs=placed,
        out_specs=(
            P(),
            P(("dp", "fsdp"), None),
            P(("dp", "fsdp"), None),
            P("fsdp", None),
            P(),
            P(("dp", "fsdp"), None),
        ),
        check_vma=False,
    )
```

```python
import functools

import jax
import jax.numpy as jnp
from jax import lax
from jax.experimental import pallas as pl
from jax.experimental.pallas import tpu as pltpu
from jax.sharding import PartitionSpec as P

EPSILON = 1e-06
MASKED_FILL = -1e30
MESH = pl.DeviceIdType.MESH
CHUNKS = 4
LAG = 1


def contract_last(left, right):
    return lax.dot_general(
        left, right, (((1,), (1,)), ((), ())), preferred_element_type=jnp.float32
    )


def ring_place(index, count):
    return jnp.where(index % 2 == 0, index // 2, count - 1 - index // 2)


def ring_index(place, count):
    return jnp.where(place < count // 2, 2 * place, 2 * (count - 1 - place) + 1)


def remote(src, dst, send_sem, recv_sem, device):
    return pltpu.make_async_remote_copy(
        src_ref=src,
        dst_ref=dst,
        send_sem=send_sem,
        recv_sem=recv_sem,
        device_id=device,
        device_id_type=MESH,
    )


def step_kernel(
    groups, ring, users_here, items_here,
    ctx_in, res_in, w_in, gain_hbm, u_in, pos_hbm, ids_hbm, counts_hbm, len_hbm,
    loss_out, rg_out, cg_out, out, gain_out, ug_out,
    ctx, ctx_t, res, w_out, u_out, acc, inv, users, pooled, emb, e_all, e_rows, e_grad,
    part_in, cross, held, arrived, totals, lent, borrowed,
    gain_in, pos_in, ids_in, counts_in, len_in,
    own_sem, w_send, w_recv, p_recv, y_recv, u_send, u_recv, ul_recv, up_recv,
    e_send, e_recv, ep_recv, x_send, x_recv, r_send, r_recv, t_send, t_recv, o_send, o_recv,
    b_send, b_recv, f_send, f_recv,
):
    group, index = lax.axis_index("dp"), lax.axis_index("fsdp")
    total = groups * ring
    me = group * ring + index
    lines = groups // 2
    cells = lines * ring
    split = lines == 2
    line = group // 2
    core = lax.rem(group, 2)
    cell = line * ring + index
    partner = group + 1 - 2 * core
    across = lax.rem(group + 2, groups)
    place = ring_place(index, ring)
    turn = 1 - 2 * core
    ends = (
        ring_index(lax.rem(place + ring + turn, ring), ring),
        ring_index(lax.rem(place + ring - turn, ring), ring),
    )
    rows, width = w_in.shape
    tokens = ctx_in.shape[0]
    item_length = tokens // items_here
    users_total, items_total = total * users_here, total * items_here
    half = rows // 2
    part = half // CHUNKS
    hops = ring - 1

    def cell_device(c):
        return (2 * (c // ring) + core, lax.rem(c, ring))

    own = [
        pltpu.make_async_copy(u_in, u_out.at[me, :, pl.ds(0, width)], own_sem.at[0]),
        pltpu.make_async_copy(ctx_in, ctx, own_sem.at[1]),
        pltpu.make_async_copy(
            w_in, w_out.at[pl.ds(pl.multiple_of(index * rows, rows), rows), :], own_sem.at[2]
        ),
        pltpu.make_async_copy(res_in, res, own_sem.at[3]),
        pltpu.make_async_copy(gain_hbm, gain_in, own_sem.at[4]),
        pltpu.make_async_copy(pos_hbm, pos_in, own_sem.at[5]),
        pltpu.make_async_copy(ids_hbm, ids_in, own_sem.at[6]),
        pltpu.make_async_copy(counts_hbm, counts_in, own_sem.at[7]),
        pltpu.make_async_copy(len_hbm, len_in, own_sem.at[8]),
    ]
    for copy in own[4:] + own[:4]:
        copy.start()

    barrier = pltpu.get_barrier_semaphore()

    def greet(k, carry):
        peer = cell_device(lax.rem(cell + k, cells))
        pl.semaphore_signal(barrier, inc=1, device_id=peer, device_id_type=MESH)
        return carry

    near = [(partner, index), (group, ends[0]), (group, ends[1]), (across, index)]
    for peer in near if split else near[:1]:
        pl.semaphore_signal(barrier, inc=1, device_id=peer, device_id_type=MESH)
    if not split:
        lax.fori_loop(1, cells, greet, 0)

    for copy in own[4:]:
        copy.wait()
    seat = lax.broadcasted_iota(jnp.int32, (users_here, 128), 0)
    lane = lax.broadcasted_iota(jnp.int32, (users_here, 128), 1)
    keys = jnp.zeros((users_here, 128), jnp.float32)
    for k in range(users_here):
        value = pos_in[k].astype(jnp.float32)
        keys = jnp.where((seat == k) & (lane == 0), value, keys)
    for k in range(items_here):
        count = counts_in[k]
        for at, number in enumerate((ids_in[k], count // 256, lax.rem(count, 256))):
            value = number.astype(jnp.float32)
            keys = jnp.where((seat == k) & (lane == at + 1), value, keys)
    u_out[me, :, pl.ds(width, 128)] = keys.astype(u_out.dtype)

    pl.semaphore_wait(barrier, len(near) if split else cells)

    def owner(m, way=turn):
        if m == hops + 2:
            return index
        away = -(m // 2) if m % 2 == 0 else m // 2
        return ring_index(lax.rem(place + ring + way * away, ring), ring)

    def chunk(j):
        if not split or j < CHUNKS - 2:
            return j
        return CHUNKS - 2 + (line if j == CHUNKS - 2 else 1 - line)

    def w_slice(who, j, side=core):
        start = pl.multiple_of(who * rows + side * half + chunk(j) * part, part)
        return w_out.at[pl.ds(start, part), :]

    def ring_pieces(m):
        if not split:
            return list(range(CHUNKS))
        first = [CHUNKS - 2] + list(range(CHUNKS - 2))
        return first + [CHUNKS - 1] if m == hops - 1 else first

    def w_ring(m, j, shift=0):
        ref = w_slice(owner(m + shift), j)
        src = ref
        if m + shift < 2:
            src = w_in.at[pl.ds(pl.multiple_of(core * half + chunk(j) * part, part), part), :]
        return remote(src, ref, w_send.at[0], w_recv.at[m, j], (group, ends[m % 2]))

    def w_part(m, j, side=core):
        ref = w_slice(owner(m + 2, 1 - 2 * side), j, side)
        return remote(ref, ref, w_send.at[0], p_recv.at[m], (partner, index))

    def w_across(m, j):
        ref = w_slice(owner(m + 2), j)
        return remote(ref, ref, w_send.at[0], y_recv.at[m], (across, index))

    def settle(ref, sem):
        remote(ref, ref, sem, sem, (partner, index)).wait_send()

    def arrive(ref, sem):
        remote(ref, ref, sem, sem, (partner, index)).wait_recv()

    def s_ring(m, shift):
        ref = u_out.at[group * ring + owner(m + shift)]
        return remote(ref, ref, u_send.at[0], u_recv.at[m], (group, ends[m % 2]))

    def s_line(s, k):
        ref = u_out.at[group * ring + owner(s + 2)]
        peer = lax.rem(group + 2 * k, groups)
        return remote(ref, ref, u_send.at[0], ul_recv.at[s, k - 1], (peer, index))

    def s_line_in(s, k):
        source = lax.rem(group + groups - 2 * k, groups)
        ref = u_out.at[source * ring + owner(s + 2)]
        return remote(ref, ref, u_send.at[0], ul_recv.at[s, k - 1], (source, index))

    def s_part(s, k):
        source = lax.rem(group + groups - 2 * k, groups)
        ref = u_out.at[source * ring + owner(s + 2)]
        return remote(ref, ref, u_send.at[0], up_recv.at[source // 2], (partner, index))

    def spread(s):
        for k in range(1, lines):
            s_line(s, k).start()
        s_part(s, 0).start()

    def s_pass(s):
        for k in range(1, lines):
            s_line_in(s, k).wait_recv()
            s_part(s, k).start()

    def s_step(m):
        s_ring(m, 2).wait_recv()
        if m + 2 < hops:
            s_ring(m + 2, 0).start()
        spread(m)
        if m == 1:
            s_pass(hops)
        if m >= 2:
            s_pass(m - 2)

    def has_across(m):
        return split and m < hops - 1

    def w_pass(m):
        if has_across(m):
            w_across(m, CHUNKS - 1).wait_recv()
            w_part(m, CHUNKS - 1).start()
            if m + 2 == hops - 1:
                w_ring(m + 2, CHUNKS - 1).start()

    def drain_gather():
        sends = sum(len(ring_pieces(m)) + has_across(m) + CHUNKS for m in range(hops))
        settle(w_out.at[pl.ds(0, sends * part), :], w_send.at[0])
        settle(u_out.at[pl.ds(0, hops + ring * (2 * lines - 1))], u_send.at[0])

    def both_rows(a, b):
        return [pl.ds(pl.multiple_of(who * rows, rows), rows) for who in (a, b)]

    def forward(a, b, start=False):
        first, second = both_rows(a, b)
        left = jnp.concatenate([ctx[:, first], ctx[:, second]], axis=1)
        right = jnp.concatenate([w_out[first, :], w_out[second, :]], axis=0)
        base = res[...].astype(jnp.float32) if start else acc[...]
        acc[...] = base + jnp.dot(left, right, preferred_element_type=jnp.float32)

    def w_ready(m):
        who = owner(m + 2, -turn)
        start = pl.multiple_of(who * rows + (1 - core) * half, half)
        arrive(w_out.at[pl.ds(start, half), :], p_recv.at[m])

    def turn_over(s, carry):
        at = pl.ds(pl.multiple_of(s * rows, rows), rows)
        ctx_t[at, :] = ctx[:, at].astype(jnp.float32).T.astype(ctx_t.dtype)
        return carry

    for j in ring_pieces(0):
        for m in range(2):
            w_ring(m, j).start()
    own[0].wait()
    spread(hops)

    def s_first():
        for m in range(2):
            s_ring(m, 0).start()

    small_jobs = [[s_first]]
    for m in range(0, hops, 2):
        small_jobs.append([functools.partial(s_step, q) for q in (m, m + 1) if q < hops])
    for _ in range(LAG):
        small_jobs.insert(0, [])

    def small_turn():
        for job in small_jobs.pop(0) if small_jobs else ():
            job()

    small_turn()
    own[1].wait()
    lax.fori_loop(0, ring, turn_over, 0)
    own[2].wait()
    own[3].wait()
    pairs = ring // 2
    for pair in range(pairs):
        both = [m for m in (2 * pair, 2 * pair + 1) if m < hops]
        for j in ring_pieces(both[0]):
            for m in both:
                w_ring(m, j, 2).wait_recv()
                if m + 2 < hops:
                    w_ring(m + 2, j).start()
                if has_across(m) and j == CHUNKS - 2:
                    w_across(m, j).start()
                w_part(m, j).start()
            if pair >= 1 and j == ring_pieces(0)[0]:
                for m in (2 * pair - 2, 2 * pair - 1):
                    w_pass(m)
        small_turn()
        if pair >= 1:
            for m in (2 * pair - 2, 2 * pair - 1):
                w_ready(m)
            forward(owner(2 * pair), owner(2 * pair + 1), pair == 1)
    w_pass(hops - 1)
    w_ready(hops - 1)
    forward(owner(hops + 1), index, pairs == 1)
    small_turn()

    gain = gain_in[...]
    block = 32
    cap = 16

    def spans(i):
        return len_in[i].astype(jnp.float32)

    def inside_of(i, r):
        at = r * block + lax.broadcasted_iota(jnp.int32, (block, 1), 0)
        return (at < len_in[i]).astype(jnp.float32)

    values = []
    for i in range(items_here):

        def pool(r, carry, i=i):
            at = pl.ds(pl.multiple_of(i * item_length + r * block, block), block)
            x = acc[at, :]
            scale = lax.rsqrt(jnp.sum(x * x, axis=1, keepdims=True) / width + EPSILON)
            inv[at, :] = scale
            y = x * (scale * inside_of(i, r))
            for q in range(block // 8):
                carry = carry + y[q * 8 : q * 8 + 8, :]
            return carry

        summed = lax.fori_loop(
            0, item_length // block, pool, jnp.zeros((8, width), jnp.float32), unroll=8
        )
        summed = jnp.sum(summed, axis=0, keepdims=True)
        mean = gain * summed / spans(i)
        scale = lax.rsqrt(jnp.mean(mean * mean, axis=1, keepdims=True) + EPSILON)
        pooled[pl.ds(i, 1), :] = mean
        values.append((mean, scale))
        emb[pl.ds(i, 1), :] = mean * scale
    e_all[me] = emb[pl.ds(0, items_here), :].astype(e_all.dtype)

    def e_push(k):
        return remote(
            e_all.at[me], e_all.at[me], e_send.at[0], e_recv.at[line],
            cell_device(lax.rem(cell + k, cells)),
        )

    def e_part(row, side=core):
        ref = e_all.at[pl.ds((2 * row + side) * ring, ring)]
        return remote(ref, ref, e_send.at[0], ep_recv.at[row], (partner, index))

    def push(k, carry):
        e_push(k).start()
        return carry

    def drain_share():
        settle(e_all.at[pl.ds(0, cells - 1 + cells)], e_send.at[0])

    lax.fori_loop(1, cells, push, 0)
    while small_jobs:
        small_turn()
    for m in range(hops - 2, hops):
        s_pass(m)

    for row in range(lines):
        arrive(u_out.at[pl.ds((2 * row + 1 - core) * ring, ring)], up_recv.at[row])

    def join(p, carry):
        block_rows = [u_out[2 * p].astype(jnp.float32), u_out[2 * p + 1].astype(jnp.float32)]
        at = pl.ds(pl.multiple_of(p * 2 * users_here, 2 * users_here), 2 * users_here)
        users[at, :] = jnp.concatenate(block_rows, axis=0).astype(users.dtype)
        return carry

    lax.fori_loop(0, total // 2, join, 0)
    tags = users[:, pl.ds(width, 128)]
    shape = (16, 128)
    pick = lax.broadcasted_iota(jnp.int32, shape, 0) == lax.broadcasted_iota(jnp.int32, shape, 1)
    pick = pick.astype(jnp.float32).astype(jnp.bfloat16)
    positive = contract_last(pick, tags)[0:1, :]
    shape = (items_total, users_total)
    item_at = lax.broadcasted_iota(jnp.int32, shape, 0)
    user_at = lax.broadcasted_iota(jnp.int32, shape, 1)
    pick = (item_at // items_here == user_at // users_here) & (
        lax.rem(item_at, items_here) == lax.rem(user_at, users_here)
    )
    pick = pick.astype(jnp.float32).astype(jnp.bfloat16)
    table = jnp.dot(pick, tags, preferred_element_type=jnp.float32)
    ids = table[:, 1:2]
    log_counts = jnp.log(table[:, 2:3] * 256.0 + table[:, 3:4])
    chosen = item_at.astype(jnp.float32) == positive
    positive_id = jnp.sum(jnp.where(chosen, ids, 0.0), axis=0, keepdims=True)
    excluded = (ids == positive_id) & jnp.logical_not(chosen)

    for k in range(lines):
        if k == 0:
            arrive(e_all.at[pl.ds((2 * line + core) * ring, ring - 1)], e_recv.at[line])
        else:
            row = lax.rem(line + k, lines)
            arrive(e_all.at[pl.ds((2 * row + core) * ring, ring)], e_recv.at[row])
        e_part(lax.rem(line + k, lines)).start()
    for row in range(lines):
        arrive(e_all.at[pl.ds((2 * row + 1 - core) * ring, ring)], ep_recv.at[row])
    for d in range(total):
        e_rows[pl.ds(d * items_here, items_here), :] = e_all[d].astype(jnp.float32)
    emb_all = e_rows[...].astype(jnp.bfloat16)
    words = users[:, pl.ds(0, width)]
    scores = contract_last(emb_all, words)
    logits = jnp.where(excluded, MASKED_FILL, scores - log_counts)
    top = jnp.max(logits, axis=0, keepdims=True)
    weights = jnp.where(excluded, 0.0, jnp.exp(logits - top))
    sums = jnp.sum(weights, axis=0, keepdims=True)
    logit_grad = (weights / sums - chosen.astype(jnp.float32)).astype(jnp.bfloat16)
    e_grad[...] = jnp.dot(logit_grad, words, preferred_element_type=jnp.float32)

    for i in range(items_here):
        mean, scale = values[i]
        grad = e_grad[pl.ds(me * items_here + i, 1), :]
        pooled_grad = scale * grad - mean * (
            scale * scale * scale * jnp.mean(mean * grad, axis=1, keepdims=True)
        )
        reach = jnp.broadcast_to(gain * (pooled_grad / spans(i)), (8, width))

        def back(r, carry, i=i, reach=reach):
            at = pl.ds(pl.multiple_of(i * item_length + r * cap, cap), cap)
            x = acc[at, :]
            scale = inv[at, :]
            h = jnp.concatenate([reach] * (cap // 8), axis=0)
            where = r * cap + lax.broadcasted_iota(jnp.int32, (cap, 1), 0)
            keep = jnp.where(where < len_in[i], scale, 0.0)
            dots = jnp.sum(x * h, axis=1, keepdims=True) / width
            rg_out[at, :] = (keep * h - x * (keep * scale * scale * dots)).astype(rg_out.dtype)
            return carry

        lax.fori_loop(0, item_length // cap, back, 0, unroll=16)

    def target(m, way=turn):
        if m == hops:
            return index
        away = ring // 2 - m // 2 if m % 2 == 0 else m // 2 - (ring - 1) // 2
        return ring_index(lax.rem(place + ring + way * away, ring), ring)

    def weight_block(a, b):
        first, second = both_rows(target(a), target(b))
        left = jnp.concatenate([ctx_t[first, :], ctx_t[second, :]], axis=0)
        found = jnp.dot(left, rg_out[...], preferred_element_type=jnp.float32)
        found = found.astype(part_in.dtype)
        part_in[first, :] = found[:rows, :]
        part_in[second, :] = found[rows:, :]

    def cross_out(m):
        start = pl.multiple_of(target(m, -turn) * rows + (1 - core) * half, half)
        return remote(
            part_in.at[pl.ds(start, half), :], cross.at[m], x_send.at[0], x_recv.at[m],
            (partner, index),
        )

    slots = CHUNKS - 1 if split else CHUNKS

    def ring_copy(s, c):
        at = pl.ds(c * part, part)
        return remote(
            held.at[s, at, :], arrived.at[s, at, :], r_send.at[0], r_recv.at[s, c],
            (group, ends[s % 2]),
        )

    def local_term(s, j):
        offset = chunk(j) * part
        start = pl.multiple_of(target(s) * rows + core * half + offset, part)
        mine = part_in[pl.ds(start, part), :].astype(jnp.float32)
        return mine + cross[s, pl.ds(pl.multiple_of(offset, part), part), :].astype(jnp.float32)

    def lend(s):
        return remote(lent.at[s], borrowed.at[s], b_send.at[0], b_recv.at[s], (across, index))

    def prepare(s):
        cross_out(s).wait_recv()
        if split:
            lent[s] = local_term(s, CHUNKS - 1).astype(lent.dtype)
            lend(s).start()

    def term_of(s, j):
        term = local_term(s, j)
        if split and j == CHUNKS - 2:
            lend(s).wait_recv()
            term = term + borrowed[s].astype(jnp.float32)
        return term

    head_width = cg_out.shape[1]

    tile = 256

    def context_block(n):
        at = pl.ds(n * tile, tile)
        cg_out[:, at] = contract_last(rg_out[...], w_out[at, :]).astype(cg_out.dtype)

    def last_bits():
        log_total = top + jnp.log(sums)
        picked = jnp.sum(jnp.where(chosen, logits, 0.0), axis=0, keepdims=True)
        loss_out[...] = jnp.mean(log_total - picked, axis=1, keepdims=True)
        shape = (16, users_total)
        seat = lax.broadcasted_iota(jnp.int32, shape, 0)
        mine = lax.broadcasted_iota(jnp.int32, shape, 1) == me * users_here + seat
        mine = (mine & (seat < users_here)).astype(jnp.float32).astype(jnp.bfloat16)
        own_grad = contract_last(mine, logit_grad).astype(jnp.bfloat16)
        found = jnp.dot(own_grad, emb_all, preferred_element_type=jnp.float32)
        ug_out[...] = found[:users_here, :].astype(ug_out.dtype)
        e = e_rows[...]
        g = e_grad[...]
        along = jnp.mean(e * g, axis=1, keepdims=True)
        gain_out[...] = jnp.sum(e * (g - e * along), axis=0, keepdims=True) / gain

    extra = [functools.partial(context_block, n) for n in range(head_width // tile)]
    extra.append(last_bits)

    def ready(m):
        weight_block(m, m + 1)
        cross_out(m).start()
        cross_out(m + 1).start()
        if m + 2 == hops:
            cross_out(hops).start()

    weight_block(0, hops)
    cross_out(0).start()
    ready(1)
    prepare(0)
    prepare(1)
    for pair in range(pairs):
        both = [m for m in (2 * pair, 2 * pair + 1) if m < hops]
        for j in range(slots):
            at = pl.ds(j * part, part)
            if j == slots - 1:
                for m in both:
                    if m + 2 < ring:
                        prepare(m + 2)
            for m in both:
                term = term_of(m, j)
                if m >= 2:
                    ring_copy(m - 2, j).wait_recv()
                    term = term + arrived[m - 2, at, :].astype(jnp.float32)
                held[m, at, :] = term.astype(held.dtype)
                ring_copy(m, j).start()
            coming = 2 * pair + 3
            if j == 0 and coming + 1 < ring:
                ready(coming)
        if pair >= 1 and extra:
            extra.pop(0)()
    for job in extra:
        job()
    last = hops

    def total_copy(k, j):
        ref = totals.at[line, pl.ds(j * part, part), :]
        return remote(
            ref, ref, t_send.at[0], t_recv.at[k - 1, j],
            (lax.rem(group + 2 * k, groups), index),
        )

    def total_in(k, j):
        source = lax.rem(group + groups - 2 * k, groups)
        ref = totals.at[source // 2, pl.ds(j * part, part), :]
        return remote(ref, ref, t_send.at[0], t_recv.at[k - 1, j], (source, index))

    def out_rows(j, side=core):
        return pl.ds(pl.multiple_of(side * half + chunk(j) * part, part), part)

    def out_copy(j, side):
        ref = out.at[out_rows(j, side), :]
        return remote(ref, ref, o_send.at[0], o_recv.at[0], (partner, index))

    def out_across(j):
        ref = out.at[out_rows(j), :]
        return remote(ref, ref, f_send.at[0], f_recv.at[0], (across, index))

    shared = range(CHUNKS - 2) if split else range(CHUNKS)
    for j in range(slots):
        at = pl.ds(j * part, part)
        term = term_of(last, j)
        for m in range(max(hops - 2, 0), hops):
            ring_copy(m, j).wait_recv()
            term = term + arrived[m, at, :].astype(jnp.float32)
        value = term.astype(totals.dtype)
        if j in shared:
            totals[line, at, :] = value
            for k in range(1, lines):
                total_copy(k, j).start()
        else:
            out[out_rows(j), :] = value
            out_across(j).start()
            out_copy(j, core).start()

    for j in shared:
        at = pl.ds(j * part, part)
        for k in range(1, lines):
            total_in(k, j).wait_recv()
        value = totals[0, at, :].astype(jnp.float32)
        for other in range(1, lines):
            value = value + totals[other, at, :].astype(jnp.float32)
        out[out_rows(j), :] = value.astype(out.dtype)
        out_copy(j, core).start()
    if split:
        out_across(CHUNKS - 1).wait_recv()
        out_copy(CHUNKS - 1, core).start()

    drain_gather()
    drain_share()
    settle(cross, x_send.at[0])
    if split:
        settle(lent, b_send.at[0])
    settle(part_in.at[pl.ds(0, hops * slots * part), :], r_send.at[0])
    settle(part_in.at[pl.ds(0, (lines - 1) * len(shared) * part), :], t_send.at[0])
    if split:
        out_across(CHUNKS - 2).wait_send()
    settle(out.at[pl.ds(pl.multiple_of(core * half, half), half), :], o_send.at[0])
    arrive(out.at[pl.ds(pl.multiple_of((1 - core) * half, half), half), :], o_recv.at[0])


def finish_kernel(*refs):
    count = len(refs) // 2
    sems = refs[-1]
    copies = [
        pltpu.make_async_copy(refs[k], refs[count + k], sems.at[k]) for k in range(count)
    ]
    for copy in copies:
        copy.start()
    for copy in copies:
        copy.wait()


def on_device(
    groups, ring,
    context, residual, out_weight, norm_gain, user_vectors, positive, item_ids, item_counts, lengths
):
    tokens, head_width = context.shape
    width = residual.shape[1]
    rows = out_weight.shape[0]
    half = rows // 2
    items_here = lengths.shape[0]
    users_here = user_vectors.shape[0]
    total = groups * ring
    lines = groups // 2
    cells = lines * ring
    hops = ring - 1
    users_total, items_total = total * users_here, total * items_here
    dma = pltpu.SemaphoreType.DMA
    half_type, full_type = jnp.bfloat16, jnp.float32
    vmem = pl.BlockSpec(memory_space=pltpu.VMEM)
    hbm = pl.BlockSpec(memory_space=pltpu.HBM)
    results = pl.pallas_call(
        functools.partial(step_kernel, groups, ring, users_here, items_here),
        out_shape=(
            jax.ShapeDtypeStruct((1, 1), full_type),
            jax.ShapeDtypeStruct((tokens, width), half_type),
            jax.ShapeDtypeStruct((tokens, head_width), half_type),
            jax.ShapeDtypeStruct((rows, width), half_type),
            jax.ShapeDtypeStruct((1, width), full_type),
            jax.ShapeDtypeStruct((users_here, width), half_type),
        ),
        in_specs=[hbm] * 9,
        out_specs=(vmem,) * 6,
        scratch_shapes=[
            pltpu.VMEM((tokens, head_width), half_type),
            pltpu.VMEM((head_width, tokens), half_type),
            pltpu.VMEM((tokens, width), half_type),
            pltpu.VMEM((ring * rows, width), half_type),
            pltpu.VMEM((total, users_here, width + 128), half_type),
            pltpu.VMEM((tokens, width), full_type),
            pltpu.VMEM((tokens, 1), full_type),
            pltpu.VMEM((users_total, width + 128), half_type),
            pltpu.VMEM((8, width), full_type),
            pltpu.VMEM((8, width), full_type),
            pltpu.VMEM((total, items_here, width), half_type),
            pltpu.VMEM((items_total, width), full_type),
            pltpu.VMEM((items_total, width), full_type),
            pltpu.VMEM((ring * rows, width), half_type),
            pltpu.VMEM((ring, half, width), half_type),
            pltpu.VMEM((hops, half, width), half_type),
            pltpu.VMEM((hops, half, width), half_type),
            pltpu.VMEM((lines, half, width), half_type),
            pltpu.VMEM((ring, half // CHUNKS, width), half_type),
            pltpu.VMEM((ring, half // CHUNKS, width), half_type),
            pltpu.VMEM((1, width), full_type),
            pltpu.SMEM((users_here,), jnp.int32),
            pltpu.SMEM((items_here,), jnp.int32),
            pltpu.SMEM((items_here,), jnp.int32),
            pltpu.SMEM((items_here,), jnp.int32),
            dma((9,)),
            dma((1,)),
            dma((hops, CHUNKS)),
            dma((hops,)),
            dma((hops,)),
            dma((1,)),
            dma((hops,)),
            dma((ring, max(lines - 1, 1))),
            dma((lines,)),
            dma((1,)),
            dma((lines,)),
            dma((lines,)),
            dma((1,)),
            dma((ring,)),
            dma((1,)),
            dma((hops, CHUNKS - 1 if lines == 2 else CHUNKS)),
            dma((1,)),
            dma((max(lines - 1, 1), CHUNKS)),
            dma((1,)),
            dma((1,)),
            dma((1,)),
            dma((ring,)),
            dma((1,)),
            dma((1,)),
        ],
        compiler_params=pltpu.CompilerParams(
            collective_id=0, has_side_effects=True, vmem_limit_bytes=48 << 20
        ),
        name="whole_step",
    )(
        *(
            pltpu.with_memory_space_constraint(operand, pltpu.HBM)
            for operand in (
                context, residual, out_weight, norm_gain[None, :], user_vectors,
                positive, item_ids, item_counts, lengths,
            )
        )
    )
    loss, residual_grad, context_grad, weight_grad, gain_grad, user_grad = pl.pallas_call(
        finish_kernel,
        out_shape=tuple(jax.ShapeDtypeStruct(r.shape, r.dtype) for r in results),
        in_specs=[vmem] * len(results),
        out_specs=(hbm,) * len(results),
        scratch_shapes=[dma((len(results),))],
        compiler_params=pltpu.CompilerParams(vmem_limit_bytes=1 << 20),
        name="finish",
    )(*results)
    return (loss[0, 0], residual_grad, context_grad, weight_grad, gain_grad[0], user_grad)


def solution(mesh):
    placed = (
        P(("dp", "fsdp"), None),
        P(("dp", "fsdp"), None),
        P("fsdp", None),
        P(),
        P(("dp", "fsdp"), None),
        P(("dp", "fsdp")),
        P(("dp", "fsdp")),
        P(("dp", "fsdp")),
        P(("dp", "fsdp")),
    )
    return jax.shard_map(
        functools.partial(on_device, mesh.shape["dp"], mesh.shape["fsdp"]),
        mesh=mesh,
        in_specs=placed,
        out_specs=(
            P(),
            P(("dp", "fsdp"), None),
            P(("dp", "fsdp"), None),
            P("fsdp", None),
            P(),
            P(("dp", "fsdp"), None),
        ),
        check_vma=False,
    )
```

```python
import functools

import jax
import jax.numpy as jnp
from jax import lax
from jax.experimental import pallas as pl
from jax.experimental.pallas import tpu as pltpu
from jax.sharding import PartitionSpec as P

EPSILON = 1e-06
MASKED_FILL = -1e30
MESH = pl.DeviceIdType.MESH
CHUNKS = 4
LAG = 1


def contract_last(left, right):
    return lax.dot_general(
        left, right, (((1,), (1,)), ((), ())), preferred_element_type=jnp.float32
    )


def ring_place(index, count):
    return jnp.where(index % 2 == 0, index // 2, count - 1 - index // 2)


def ring_index(place, count):
    return jnp.where(place < count // 2, 2 * place, 2 * (count - 1 - place) + 1)


def remote(src, dst, send_sem, recv_sem, device):
    return pltpu.make_async_remote_copy(
        src_ref=src,
        dst_ref=dst,
        send_sem=send_sem,
        recv_sem=recv_sem,
        device_id=device,
        device_id_type=MESH,
    )


def step_kernel(
    groups, ring, users_here, items_here,
    ctx_in, res_in, w_in, gain_hbm, u_in, pos_hbm, ids_hbm, counts_hbm, len_hbm,
    loss_out, rg_out, cg_out, out, gain_out, ug_out,
    ctx, ctx_t, res, w_out, u_out, acc, inv, users, pooled, emb, e_all, e_rows, e_grad,
    part_in, cross, held, arrived, totals, lent, borrowed,
    gain_in, pos_in, ids_in, counts_in, len_in,
    own_sem, w_send, w_recv, p_recv, y_recv, u_send, u_recv, ul_recv, up_recv,
    e_send, e_recv, ep_recv, x_send, x_recv, r_send, r_recv, t_send, t_recv, o_send, o_recv,
    b_send, b_recv, f_send, f_recv,
):
    group, index = lax.axis_index("dp"), lax.axis_index("fsdp")
    total = groups * ring
    me = group * ring + index
    lines = groups // 2
    cells = lines * ring
    split = lines == 2
    line = group // 2
    core = lax.rem(group, 2)
    cell = line * ring + index
    partner = group + 1 - 2 * core
    across = lax.rem(group + 2, groups)
    place = ring_place(index, ring)
    turn = 1 - 2 * core
    ends = (
        ring_index(lax.rem(place + ring + turn, ring), ring),
        ring_index(lax.rem(place + ring - turn, ring), ring),
    )
    rows, width = w_in.shape
    tokens = ctx_in.shape[0]
    item_length = tokens // items_here
    users_total, items_total = total * users_here, total * items_here
    half = rows // 2
    part = half // CHUNKS
    hops = ring - 1

    def cell_device(c):
        return (2 * (c // ring) + core, lax.rem(c, ring))

    own = [
        pltpu.make_async_copy(u_in, u_out.at[me, :, pl.ds(0, width)], own_sem.at[0]),
        pltpu.make_async_copy(ctx_in, ctx, own_sem.at[1]),
        pltpu.make_async_copy(
            w_in, w_out.at[pl.ds(pl.multiple_of(index * rows, rows), rows), :], own_sem.at[2]
        ),
        pltpu.make_async_copy(res_in, res, own_sem.at[3]),
        pltpu.make_async_copy(gain_hbm, gain_in, own_sem.at[4]),
        pltpu.make_async_copy(pos_hbm, pos_in, own_sem.at[5]),
        pltpu.make_async_copy(ids_hbm, ids_in, own_sem.at[6]),
        pltpu.make_async_copy(counts_hbm, counts_in, own_sem.at[7]),
        pltpu.make_async_copy(len_hbm, len_in, own_sem.at[8]),
    ]
    for copy in own[4:] + [own[2], own[0], own[1], own[3]]:
        copy.start()

    barrier = pltpu.get_barrier_semaphore()

    def greet(k, carry):
        peer = cell_device(lax.rem(cell + k, cells))
        pl.semaphore_signal(barrier, inc=1, device_id=peer, device_id_type=MESH)
        return carry

    near = [(partner, index), (group, ends[0]), (group, ends[1]), (across, index)]
    for peer in near if split else near[:1]:
        pl.semaphore_signal(barrier, inc=1, device_id=peer, device_id_type=MESH)
    if not split:
        lax.fori_loop(1, cells, greet, 0)

    for copy in own[4:]:
        copy.wait()
    seat = lax.broadcasted_iota(jnp.int32, (users_here, 128), 0)
    lane = lax.broadcasted_iota(jnp.int32, (users_here, 128), 1)
    keys = jnp.zeros((users_here, 128), jnp.float32)
    for k in range(users_here):
        value = pos_in[k].astype(jnp.float32)
        keys = jnp.where((seat == k) & (lane == 0), value, keys)
    for k in range(items_here):
        count = counts_in[k]
        for at, number in enumerate((ids_in[k], count // 256, lax.rem(count, 256))):
            value = number.astype(jnp.float32)
            keys = jnp.where((seat == k) & (lane == at + 1), value, keys)
    u_out[me, :, pl.ds(width, 128)] = keys.astype(u_out.dtype)

    pl.semaphore_wait(barrier, len(near) if split else cells)

    def owner(m, way=turn):
        if m == hops + 2:
            return index
        away = -(m // 2) if m % 2 == 0 else m // 2
        return ring_index(lax.rem(place + ring + way * away, ring), ring)

    def chunk(j):
        if not split or j < CHUNKS - 2:
            return j
        return CHUNKS - 2 + (line if j == CHUNKS - 2 else 1 - line)

    def w_slice(who, j, side=core):
        start = pl.multiple_of(who * rows + side * half + chunk(j) * part, part)
        return w_out.at[pl.ds(start, part), :]

    def ring_pieces(m):
        if not split:
            return list(range(CHUNKS))
        first = [CHUNKS - 2] + list(range(CHUNKS - 2))
        return first + [CHUNKS - 1] if m == hops - 1 else first

    def w_ring(m, j, shift=0):
        ref = w_slice(owner(m + shift), j)
        return remote(ref, ref, w_send.at[0], w_recv.at[m, j], (group, ends[m % 2]))

    def w_part(m, j, side=core):
        ref = w_slice(owner(m + 2, 1 - 2 * side), j, side)
        return remote(ref, ref, w_send.at[0], p_recv.at[m], (partner, index))

    def w_across(m, j):
        ref = w_slice(owner(m + 2), j)
        return remote(ref, ref, w_send.at[0], y_recv.at[m], (across, index))

    def settle(ref, sem):
        remote(ref, ref, sem, sem, (partner, index)).wait_send()

    def arrive(ref, sem):
        remote(ref, ref, sem, sem, (partner, index)).wait_recv()

    def s_ring(m, shift):
        ref = u_out.at[group * ring + owner(m + shift)]
        return remote(ref, ref, u_send.at[0], u_recv.at[m], (group, ends[m % 2]))

    def s_line(s, k):
        ref = u_out.at[group * ring + owner(s + 2)]
        peer = lax.rem(group + 2 * k, groups)
        return remote(ref, ref, u_send.at[0], ul_recv.at[s, k - 1], (peer, index))

    def s_line_in(s, k):
        source = lax.rem(group + groups - 2 * k, groups)
        ref = u_out.at[source * ring + owner(s + 2)]
        return remote(ref, ref, u_send.at[0], ul_recv.at[s, k - 1], (source, index))

    def s_part(s, k):
        source = lax.rem(group + groups - 2 * k, groups)
        ref = u_out.at[source * ring + owner(s + 2)]
        return remote(ref, ref, u_send.at[0], up_recv.at[source // 2], (partner, index))

    def spread(s):
        for k in range(1, lines):
            s_line(s, k).start()
        s_part(s, 0).start()

    def s_pass(s):
        for k in range(1, lines):
            s_line_in(s, k).wait_recv()
            s_part(s, k).start()

    def s_step(m):
        s_ring(m, 2).wait_recv()
        if m + 2 < hops:
            s_ring(m + 2, 0).start()
        spread(m)
        if m == 1:
            s_pass(hops)
        if m >= 2:
            s_pass(m - 2)

    def has_across(m):
        return split and m < hops - 1

    def w_pass(m):
        if has_across(m):
            w_across(m, CHUNKS - 1).wait_recv()
            w_part(m, CHUNKS - 1).start()
            if m + 2 == hops - 1:
                w_ring(m + 2, CHUNKS - 1).start()

    def drain_gather():
        sends = sum(len(ring_pieces(m)) + has_across(m) + CHUNKS for m in range(hops))
        settle(w_out.at[pl.ds(0, sends * part), :], w_send.at[0])
        settle(u_out.at[pl.ds(0, hops + ring * (2 * lines - 1))], u_send.at[0])

    def both_rows(a, b):
        return [pl.ds(pl.multiple_of(who * rows, rows), rows) for who in (a, b)]

    def forward(a, b, start=False):
        first, second = both_rows(a, b)
        left = jnp.concatenate([ctx[:, first], ctx[:, second]], axis=1)
        right = jnp.concatenate([w_out[first, :], w_out[second, :]], axis=0)
        base = res[...].astype(jnp.float32) if start else acc[...]
        acc[...] = base + jnp.dot(left, right, preferred_element_type=jnp.float32)

    def w_ready(m):
        who = owner(m + 2, -turn)
        start = pl.multiple_of(who * rows + (1 - core) * half, half)
        arrive(w_out.at[pl.ds(start, half), :], p_recv.at[m])

    def turn_over(s, carry):
        at = pl.ds(pl.multiple_of(s * rows, rows), rows)
        ctx_t[at, :] = ctx[:, at].astype(jnp.float32).T.astype(ctx_t.dtype)
        return carry

    own[2].wait()
    for j in ring_pieces(0):
        for m in range(2):
            w_ring(m, j).start()
    own[0].wait()
    spread(hops)

    def s_first():
        for m in range(2):
            s_ring(m, 0).start()

    small_jobs = [[s_first]]
    for m in range(0, hops, 2):
        small_jobs.append([functools.partial(s_step, q) for q in (m, m + 1) if q < hops])
    for _ in range(LAG):
        small_jobs.insert(0, [])

    def small_turn():
        for job in small_jobs.pop(0) if small_jobs else ():
            job()

    small_turn()
    own[1].wait()
    lax.fori_loop(0, ring, turn_over, 0)
    own[3].wait()
    pairs = ring // 2
    for pair in range(pairs):
        both = [m for m in (2 * pair, 2 * pair + 1) if m < hops]
        for j in ring_pieces(both[0]):
            for m in both:
                w_ring(m, j, 2).wait_recv()
                if m + 2 < hops:
                    w_ring(m + 2, j).start()
                if has_across(m) and j == CHUNKS - 2:
                    w_across(m, j).start()
                w_part(m, j).start()
            if pair >= 1 and j == ring_pieces(0)[0]:
                for m in (2 * pair - 2, 2 * pair - 1):
                    w_pass(m)
        small_turn()
        if pair >= 1:
            for m in (2 * pair - 2, 2 * pair - 1):
                w_ready(m)
            forward(owner(2 * pair), owner(2 * pair + 1), pair == 1)
    w_pass(hops - 1)
    w_ready(hops - 1)
    forward(owner(hops + 1), index, pairs == 1)
    small_turn()

    gain = gain_in[...]
    block = 32
    cap = 16

    def spans(i):
        return len_in[i].astype(jnp.float32)

    def inside_of(i, r):
        at = r * block + lax.broadcasted_iota(jnp.int32, (block, 1), 0)
        return (at < len_in[i]).astype(jnp.float32)

    values = []
    for i in range(items_here):

        def pool(r, carry, i=i):
            at = pl.ds(pl.multiple_of(i * item_length + r * block, block), block)
            x = acc[at, :]
            scale = lax.rsqrt(jnp.sum(x * x, axis=1, keepdims=True) / width + EPSILON)
            inv[at, :] = scale
            y = x * (scale * inside_of(i, r))
            for q in range(block // 8):
                carry = carry + y[q * 8 : q * 8 + 8, :]
            return carry

        summed = lax.fori_loop(
            0, item_length // block, pool, jnp.zeros((8, width), jnp.float32), unroll=8
        )
        summed = jnp.sum(summed, axis=0, keepdims=True)
        mean = gain * summed / spans(i)
        scale = lax.rsqrt(jnp.mean(mean * mean, axis=1, keepdims=True) + EPSILON)
        pooled[pl.ds(i, 1), :] = mean
        values.append((mean, scale))
        emb[pl.ds(i, 1), :] = mean * scale
    e_all[me] = emb[pl.ds(0, items_here), :].astype(e_all.dtype)

    def e_push(k):
        return remote(
            e_all.at[me], e_all.at[me], e_send.at[0], e_recv.at[line],
            cell_device(lax.rem(cell + k, cells)),
        )

    def e_part(row, side=core):
        ref = e_all.at[pl.ds((2 * row + side) * ring, ring)]
        return remote(ref, ref, e_send.at[0], ep_recv.at[row], (partner, index))

    def push(k, carry):
        e_push(k).start()
        return carry

    def drain_share():
        settle(e_all.at[pl.ds(0, cells - 1 + cells)], e_send.at[0])

    lax.fori_loop(1, cells, push, 0)
    while small_jobs:
        small_turn()
    for m in range(hops - 2, hops):
        s_pass(m)

    for row in range(lines):
        arrive(u_out.at[pl.ds((2 * row + 1 - core) * ring, ring)], up_recv.at[row])

    def join(p, carry):
        block_rows = [u_out[2 * p].astype(jnp.float32), u_out[2 * p + 1].astype(jnp.float32)]
        at = pl.ds(pl.multiple_of(p * 2 * users_here, 2 * users_here), 2 * users_here)
        users[at, :] = jnp.concatenate(block_rows, axis=0).astype(users.dtype)
        return carry

    lax.fori_loop(0, total // 2, join, 0)
    tags = users[:, pl.ds(width, 128)]
    shape = (16, 128)
    pick = lax.broadcasted_iota(jnp.int32, shape, 0) == lax.broadcasted_iota(jnp.int32, shape, 1)
    pick = pick.astype(jnp.float32).astype(jnp.bfloat16)
    positive = contract_last(pick, tags)[0:1, :]
    shape = (items_total, users_total)
    item_at = lax.broadcasted_iota(jnp.int32, shape, 0)
    user_at = lax.broadcasted_iota(jnp.int32, shape, 1)
    pick = (item_at // items_here == user_at // users_here) & (
        lax.rem(item_at, items_here) == lax.rem(user_at, users_here)
    )
    pick = pick.astype(jnp.float32).astype(jnp.bfloat16)
    table = jnp.dot(pick, tags, preferred_element_type=jnp.float32)
    ids = table[:, 1:2]
    log_counts = jnp.log(table[:, 2:3] * 256.0 + table[:, 3:4])
    chosen = item_at.astype(jnp.float32) == positive
    positive_id = jnp.sum(jnp.where(chosen, ids, 0.0), axis=0, keepdims=True)
    excluded = (ids == positive_id) & jnp.logical_not(chosen)

    for k in range(lines):
        if k == 0:
            arrive(e_all.at[pl.ds((2 * line + core) * ring, ring - 1)], e_recv.at[line])
        else:
            row = lax.rem(line + k, lines)
            arrive(e_all.at[pl.ds((2 * row + core) * ring, ring)], e_recv.at[row])
        e_part(lax.rem(line + k, lines)).start()
    for row in range(lines):
        arrive(e_all.at[pl.ds((2 * row + 1 - core) * ring, ring)], ep_recv.at[row])
    for d in range(total):
        e_rows[pl.ds(d * items_here, items_here), :] = e_all[d].astype(jnp.float32)
    emb_all = e_rows[...].astype(jnp.bfloat16)
    words = users[:, pl.ds(0, width)]
    scores = contract_last(emb_all, words)
    logits = jnp.where(excluded, MASKED_FILL, scores - log_counts)
    top = jnp.max(logits, axis=0, keepdims=True)
    weights = jnp.where(excluded, 0.0, jnp.exp(logits - top))
    sums = jnp.sum(weights, axis=0, keepdims=True)
    logit_grad = (weights / sums - chosen.astype(jnp.float32)).astype(jnp.bfloat16)
    e_grad[...] = jnp.dot(logit_grad, words, preferred_element_type=jnp.float32)

    for i in range(items_here):
        mean, scale = values[i]
        grad = e_grad[pl.ds(me * items_here + i, 1), :]
        pooled_grad = scale * grad - mean * (
            scale * scale * scale * jnp.mean(mean * grad, axis=1, keepdims=True)
        )
        reach = jnp.broadcast_to(gain * (pooled_grad / spans(i)), (8, width))

        def back(r, carry, i=i, reach=reach):
            at = pl.ds(pl.multiple_of(i * item_length + r * cap, cap), cap)
            x = acc[at, :]
            scale = inv[at, :]
            h = jnp.concatenate([reach] * (cap // 8), axis=0)
            where = r * cap + lax.broadcasted_iota(jnp.int32, (cap, 1), 0)
            keep = jnp.where(where < len_in[i], scale, 0.0)
            dots = jnp.sum(x * h, axis=1, keepdims=True) / width
            rg_out[at, :] = (keep * h - x * (keep * scale * scale * dots)).astype(rg_out.dtype)
            return carry

        lax.fori_loop(0, item_length // cap, back, 0, unroll=16)

    def target(m, way=turn):
        if m == hops:
            return index
        away = ring // 2 - m // 2 if m % 2 == 0 else m // 2 - (ring - 1) // 2
        return ring_index(lax.rem(place + ring + way * away, ring), ring)

    def weight_block(a, b):
        first, second = both_rows(target(a), target(b))
        left = jnp.concatenate([ctx_t[first, :], ctx_t[second, :]], axis=0)
        found = jnp.dot(left, rg_out[...], preferred_element_type=jnp.float32)
        found = found.astype(part_in.dtype)
        part_in[first, :] = found[:rows, :]
        part_in[second, :] = found[rows:, :]

    def cross_out(m):
        start = pl.multiple_of(target(m, -turn) * rows + (1 - core) * half, half)
        return remote(
            part_in.at[pl.ds(start, half), :], cross.at[m], x_send.at[0], x_recv.at[m],
            (partner, index),
        )

    slots = CHUNKS - 1 if split else CHUNKS

    def ring_copy(s, c):
        at = pl.ds(c * part, part)
        return remote(
            held.at[s, at, :], arrived.at[s, at, :], r_send.at[0], r_recv.at[s, c],
            (group, ends[s % 2]),
        )

    def local_term(s, j):
        offset = chunk(j) * part
        start = pl.multiple_of(target(s) * rows + core * half + offset, part)
        mine = part_in[pl.ds(start, part), :].astype(jnp.float32)
        return mine + cross[s, pl.ds(pl.multiple_of(offset, part), part), :].astype(jnp.float32)

    def lend(s):
        return remote(lent.at[s], borrowed.at[s], b_send.at[0], b_recv.at[s], (across, index))

    def prepare(s):
        cross_out(s).wait_recv()
        if split:
            lent[s] = local_term(s, CHUNKS - 1).astype(lent.dtype)
            lend(s).start()

    def term_of(s, j):
        term = local_term(s, j)
        if split and j == CHUNKS - 2:
            lend(s).wait_recv()
            term = term + borrowed[s].astype(jnp.float32)
        return term

    head_width = cg_out.shape[1]

    tile = 256

    def context_block(n):
        at = pl.ds(n * tile, tile)
        cg_out[:, at] = contract_last(rg_out[...], w_out[at, :]).astype(cg_out.dtype)

    def last_bits():
        log_total = top + jnp.log(sums)
        picked = jnp.sum(jnp.where(chosen, logits, 0.0), axis=0, keepdims=True)
        loss_out[...] = jnp.mean(log_total - picked, axis=1, keepdims=True)
        shape = (16, users_total)
        seat = lax.broadcasted_iota(jnp.int32, shape, 0)
        mine = lax.broadcasted_iota(jnp.int32, shape, 1) == me * users_here + seat
        mine = (mine & (seat < users_here)).astype(jnp.float32).astype(jnp.bfloat16)
        own_grad = contract_last(mine, logit_grad).astype(jnp.bfloat16)
        found = jnp.dot(own_grad, emb_all, preferred_element_type=jnp.float32)
        ug_out[...] = found[:users_here, :].astype(ug_out.dtype)
        e = e_rows[...]
        g = e_grad[...]
        along = jnp.mean(e * g, axis=1, keepdims=True)
        gain_out[...] = jnp.sum(e * (g - e * along), axis=0, keepdims=True) / gain

    extra = [functools.partial(context_block, n) for n in range(head_width // tile)]
    extra.append(last_bits)

    def ready(m):
        weight_block(m, m + 1)
        cross_out(m).start()
        cross_out(m + 1).start()
        if m + 2 == hops:
            cross_out(hops).start()

    weight_block(0, hops)
    cross_out(0).start()
    ready(1)
    prepare(0)
    for pair in range(pairs):
        both = [m for m in (2 * pair, 2 * pair + 1) if m < hops]
        for j in range(slots):
            at = pl.ds(j * part, part)
            if j == slots - 1:
                for m in both:
                    if m + 2 < ring:
                        prepare(m + 2)
            for m in both:
                if m == 1 and j == 0:
                    prepare(1)
                term = term_of(m, j)
                if m >= 2:
                    ring_copy(m - 2, j).wait_recv()
                    term = term + arrived[m - 2, at, :].astype(jnp.float32)
                held[m, at, :] = term.astype(held.dtype)
                ring_copy(m, j).start()
            if pair >= 1 and j < 2 and extra:
                extra.pop(0)()
            coming = 2 * pair + 3
            if j == 0 and coming + 1 < ring:
                ready(coming)
    for job in extra:
        job()
    last = hops

    def total_copy(k, j):
        ref = totals.at[line, pl.ds(j * part, part), :]
        return remote(
            ref, ref, t_send.at[0], t_recv.at[k - 1, j],
            (lax.rem(group + 2 * k, groups), index),
        )

    def total_in(k, j):
        source = lax.rem(group + groups - 2 * k, groups)
        ref = totals.at[source // 2, pl.ds(j * part, part), :]
        return remote(ref, ref, t_send.at[0], t_recv.at[k - 1, j], (source, index))

    def out_rows(j, side=core):
        return pl.ds(pl.multiple_of(side * half + chunk(j) * part, part), part)

    def out_copy(j, side):
        ref = out.at[out_rows(j, side), :]
        return remote(ref, ref, o_send.at[0], o_recv.at[0], (partner, index))

    def out_across(j):
        ref = out.at[out_rows(j), :]
        return remote(ref, ref, f_send.at[0], f_recv.at[0], (across, index))

    shared = range(CHUNKS - 2) if split else range(CHUNKS)
    for j in range(slots):
        at = pl.ds(j * part, part)
        term = term_of(last, j)
        for m in range(max(hops - 2, 0), hops):
            ring_copy(m, j).wait_recv()
            term = term + arrived[m, at, :].astype(jnp.float32)
        value = term.astype(totals.dtype)
        if j in shared:
            totals[line, at, :] = value
            for k in range(1, lines):
                total_copy(k, j).start()
        else:
            out[out_rows(j), :] = value
            out_across(j).start()
            out_copy(j, core).start()

    for j in shared:
        at = pl.ds(j * part, part)
        for k in range(1, lines):
            total_in(k, j).wait_recv()
        value = totals[0, at, :].astype(jnp.float32)
        for other in range(1, lines):
            value = value + totals[other, at, :].astype(jnp.float32)
        out[out_rows(j), :] = value.astype(out.dtype)
        out_copy(j, core).start()
    if split:
        out_across(CHUNKS - 1).wait_recv()
        out_copy(CHUNKS - 1, core).start()

    drain_gather()
    drain_share()
    settle(cross, x_send.at[0])
    if split:
        settle(lent, b_send.at[0])
    settle(part_in.at[pl.ds(0, hops * slots * part), :], r_send.at[0])
    settle(part_in.at[pl.ds(0, (lines - 1) * len(shared) * part), :], t_send.at[0])
    if split:
        out_across(CHUNKS - 2).wait_send()
    settle(out.at[pl.ds(pl.multiple_of(core * half, half), half), :], o_send.at[0])
    arrive(out.at[pl.ds(pl.multiple_of((1 - core) * half, half), half), :], o_recv.at[0])


def finish_kernel(*refs):
    count = len(refs) // 2
    sems = refs[-1]
    copies = [
        pltpu.make_async_copy(refs[k], refs[count + k], sems.at[k]) for k in range(count)
    ]
    for copy in copies:
        copy.start()
    for copy in copies:
        copy.wait()


def on_device(
    groups, ring,
    context, residual, out_weight, norm_gain, user_vectors, positive, item_ids, item_counts, lengths
):
    tokens, head_width = context.shape
    width = residual.shape[1]
    rows = out_weight.shape[0]
    half = rows // 2
    items_here = lengths.shape[0]
    users_here = user_vectors.shape[0]
    total = groups * ring
    lines = groups // 2
    cells = lines * ring
    hops = ring - 1
    users_total, items_total = total * users_here, total * items_here
    dma = pltpu.SemaphoreType.DMA
    half_type, full_type = jnp.bfloat16, jnp.float32
    vmem = pl.BlockSpec(memory_space=pltpu.VMEM)
    hbm = pl.BlockSpec(memory_space=pltpu.HBM)
    results = pl.pallas_call(
        functools.partial(step_kernel, groups, ring, users_here, items_here),
        out_shape=(
            jax.ShapeDtypeStruct((1, 1), full_type),
            jax.ShapeDtypeStruct((tokens, width), half_type),
            jax.ShapeDtypeStruct((tokens, head_width), half_type),
            jax.ShapeDtypeStruct((rows, width), half_type),
            jax.ShapeDtypeStruct((1, width), full_type),
            jax.ShapeDtypeStruct((users_here, width), half_type),
        ),
        in_specs=[hbm] * 9,
        out_specs=(vmem,) * 6,
        scratch_shapes=[
            pltpu.VMEM((tokens, head_width), half_type),
            pltpu.VMEM((head_width, tokens), half_type),
            pltpu.VMEM((tokens, width), half_type),
            pltpu.VMEM((ring * rows, width), half_type),
            pltpu.VMEM((total, users_here, width + 128), half_type),
            pltpu.VMEM((tokens, width), full_type),
            pltpu.VMEM((tokens, 1), full_type),
            pltpu.VMEM((users_total, width + 128), half_type),
            pltpu.VMEM((8, width), full_type),
            pltpu.VMEM((8, width), full_type),
            pltpu.VMEM((total, items_here, width), half_type),
            pltpu.VMEM((items_total, width), full_type),
            pltpu.VMEM((items_total, width), full_type),
            pltpu.VMEM((ring * rows, width), half_type),
            pltpu.VMEM((ring, half, width), half_type),
            pltpu.VMEM((hops, half, width), half_type),
            pltpu.VMEM((hops, half, width), half_type),
            pltpu.VMEM((lines, half, width), half_type),
            pltpu.VMEM((ring, half // CHUNKS, width), half_type),
            pltpu.VMEM((ring, half // CHUNKS, width), half_type),
            pltpu.VMEM((1, width), full_type),
            pltpu.SMEM((users_here,), jnp.int32),
            pltpu.SMEM((items_here,), jnp.int32),
            pltpu.SMEM((items_here,), jnp.int32),
            pltpu.SMEM((items_here,), jnp.int32),
            dma((9,)),
            dma((1,)),
            dma((hops, CHUNKS)),
            dma((hops,)),
            dma((hops,)),
            dma((1,)),
            dma((hops,)),
            dma((ring, max(lines - 1, 1))),
            dma((lines,)),
            dma((1,)),
            dma((lines,)),
            dma((lines,)),
            dma((1,)),
            dma((ring,)),
            dma((1,)),
            dma((hops, CHUNKS - 1 if lines == 2 else CHUNKS)),
            dma((1,)),
            dma((max(lines - 1, 1), CHUNKS)),
            dma((1,)),
            dma((1,)),
            dma((1,)),
            dma((ring,)),
            dma((1,)),
            dma((1,)),
        ],
        compiler_params=pltpu.CompilerParams(
            collective_id=0, has_side_effects=True, vmem_limit_bytes=48 << 20
        ),
        name="whole_step",
    )(
        *(
            pltpu.with_memory_space_constraint(operand, pltpu.HBM)
            for operand in (
                context, residual, out_weight, norm_gain[None, :], user_vectors,
                positive, item_ids, item_counts, lengths,
            )
        )
    )
    loss, residual_grad, context_grad, weight_grad, gain_grad, user_grad = pl.pallas_call(
        finish_kernel,
        out_shape=tuple(jax.ShapeDtypeStruct(r.shape, r.dtype) for r in results),
        in_specs=[vmem] * len(results),
        out_specs=(hbm,) * len(results),
        scratch_shapes=[dma((len(results),))],
        compiler_params=pltpu.CompilerParams(vmem_limit_bytes=1 << 20),
        name="finish",
    )(*results)
    return (loss[0, 0], residual_grad, context_grad, weight_grad, gain_grad[0], user_grad)


def solution(mesh):
    placed = (
        P(("dp", "fsdp"), None),
        P(("dp", "fsdp"), None),
        P("fsdp", None),
        P(),
        P(("dp", "fsdp"), None),
        P(("dp", "fsdp")),
        P(("dp", "fsdp")),
        P(("dp", "fsdp")),
        P(("dp", "fsdp")),
    )
    return jax.shard_map(
        functools.partial(on_device, mesh.shape["dp"], mesh.shape["fsdp"]),
        mesh=mesh,
        in_specs=placed,
        out_specs=(
            P(),
            P(("dp", "fsdp"), None),
            P(("dp", "fsdp"), None),
            P("fsdp", None),
            P(),
            P(("dp", "fsdp"), None),
        ),
        check_vma=False,
    )
```

```python
import functools

import jax
import jax.numpy as jnp
from jax import lax
from jax.experimental import pallas as pl
from jax.experimental.pallas import tpu as pltpu
from jax.sharding import PartitionSpec as P

EPSILON = 1e-06
MASKED_FILL = -1e30
MESH = pl.DeviceIdType.MESH
CHUNKS = 4
LAG = 1


def contract_last(left, right):
    return lax.dot_general(
        left, right, (((1,), (1,)), ((), ())), preferred_element_type=jnp.float32
    )


def ring_place(index, count):
    return jnp.where(index % 2 == 0, index // 2, count - 1 - index // 2)


def ring_index(place, count):
    return jnp.where(place < count // 2, 2 * place, 2 * (count - 1 - place) + 1)


def remote(src, dst, send_sem, recv_sem, device):
    return pltpu.make_async_remote_copy(
        src_ref=src,
        dst_ref=dst,
        send_sem=send_sem,
        recv_sem=recv_sem,
        device_id=device,
        device_id_type=MESH,
    )


def step_kernel(
    groups, ring, users_here, items_here,
    ctx_in, res_in, w_in, gain_hbm, u_in, pos_hbm, ids_hbm, counts_hbm, len_hbm,
    loss_out, rg_out, cg_out, out, gain_out, ug_out,
    ctx, ctx_t, res, w_out, u_out, acc, inv, users, pooled, emb, e_all, e_rows, e_grad,
    part_in, cross, held, arrived, totals, lent, borrowed,
    gain_in, pos_in, ids_in, counts_in, len_in,
    own_sem, w_send, w_recv, p_recv, y_recv, u_send, u_recv, ul_recv, up_recv,
    e_send, e_recv, ep_recv, x_send, x_recv, r_send, r_recv, t_send, t_recv, o_send, o_recv,
    b_send, b_recv, f_send, f_recv,
):
    group, index = lax.axis_index("dp"), lax.axis_index("fsdp")
    total = groups * ring
    me = group * ring + index
    lines = groups // 2
    cells = lines * ring
    split = lines == 2
    line = group // 2
    core = lax.rem(group, 2)
    cell = line * ring + index
    partner = group + 1 - 2 * core
    across = lax.rem(group + 2, groups)
    place = ring_place(index, ring)
    turn = 1 - 2 * core
    ends = (
        ring_index(lax.rem(place + ring + turn, ring), ring),
        ring_index(lax.rem(place + ring - turn, ring), ring),
    )
    rows, width = w_in.shape
    tokens = ctx_in.shape[0]
    item_length = tokens // items_here
    users_total, items_total = total * users_here, total * items_here
    half = rows // 2
    part = half // CHUNKS
    hops = ring - 1

    def cell_device(c):
        return (2 * (c // ring) + core, lax.rem(c, ring))

    own = [
        pltpu.make_async_copy(u_in, u_out.at[me, :, pl.ds(0, width)], own_sem.at[0]),
        pltpu.make_async_copy(ctx_in, ctx, own_sem.at[1]),
        pltpu.make_async_copy(
            w_in, w_out.at[pl.ds(pl.multiple_of(index * rows, rows), rows), :], own_sem.at[2]
        ),
        pltpu.make_async_copy(res_in, res, own_sem.at[3]),
        pltpu.make_async_copy(gain_hbm, gain_in, own_sem.at[4]),
        pltpu.make_async_copy(pos_hbm, pos_in, own_sem.at[5]),
        pltpu.make_async_copy(ids_hbm, ids_in, own_sem.at[6]),
        pltpu.make_async_copy(counts_hbm, counts_in, own_sem.at[7]),
        pltpu.make_async_copy(len_hbm, len_in, own_sem.at[8]),
    ]
    for copy in own[4:] + [own[2], own[0], own[1], own[3]]:
        copy.start()

    barrier = pltpu.get_barrier_semaphore()

    def greet(k, carry):
        peer = cell_device(lax.rem(cell + k, cells))
        pl.semaphore_signal(barrier, inc=1, device_id=peer, device_id_type=MESH)
        return carry

    near = [(partner, index), (group, ends[0]), (group, ends[1]), (across, index)]
    for peer in near if split else near[:1]:
        pl.semaphore_signal(barrier, inc=1, device_id=peer, device_id_type=MESH)
    if not split:
        lax.fori_loop(1, cells, greet, 0)

    for copy in own[4:]:
        copy.wait()
    seat = lax.broadcasted_iota(jnp.int32, (users_here, 128), 0)
    lane = lax.broadcasted_iota(jnp.int32, (users_here, 128), 1)
    keys = jnp.zeros((users_here, 128), jnp.float32)
    for k in range(users_here):
        value = pos_in[k].astype(jnp.float32)
        keys = jnp.where((seat == k) & (lane == 0), value, keys)
    for k in range(items_here):
        count = counts_in[k]
        for at, number in enumerate((ids_in[k], count // 256, lax.rem(count, 256))):
            value = number.astype(jnp.float32)
            keys = jnp.where((seat == k) & (lane == at + 1), value, keys)
    u_out[me, :, pl.ds(width, 128)] = keys.astype(u_out.dtype)

    pl.semaphore_wait(barrier, len(near) if split else cells)

    def owner(m, way=turn):
        if m == hops + 2:
            return index
        away = -(m // 2) if m % 2 == 0 else m // 2
        return ring_index(lax.rem(place + ring + way * away, ring), ring)

    def chunk(j):
        if not split or j < CHUNKS - 2:
            return j
        return CHUNKS - 2 + (line if j == CHUNKS - 2 else 1 - line)

    def w_slice(who, j, side=core):
        start = pl.multiple_of(who * rows + side * half + chunk(j) * part, part)
        return w_out.at[pl.ds(start, part), :]

    def ring_pieces(m):
        if not split:
            return list(range(CHUNKS))
        first = [CHUNKS - 2] + list(range(CHUNKS - 2))
        return first + [CHUNKS - 1] if m == hops - 1 else first

    def w_ring(m, j, shift=0):
        ref = w_slice(owner(m + shift), j)
        return remote(ref, ref, w_send.at[0], w_recv.at[m, j], (group, ends[m % 2]))

    def w_part(m, j, side=core):
        ref = w_slice(owner(m + 2, 1 - 2 * side), j, side)
        return remote(ref, ref, w_send.at[0], p_recv.at[m], (partner, index))

    def w_across(m, j):
        ref = w_slice(owner(m + 2), j)
        return remote(ref, ref, w_send.at[0], y_recv.at[m], (across, index))

    def settle(ref, sem):
        remote(ref, ref, sem, sem, (partner, index)).wait_send()

    def arrive(ref, sem):
        remote(ref, ref, sem, sem, (partner, index)).wait_recv()

    def s_ring(m, shift):
        ref = u_out.at[group * ring + owner(m + shift)]
        return remote(ref, ref, u_send.at[0], u_recv.at[m], (group, ends[m % 2]))

    def s_line(s, k):
        ref = u_out.at[group * ring + owner(s + 2)]
        peer = lax.rem(group + 2 * k, groups)
        return remote(ref, ref, u_send.at[0], ul_recv.at[s, k - 1], (peer, index))

    def s_line_in(s, k):
        source = lax.rem(group + groups - 2 * k, groups)
        ref = u_out.at[source * ring + owner(s + 2)]
        return remote(ref, ref, u_send.at[0], ul_recv.at[s, k - 1], (source, index))

    def s_part(s, k):
        source = lax.rem(group + groups - 2 * k, groups)
        ref = u_out.at[source * ring + owner(s + 2)]
        return remote(ref, ref, u_send.at[0], up_recv.at[source // 2], (partner, index))

    def spread(s):
        for k in range(1, lines):
            s_line(s, k).start()
        s_part(s, 0).start()

    def s_pass(s):
        for k in range(1, lines):
            s_line_in(s, k).wait_recv()
            s_part(s, k).start()

    def s_step(m):
        s_ring(m, 2).wait_recv()
        if m + 2 < hops:
            s_ring(m + 2, 0).start()
        spread(m)
        if m == 1:
            s_pass(hops)
        if m >= 2:
            s_pass(m - 2)

    def has_across(m):
        return split and m < hops - 1

    def w_pass(m):
        if has_across(m):
            w_across(m, CHUNKS - 1).wait_recv()
            w_part(m, CHUNKS - 1).start()
            if m + 2 == hops - 1:
                w_ring(m + 2, CHUNKS - 1).start()

    def drain_gather():
        sends = sum(len(ring_pieces(m)) + has_across(m) + CHUNKS for m in range(hops))
        settle(w_out.at[pl.ds(0, sends * part), :], w_send.at[0])
        settle(u_out.at[pl.ds(0, hops + ring * (2 * lines - 1))], u_send.at[0])

    def both_rows(a, b):
        return [pl.ds(pl.multiple_of(who * rows, rows), rows) for who in (a, b)]

    def forward(a, b, start=False):
        first, second = both_rows(a, b)
        left = jnp.concatenate([ctx[:, first], ctx[:, second]], axis=1)
        right = jnp.concatenate([w_out[first, :], w_out[second, :]], axis=0)
        base = res[...].astype(jnp.float32) if start else acc[...]
        acc[...] = base + jnp.dot(left, right, preferred_element_type=jnp.float32)

    def w_ready(m):
        who = owner(m + 2, -turn)
        start = pl.multiple_of(who * rows + (1 - core) * half, half)
        arrive(w_out.at[pl.ds(start, half), :], p_recv.at[m])

    def turn_over(s, carry):
        at = pl.ds(pl.multiple_of(s * rows, rows), rows)
        ctx_t[at, :] = ctx[:, at].astype(jnp.float32).T.astype(ctx_t.dtype)
        return carry

    own[2].wait()
    for j in ring_pieces(0):
        for m in range(2):
            w_ring(m, j).start()
    own[0].wait()
    spread(hops)

    def s_first():
        for m in range(2):
            s_ring(m, 0).start()

    small_jobs = [[s_first]]
    for m in range(0, hops, 2):
        small_jobs.append([functools.partial(s_step, q) for q in (m, m + 1) if q < hops])
    for _ in range(LAG):
        small_jobs.insert(0, [])

    def small_turn():
        for job in small_jobs.pop(0) if small_jobs else ():
            job()

    small_turn()
    own[1].wait()
    lax.fori_loop(0, ring, turn_over, 0)
    own[3].wait()
    pairs = ring // 2
    for pair in range(pairs):
        both = [m for m in (2 * pair, 2 * pair + 1) if m < hops]
        for j in ring_pieces(both[0]):
            for m in both:
                w_ring(m, j, 2).wait_recv()
                if m + 2 < hops:
                    w_ring(m + 2, j).start()
                if has_across(m) and j == CHUNKS - 2:
                    w_across(m, j).start()
                w_part(m, j).start()
            if pair >= 1 and j == ring_pieces(0)[0]:
                for m in (2 * pair - 2, 2 * pair - 1):
                    w_pass(m)
        small_turn()
        if pair >= 1:
            for m in (2 * pair - 2, 2 * pair - 1):
                w_ready(m)
            forward(owner(2 * pair), owner(2 * pair + 1), pair == 1)
    w_pass(hops - 1)
    w_ready(hops - 1)
    forward(owner(hops + 1), index, pairs == 1)
    small_turn()

    gain = gain_in[...]
    block = 32
    cap = 16

    def spans(i):
        return len_in[i].astype(jnp.float32)

    def inside_of(i, r):
        at = r * block + lax.broadcasted_iota(jnp.int32, (block, 1), 0)
        return (at < len_in[i]).astype(jnp.float32)

    values = []
    for i in range(items_here):

        def pool(r, carry, i=i):
            at = pl.ds(pl.multiple_of(i * item_length + r * block, block), block)
            x = acc[at, :]
            scale = lax.rsqrt(jnp.sum(x * x, axis=1, keepdims=True) / width + EPSILON)
            inv[at, :] = scale
            y = x * (scale * inside_of(i, r))
            for q in range(block // 8):
                carry = carry + y[q * 8 : q * 8 + 8, :]
            return carry

        summed = lax.fori_loop(
            0, item_length // block, pool, jnp.zeros((8, width), jnp.float32), unroll=8
        )
        summed = jnp.sum(summed, axis=0, keepdims=True)
        mean = gain * summed / spans(i)
        scale = lax.rsqrt(jnp.mean(mean * mean, axis=1, keepdims=True) + EPSILON)
        pooled[pl.ds(i, 1), :] = mean
        values.append((mean, scale))
        emb[pl.ds(i, 1), :] = mean * scale
    e_all[me] = emb[pl.ds(0, items_here), :].astype(e_all.dtype)

    def e_push(k):
        return remote(
            e_all.at[me], e_all.at[me], e_send.at[0], e_recv.at[line],
            cell_device(lax.rem(cell + k, cells)),
        )

    def e_part(row, side=core):
        ref = e_all.at[pl.ds((2 * row + side) * ring, ring)]
        return remote(ref, ref, e_send.at[0], ep_recv.at[row], (partner, index))

    def push(k, carry):
        e_push(k).start()
        return carry

    def drain_share():
        settle(e_all.at[pl.ds(0, cells - 1 + cells)], e_send.at[0])

    lax.fori_loop(1, cells, push, 0)
    while small_jobs:
        small_turn()
    for m in range(hops - 2, hops):
        s_pass(m)

    for row in range(lines):
        arrive(u_out.at[pl.ds((2 * row + 1 - core) * ring, ring)], up_recv.at[row])

    def join(p, carry):
        block_rows = [u_out[2 * p].astype(jnp.float32), u_out[2 * p + 1].astype(jnp.float32)]
        at = pl.ds(pl.multiple_of(p * 2 * users_here, 2 * users_here), 2 * users_here)
        users[at, :] = jnp.concatenate(block_rows, axis=0).astype(users.dtype)
        return carry

    lax.fori_loop(0, total // 2, join, 0)
    tags = users[:, pl.ds(width, 128)]
    shape = (16, 128)
    pick = lax.broadcasted_iota(jnp.int32, shape, 0) == lax.broadcasted_iota(jnp.int32, shape, 1)
    pick = pick.astype(jnp.float32).astype(jnp.bfloat16)
    positive = contract_last(pick, tags)[0:1, :]
    shape = (items_total, users_total)
    item_at = lax.broadcasted_iota(jnp.int32, shape, 0)
    user_at = lax.broadcasted_iota(jnp.int32, shape, 1)
    pick = (item_at // items_here == user_at // users_here) & (
        lax.rem(item_at, items_here) == lax.rem(user_at, users_here)
    )
    pick = pick.astype(jnp.float32).astype(jnp.bfloat16)
    table = jnp.dot(pick, tags, preferred_element_type=jnp.float32)
    ids = table[:, 1:2]
    log_counts = jnp.log(table[:, 2:3] * 256.0 + table[:, 3:4])
    chosen = item_at.astype(jnp.float32) == positive
    positive_id = jnp.sum(jnp.where(chosen, ids, 0.0), axis=0, keepdims=True)
    excluded = (ids == positive_id) & jnp.logical_not(chosen)

    for k in range(lines):
        if k == 0:
            arrive(e_all.at[pl.ds((2 * line + core) * ring, ring - 1)], e_recv.at[line])
        else:
            row = lax.rem(line + k, lines)
            arrive(e_all.at[pl.ds((2 * row + core) * ring, ring)], e_recv.at[row])
        e_part(lax.rem(line + k, lines)).start()
    for row in range(lines):
        arrive(e_all.at[pl.ds((2 * row + 1 - core) * ring, ring)], ep_recv.at[row])
    for d in range(total):
        e_rows[pl.ds(d * items_here, items_here), :] = e_all[d].astype(jnp.float32)
    emb_all = e_rows[...].astype(jnp.bfloat16)
    words = users[:, pl.ds(0, width)]
    scores = contract_last(emb_all, words)
    logits = jnp.where(excluded, MASKED_FILL, scores - log_counts)
    top = jnp.max(logits, axis=0, keepdims=True)
    weights = jnp.where(excluded, 0.0, jnp.exp(logits - top))
    sums = jnp.sum(weights, axis=0, keepdims=True)
    logit_grad = (weights / sums - chosen.astype(jnp.float32)).astype(jnp.bfloat16)
    e_grad[...] = jnp.dot(logit_grad, words, preferred_element_type=jnp.float32)

    for i in range(items_here):
        mean, scale = values[i]
        grad = e_grad[pl.ds(me * items_here + i, 1), :]
        pooled_grad = scale * grad - mean * (
            scale * scale * scale * jnp.mean(mean * grad, axis=1, keepdims=True)
        )
        reach = jnp.broadcast_to(gain * (pooled_grad / spans(i)), (8, width))

        def back(r, carry, i=i, reach=reach):
            at = pl.ds(pl.multiple_of(i * item_length + r * cap, cap), cap)
            x = acc[at, :]
            scale = inv[at, :]
            h = jnp.concatenate([reach] * (cap // 8), axis=0)
            where = r * cap + lax.broadcasted_iota(jnp.int32, (cap, 1), 0)
            keep = jnp.where(where < len_in[i], scale, 0.0)
            dots = jnp.sum(x * h, axis=1, keepdims=True) / width
            rg_out[at, :] = (keep * h - x * (keep * scale * scale * dots)).astype(rg_out.dtype)
            return carry

        lax.fori_loop(0, item_length // cap, back, 0, unroll=16)

    def target(m, way=turn):
        if m == hops:
            return index
        away = ring // 2 - m // 2 if m % 2 == 0 else m // 2 - (ring - 1) // 2
        return ring_index(lax.rem(place + ring + way * away, ring), ring)

    def weight_block(a, b):
        first, second = both_rows(target(a), target(b))
        left = jnp.concatenate([ctx_t[first, :], ctx_t[second, :]], axis=0)
        found = jnp.dot(left, rg_out[...], preferred_element_type=jnp.float32)
        found = found.astype(part_in.dtype)
        part_in[first, :] = found[:rows, :]
        part_in[second, :] = found[rows:, :]

    def cross_out(m):
        start = pl.multiple_of(target(m, -turn) * rows + (1 - core) * half, half)
        return remote(
            part_in.at[pl.ds(start, half), :], cross.at[m], x_send.at[0], x_recv.at[m],
            (partner, index),
        )

    slots = CHUNKS - 1 if split else CHUNKS

    def ring_copy(s, c):
        at = pl.ds(c * part, part)
        return remote(
            held.at[s, at, :], arrived.at[s, at, :], r_send.at[0], r_recv.at[s, c],
            (group, ends[s % 2]),
        )

    def local_term(s, j):
        offset = chunk(j) * part
        start = pl.multiple_of(target(s) * rows + core * half + offset, part)
        mine = part_in[pl.ds(start, part), :].astype(jnp.float32)
        return mine + cross[s, pl.ds(pl.multiple_of(offset, part), part), :].astype(jnp.float32)

    def lend(s):
        return remote(lent.at[s], borrowed.at[s], b_send.at[0], b_recv.at[s], (across, index))

    def prepare(s):
        cross_out(s).wait_recv()
        if split:
            lent[s] = local_term(s, CHUNKS - 1).astype(lent.dtype)
            lend(s).start()

    def term_of(s, j):
        term = local_term(s, j)
        if split and j == CHUNKS - 2:
            lend(s).wait_recv()
            term = term + borrowed[s].astype(jnp.float32)
        return term

    head_width = cg_out.shape[1]

    tile = 256

    def context_block(n):
        at = pl.ds(n * tile, tile)
        cg_out[:, at] = contract_last(rg_out[...], w_out[at, :]).astype(cg_out.dtype)

    def last_bits():
        log_total = top + jnp.log(sums)
        picked = jnp.sum(jnp.where(chosen, logits, 0.0), axis=0, keepdims=True)
        loss_out[...] = jnp.mean(log_total - picked, axis=1, keepdims=True)
        shape = (16, users_total)
        seat = lax.broadcasted_iota(jnp.int32, shape, 0)
        mine = lax.broadcasted_iota(jnp.int32, shape, 1) == me * users_here + seat
        mine = (mine & (seat < users_here)).astype(jnp.float32).astype(jnp.bfloat16)
        own_grad = contract_last(mine, logit_grad).astype(jnp.bfloat16)
        found = jnp.dot(own_grad, emb_all, preferred_element_type=jnp.float32)
        ug_out[...] = found[:users_here, :].astype(ug_out.dtype)
        e = e_rows[...]
        g = e_grad[...]
        along = jnp.mean(e * g, axis=1, keepdims=True)
        gain_out[...] = jnp.sum(e * (g - e * along), axis=0, keepdims=True) / gain

    extra = [functools.partial(context_block, n) for n in range(head_width // tile)]
    extra.append(last_bits)

    def ready(m):
        weight_block(m, m + 1)
        cross_out(m).start()
        cross_out(m + 1).start()
        if m + 2 == hops:
            cross_out(hops).start()

    weight_block(0, hops)
    cross_out(0).start()
    ready(1)
    prepare(0)
    for pair in range(pairs):
        both = [m for m in (2 * pair, 2 * pair + 1) if m < hops]
        for j in range(slots):
            at = pl.ds(j * part, part)
            if j == slots - 1:
                for m in both:
                    if m + 2 < ring:
                        prepare(m + 2)
            for m in both:
                if m == 1 and j == 0:
                    prepare(1)
                term = term_of(m, j)
                if m >= 2:
                    ring_copy(m - 2, j).wait_recv()
                    term = term + arrived[m - 2, at, :].astype(jnp.float32)
                held[m, at, :] = term.astype(held.dtype)
                ring_copy(m, j).start()
            if pair >= 1 and j < 2 and extra:
                extra.pop(0)()
            coming = 2 * pair + 3
            if j == 0 and coming + 1 < ring:
                ready(coming)
    for job in extra:
        job()
    last = hops

    def total_copy(k, j):
        ref = totals.at[line, pl.ds(j * part, part), :]
        return remote(
            ref, ref, t_send.at[0], t_recv.at[k - 1, j],
            (lax.rem(group + 2 * k, groups), index),
        )

    def total_in(k, j):
        source = lax.rem(group + groups - 2 * k, groups)
        ref = totals.at[source // 2, pl.ds(j * part, part), :]
        return remote(ref, ref, t_send.at[0], t_recv.at[k - 1, j], (source, index))

    def out_rows(j, side=core):
        return pl.ds(pl.multiple_of(side * half + chunk(j) * part, part), part)

    def out_copy(j, side):
        ref = out.at[out_rows(j, side), :]
        return remote(ref, ref, o_send.at[0], o_recv.at[0], (partner, index))

    def out_across(j):
        ref = out.at[out_rows(j), :]
        return remote(ref, ref, f_send.at[0], f_recv.at[0], (across, index))

    shared = range(CHUNKS - 2) if split else range(CHUNKS)
    for j in range(slots):
        at = pl.ds(j * part, part)
        term = term_of(last, j)
        for m in range(max(hops - 2, 0), hops):
            ring_copy(m, j).wait_recv()
            term = term + arrived[m, at, :].astype(jnp.float32)
        value = term.astype(totals.dtype)
        if j in shared:
            totals[line, at, :] = value
            for k in range(1, lines):
                total_copy(k, j).start()
        else:
            out[out_rows(j), :] = value
            out_across(j).start()
            out_copy(j, core).start()

    for j in shared:
        at = pl.ds(j * part, part)
        for k in range(1, lines):
            total_in(k, j).wait_recv()
        value = totals[0, at, :].astype(jnp.float32)
        for other in range(1, lines):
            value = value + totals[other, at, :].astype(jnp.float32)
        out[out_rows(j), :] = value.astype(out.dtype)
        out_copy(j, core).start()
    if split:
        out_across(CHUNKS - 1).wait_recv()
        out_copy(CHUNKS - 1, core).start()

    drain_gather()
    drain_share()
    settle(cross, x_send.at[0])
    if split:
        settle(lent, b_send.at[0])
    settle(part_in.at[pl.ds(0, hops * slots * part), :], r_send.at[0])
    settle(part_in.at[pl.ds(0, (lines - 1) * len(shared) * part), :], t_send.at[0])
    if split:
        out_across(CHUNKS - 2).wait_send()
    settle(out.at[pl.ds(pl.multiple_of(core * half, half), half), :], o_send.at[0])
    arrive(out.at[pl.ds(pl.multiple_of((1 - core) * half, half), half), :], o_recv.at[0])


def finish_kernel(*refs):
    count = len(refs) // 2
    sems = refs[-1]
    copies = [
        pltpu.make_async_copy(refs[k], refs[count + k], sems.at[k]) for k in range(count)
    ]
    for copy in copies:
        copy.start()
    for copy in copies:
        copy.wait()


def on_device(
    groups, ring,
    context, residual, out_weight, norm_gain, user_vectors, positive, item_ids, item_counts, lengths
):
    tokens, head_width = context.shape
    width = residual.shape[1]
    rows = out_weight.shape[0]
    half = rows // 2
    items_here = lengths.shape[0]
    users_here = user_vectors.shape[0]
    total = groups * ring
    lines = groups // 2
    cells = lines * ring
    hops = ring - 1
    users_total, items_total = total * users_here, total * items_here
    dma = pltpu.SemaphoreType.DMA
    half_type, full_type = jnp.bfloat16, jnp.float32
    vmem = pl.BlockSpec(memory_space=pltpu.VMEM)
    hbm = pl.BlockSpec(memory_space=pltpu.HBM)
    results = pl.pallas_call(
        functools.partial(step_kernel, groups, ring, users_here, items_here),
        out_shape=(
            jax.ShapeDtypeStruct((1, 1), full_type),
            jax.ShapeDtypeStruct((tokens, width), half_type),
            jax.ShapeDtypeStruct((tokens, head_width), half_type),
            jax.ShapeDtypeStruct((rows, width), half_type),
            jax.ShapeDtypeStruct((1, width), full_type),
            jax.ShapeDtypeStruct((users_here, width), half_type),
        ),
        in_specs=[hbm] * 9,
        out_specs=(vmem,) * 6,
        scratch_shapes=[
            pltpu.VMEM((tokens, head_width), half_type),
            pltpu.VMEM((head_width, tokens), half_type),
            pltpu.VMEM((tokens, width), half_type),
            pltpu.VMEM((ring * rows, width), half_type),
            pltpu.VMEM((total, users_here, width + 128), half_type),
            pltpu.VMEM((tokens, width), full_type),
            pltpu.VMEM((tokens, 1), full_type),
            pltpu.VMEM((users_total, width + 128), half_type),
            pltpu.VMEM((8, width), full_type),
            pltpu.VMEM((8, width), full_type),
            pltpu.VMEM((total, items_here, width), half_type),
            pltpu.VMEM((items_total, width), full_type),
            pltpu.VMEM((items_total, width), full_type),
            pltpu.VMEM((ring * rows, width), half_type),
            pltpu.VMEM((ring, half, width), half_type),
            pltpu.VMEM((hops, half, width), half_type),
            pltpu.VMEM((hops, half, width), half_type),
            pltpu.VMEM((lines, half, width), half_type),
            pltpu.VMEM((ring, half // CHUNKS, width), half_type),
            pltpu.VMEM((ring, half // CHUNKS, width), half_type),
            pltpu.VMEM((1, width), full_type),
            pltpu.SMEM((users_here,), jnp.int32),
            pltpu.SMEM((items_here,), jnp.int32),
            pltpu.SMEM((items_here,), jnp.int32),
            pltpu.SMEM((items_here,), jnp.int32),
            dma((9,)),
            dma((1,)),
            dma((hops, CHUNKS)),
            dma((hops,)),
            dma((hops,)),
            dma((1,)),
            dma((hops,)),
            dma((ring, max(lines - 1, 1))),
            dma((lines,)),
            dma((1,)),
            dma((lines,)),
            dma((lines,)),
            dma((1,)),
            dma((ring,)),
            dma((1,)),
            dma((hops, CHUNKS - 1 if lines == 2 else CHUNKS)),
            dma((1,)),
            dma((max(lines - 1, 1), CHUNKS)),
            dma((1,)),
            dma((1,)),
            dma((1,)),
            dma((ring,)),
            dma((1,)),
            dma((1,)),
        ],
        compiler_params=pltpu.CompilerParams(
            collective_id=0, has_side_effects=True, vmem_limit_bytes=48 << 20
        ),
        name="whole_step",
    )(
        *(
            pltpu.with_memory_space_constraint(operand, pltpu.HBM)
            for operand in (
                context, residual, out_weight, norm_gain[None, :], user_vectors,
                positive, item_ids, item_counts, lengths,
            )
        )
    )
    loss, residual_grad, context_grad, weight_grad, gain_grad, user_grad = pl.pallas_call(
        finish_kernel,
        out_shape=tuple(jax.ShapeDtypeStruct(r.shape, r.dtype) for r in results),
        in_specs=[vmem] * len(results),
        out_specs=(hbm,) * len(results),
        scratch_shapes=[dma((len(results),))],
        compiler_params=pltpu.CompilerParams(vmem_limit_bytes=8 << 20),
        name="finish",
    )(*results)
    return (loss[0, 0], residual_grad, context_grad, weight_grad, gain_grad[0], user_grad)


def solution(mesh):
    placed = (
        P(("dp", "fsdp"), None),
        P(("dp", "fsdp"), None),
        P("fsdp", None),
        P(),
        P(("dp", "fsdp"), None),
        P(("dp", "fsdp")),
        P(("dp", "fsdp")),
        P(("dp", "fsdp")),
        P(("dp", "fsdp")),
    )
    return jax.shard_map(
        functools.partial(on_device, mesh.shape["dp"], mesh.shape["fsdp"]),
        mesh=mesh,
        in_specs=placed,
        out_specs=(
            P(),
            P(("dp", "fsdp"), None),
            P(("dp", "fsdp"), None),
            P("fsdp", None),
            P(),
            P(("dp", "fsdp"), None),
        ),
        check_vma=False,
    )
```
